32 devices in a mesh: head: 4 (over z), span: 8 (over y, x, core).
Axes of the slice: x: 2, y: 2, z: 4, core: 2. Of those that a mesh axis runs over, the one named last changes fastest.
Arguments:
- tokens: bfloat16 [8, 4096, 512], P('span', 'head'), may hold values from -6 to 6
- segment_ids: int32 [8, 4096], P('span'), may hold values from 0 to 4, as said below
- first_gain: float32 [512], P(('head', 'span')), may hold values from 0.5 to 1.5
- first_shift: float32 [512], P(('head', 'span')), may hold values from -3 to 3
- project_weight: bfloat16 [3, 512, 512], P(None, ('head', 'span')), may hold values from -0.25 to 0.25
- project_bias: float32 [3, 512], P(None, ('head', 'span')), may hold values from -1.2 to 1.2
- output_weight: bfloat16 [512, 512], P(('head', 'span')), may hold values from -1 to 1
- output_bias: float32 [512], P(('head', 'span')), may hold values from -3 to 3
- second_gain: float32 [512], P(('head', 'span')), may hold values from 0.5 to 1.5
- second_shift: float32 [512], P(('head', 'span')), may hold values from -3 to 3
- expand_weight: bfloat16 [512, 2048], P(('head', 'span')), may hold values from -0.25 to 0.25
- expand_bias: float32 [2048], P(('head', 'span')), may hold values from -3 to 3
- reduce_weight: bfloat16 [2048, 512], P(('head', 'span')), may hold values from -0.125 to 0.125
- reduce_bias: float32 [512], P(('head', 'span')), may hold values from -3 to 3
- cotangent: bfloat16 [8, 4096, 512], P('span', 'head'), may hold values from -6 to 6
Outputs:
- layer_output: bfloat16 [8, 4096, 512], P('span', 'head')
- tokens_grad: bfloat16 [8, 4096, 512], P('span', 'head')
- first_gain_grad: float32 [512], P(('head', 'span'))
- first_shift_grad: float32 [512], P(('head', 'span'))
- project_weight_grad: float32 [3, 512, 512], P(None, ('head', 'span'))
- project_bias_grad: float32 [3, 512], P(None, ('head', 'span'))
- output_weight_grad: float32 [512, 512], P(('head', 'span'))
- output_bias_grad: float32 [512], P(('head', 'span'))
- second_gain_grad: float32 [512], P(('head', 'span'))
- second_shift_grad: float32 [512], P(('head', 'span'))
- expand_weight_grad: float32 [512, 2048], P(('head', 'span'))
- expand_bias_grad: float32 [2048], P(('head', 'span'))
- reduce_weight_grad: float32 [2048, 512], P(('head', 'span'))
- reduce_bias_grad: float32 [512], P(('head', 'span'))
The draws below stay inside these ranges and needn't reach their ends.
Inputs may be any that keep to these rules, and one draw needn't show every extreme that they name: `segment_ids`: row r is spans 2r and 2r+1 laid end to end (8192 positions). Along a row the ids rise from 1 without falling, and every row ends with one or more padding positions of id 0, the only zeros of the row.
All inputs are finite; a program needn't handle non-finite values.
Results may differ from the reference program's by a relative error of at most 0.039.
Values may be sent and summed in bfloat16 or wider, within the bound.
A program may use at most 320 MiB of HBM per device.

```python
import jax
import jax.numpy as jnp
from jax import lax

D = 512
HEADS = 8
HEAD_DIM = 64
FF = 2048
BLOCK = 16
DOCS = 4
TOK_SPAN = 4096
SPANS = 8
ROWS = 4
ROW_LEN = 8192


def draw_segment_ids(key, part):
    row_count = SPANS // 2
    length = 2 * TOK_SPAN
    jitter_key, padding_key = jax.random.split(jax.random.fold_in(key, 11))
    marks = jnp.arange(1, DOCS, dtype=jnp.int32) * (length // DOCS)
    jitter = jax.random.randint(jitter_key, (row_count, DOCS - 1), -(length // 16), length // 16 + 1)
    cuts = marks[None, :] + jitter
    padding = jax.random.randint(padding_key, (row_count, 1), 1, length // 8)
    places = jnp.arange(length, dtype=jnp.int32)[None, :]
    labels = 1 + jnp.sum((places[:, :, None] >= cuts[:, None, :]).astype(jnp.int32), axis=-1)
    labels = jnp.where(places < length - padding, labels, 0)
    return labels.reshape(SPANS, TOK_SPAN).astype(jnp.int32)


def raised(values, own_key, source, target, blocks, factor):
    owner, partner = [(jnp.arange(values.shape[dim]) // (values.shape[dim] // blocks)).reshape([-1 if axis == dim else 1 for axis in range(values.ndim)]) for dim in (source, target)]
    chosen = jax.random.permutation(own_key, blocks)[partner]
    strong = (owner == chosen) | (owner == (partner + blocks // 2) % blocks)
    return jnp.where(strong, factor * values, values)


def shard_levels(key, shape, cuts, low, top_value):
    factor_of, own = 1.0, jax.random.fold_in(key, 6)
    for axis_at, parts in cuts:
        draws = jnp.exp(jax.random.uniform(jax.random.fold_in(own, axis_at), (parts,), jnp.float32, low / len(cuts), top_value / len(cuts)))
        factor_of = factor_of * jnp.repeat(draws, shape[axis_at] // parts).reshape([-1 if axis == axis_at else 1 for axis in range(len(shape))])
    return factor_of


def bell_draw(rng, dims, width, bound, cuts=(), kind=jnp.bfloat16):
    entries = width * jax.random.normal(rng, dims, jnp.float32)
    if cuts:
        entries = entries * shard_levels(rng, dims, cuts, -0.22, 0.18)
    return jnp.clip(entries, -bound, bound).astype(kind)


def noise_with(own_key, shape, spread, limit, cuts, heavy, held_as=jnp.bfloat16):
    entries = spread * jax.random.normal(own_key, shape, jnp.float32)
    if cuts:
        entries = entries * shard_levels(own_key, shape, cuts, -0.22, 0.18)
    return jnp.clip(raised(entries, jax.random.fold_in(own_key, 3), *heavy), -limit, limit).astype(held_as)


def setup_inputs(seed: int = 0) -> dict:
    splits = jax.random.split(jax.random.key(seed), 16)
    tokens = bell_draw(splits[0], (SPANS, TOK_SPAN, D), 1.0, 6.0, ((0, 8), (1, 4)))
    segment_ids = draw_segment_ids(jax.random.fold_in(splits[15], 71), 0)
    first_gain = jnp.clip(1.0 + 0.1 * jax.random.normal(splits[2], (D,), jnp.float32), 0.5, 1.5)
    first_shift = bell_draw(splits[3], (D,), 0.5, 3.0, ((0, 32),), jnp.float32)
    project_weight = bell_draw(splits[4], (3, D, D), D ** -0.5, 0.25, ((1, 32),))
    project_bias = bell_draw(splits[5], (3, D), 0.2, 1.2, ((1, 32),), jnp.float32)
    output_weight = bell_draw(splits[6], (D, D), (D // 16) ** -0.5, 1.0, ((0, 32),))
    output_bias = bell_draw(splits[7], (D,), 0.5, 3.0, ((0, 32),), jnp.float32)
    second_gain = jnp.clip(1.0 + 0.1 * jax.random.normal(splits[8], (D,), jnp.float32), 0.5, 1.5)
    second_shift = bell_draw(splits[9], (D,), 0.5, 3.0, ((0, 32),), jnp.float32)
    expand_weight = bell_draw(splits[10], (D, FF), D ** -0.5, 0.25, ((0, 32),))
    expand_bias = bell_draw(splits[11], (FF,), 0.5, 3.0, ((0, 32),), jnp.float32)
    reduce_weight = bell_draw(splits[12], (FF, D), FF ** -0.5, 0.125, ((0, 32),))
    reduce_bias = bell_draw(splits[13], (D,), 0.5, 3.0, ((0, 32),), jnp.float32)
    cotangent = noise_with(splits[14], (SPANS, TOK_SPAN, D), 1.0, 6.0, ((0, 8), (1, 4)), (0, 2, 8, 2.0))
    return {"tokens": tokens, "segment_ids": segment_ids, "first_gain": first_gain, "first_shift": first_shift, "project_weight": project_weight, "project_bias": project_bias, "output_weight": output_weight, "output_bias": output_bias, "second_gain": second_gain, "second_shift": second_shift, "expand_weight": expand_weight, "expand_bias": expand_bias, "reduce_weight": reduce_weight, "reduce_bias": reduce_bias, "cotangent": cotangent}


epsilon = 1e-05
highest = lax.Precision.HIGHEST

@jax.custom_vjp
def low(v):
    return lax.optimization_barrier(v.astype(jnp.bfloat16)).astype(jnp.float32)

@jax.custom_vjp
def low_back(v):
    return v

def low_keep(v):
    return (low(v), None)

def low_pass(kept, grad):
    return (grad,)

def back_keep(v):
    return (v, None)

def back_low(kept, grad):
    return (low(grad),)
low.defvjp(low_keep, low_pass)
low_back.defvjp(back_keep, back_low)

def normalized(values_in, gain, shift):
    center = values_in - lax.optimization_barrier(jnp.mean(values_in, axis=-1, keepdims=True))
    inverse = lax.rsqrt(lax.optimization_barrier(jnp.mean(center * center, axis=-1, keepdims=True)) + epsilon)
    return center * inverse * gain + shift

def coarse_labels(labels):
    paired = labels.reshape(-1, 2)
    return jnp.where(paired[:, 0] == paired[:, 1], paired[:, 0], 0)

def windows(padded, blocks):
    shaped = padded.reshape((blocks + 2, BLOCK) + padded.shape[1:])
    return jnp.concatenate([shaped[:-2], shaped[1:-1], shaped[2:]], axis=1)

def allowed(query_labels, key_labels, height):
    blocks = query_labels.shape[0]
    query_side = query_labels.T[:, None, :]
    key_side = key_labels.T[None, :, :]
    matching = (query_side == key_side) & (key_side != 0)
    query_pos = lax.broadcasted_iota(jnp.int32, (BLOCK, 3 * BLOCK, blocks), 0)
    key_pos = lax.broadcasted_iota(jnp.int32, (BLOCK, 3 * BLOCK, blocks), 1)
    if height == 0:
        return matching | (query_pos + BLOCK == key_pos)
    half_block = BLOCK // 2
    return matching & (jnp.abs(query_pos // half_block - key_pos // half_block + BLOCK // half_block) >= 2)

def row_attention(queries, keys, values, labels):
    length = queries.shape[0]
    factor = HEAD_DIM ** (-0.5)
    count = (length // BLOCK).bit_length() - 1
    totals = jnp.zeros((length, HEADS), jnp.float32)
    numerators = jnp.zeros((length, HEADS, HEAD_DIM), jnp.float32)
    level_labels = labels
    for height in range(count):
        multiple = 2 ** height
        extent = length // multiple
        blocks = extent // BLOCK
        if height > 0:
            level_labels = coarse_labels(level_labels)
        query_coarse = lax.optimization_barrier(jnp.mean(queries.reshape(extent, multiple, HEADS, HEAD_DIM), axis=1))
        key_coarse = lax.optimization_barrier(jnp.mean(keys.reshape(extent, multiple, HEADS, HEAD_DIM), axis=1))
        value_coarse = lax.optimization_barrier(jnp.sum(values.reshape(extent, multiple, HEADS, HEAD_DIM), axis=1))
        border = ((BLOCK, BLOCK), (0, 0), (0, 0))
        key_window = windows(jnp.pad(key_coarse, border), blocks)
        value_window = windows(jnp.pad(value_coarse, border), blocks)
        label_window = windows(jnp.pad(level_labels, (BLOCK, BLOCK)), blocks)
        allowed_pairs = allowed(level_labels.reshape(blocks, BLOCK), label_window, height)
        query_block = query_coarse.reshape(blocks, BLOCK, HEADS, HEAD_DIM)
        scores = factor * jnp.einsum('bihd,bjhd->hijb', query_block, key_window, precision=highest)
        weights = jnp.where(allowed_pairs[None], jnp.exp(scores), 0.0)
        level_total = multiple * lax.optimization_barrier(jnp.sum(weights, axis=2))
        numerator = jnp.einsum('hijb,bjhd->bihd', weights, value_window, precision=highest)
        level_total = level_total.transpose(2, 1, 0).reshape(extent, HEADS)
        totals = totals + jnp.repeat(level_total, multiple, axis=0)
        numerators = numerators + jnp.repeat(numerator.reshape(extent, HEADS, HEAD_DIM), multiple, axis=0)
    return (numerators / totals[:, :, None]).reshape(length, HEADS * HEAD_DIM)

def layer(row, params, labels):
    gain_one, shift_one, proj_weight, proj_bias, out_weight, out_bias, gain_two, shift_two, up_weight, up_bias, down_weight, down_bias = params
    act_one = low(normalized(row, gain_one, shift_one))
    projected = jnp.einsum('td,cde->cte', act_one, proj_weight, precision=highest) + proj_bias[:, None, :]
    projected = low_back(low(projected))
    attended = row_attention(projected[0], projected[1], projected[2], labels)
    attended = low_back(low(attended))
    branch = low_back(jnp.dot(attended, out_weight, precision=highest) + out_bias)
    hidden = row + branch
    act_two = low(normalized(hidden, gain_two, shift_two))
    pre_up = low_back(jnp.dot(act_two, up_weight, precision=highest) + up_bias)
    act_up = low(jax.nn.gelu(pre_up))
    return hidden + jnp.dot(act_up, down_weight, precision=highest) + down_bias

def reference(tokens, segment_ids, first_gain, first_shift, project_weight, project_bias, output_weight, output_bias, second_gain, second_shift, expand_weight, expand_bias, reduce_weight, reduce_bias, cotangent):
    params = tuple((item.astype(jnp.float32) for item in (first_gain, first_shift, project_weight, project_bias, output_weight, output_bias, second_gain, second_shift, expand_weight, expand_bias, reduce_weight, reduce_bias)))
    token_rows = tokens.astype(jnp.float32).reshape(ROWS, ROW_LEN, D)
    label_rows = segment_ids.reshape(ROWS, ROW_LEN)
    cot_rows = cotangent.astype(jnp.float32).reshape(ROWS, ROW_LEN, D)

    def one_row(carry, item):
        row, labels, grad_out = item
        result, pullback = jax.vjp(lambda row_in, param_in: layer(row_in, param_in, labels), row, params)
        grad_row, grad_params = pullback(grad_out)
        carry = jax.tree.map(lambda first, second: first + second, carry, grad_params)
        return (carry, (result.astype(jnp.bfloat16), grad_row.astype(jnp.bfloat16)))
    zeroed = tuple((jnp.zeros_like(item) for item in params))
    sums, (results, grad_rows) = lax.scan(one_row, zeroed, (token_rows, label_rows, cot_rows))
    layer_output = results.reshape(SPANS, TOK_SPAN, D)
    tokens_grad = grad_rows.reshape(SPANS, TOK_SPAN, D)
    return (layer_output, tokens_grad, sums[0], sums[1], sums[2], sums[3], sums[4], sums[5], sums[6], sums[7], sums[8], sums[9], sums[10], sums[11])
```

```python
import functools
import jax
import jax.numpy as jnp
from jax import lax
from jax.experimental import pallas as pl
from jax.experimental.pallas import tpu as pltpu
from jax.sharding import PartitionSpec as P

F32, BF16, I32 = jnp.float32, jnp.bfloat16, jnp.int32
MESH = pl.DeviceIdType.MESH
VMEM = pltpu.VMEM
NEG = -1e30
EPS = 1e-5
TOK = 1024
TILE = 256
D = 512
FF = 2048
EXT = 2384
LEVEL_SIZE = (1024, 512, 256, 128, 64, 32, 16)
COARSE_AT = (None, 0, 512, 768, 896, 960, 992)
EXT_AT = (0, 1056, 1600, 1888, 2048, 2144, 2208)
WIDE_AT = 2256
TRANS_B = (((1,), (1,)), ((), ()))
TRANS_A = (((0,), (0,)), ((), ()))


def mm(a, b):
    return jnp.dot(a, b, preferred_element_type=F32)


def mm_bt(a, b):
    return lax.dot_general(a, b, TRANS_B, preferred_element_type=F32)


def mm_at(a, b):
    return lax.dot_general(a, b, TRANS_A, preferred_element_type=F32)


def iota(shape, dim):
    return lax.broadcasted_iota(I32, shape, dim)


def split(v):
    high = v.astype(BF16)
    return high, (v - high.astype(F32)).astype(BF16)


def covers(t, c, block):
    if block == 0:
        return ((t & 255) >> 1) == c
    if block == 1:
        return ((t & 511) >> 2) == c
    if block == 2:
        return (t >> 3) == c
    level, start = mixed_levels(c)
    return (jnp.right_shift(t, level) == c - start) & (c < 124)


def mixed_levels(c):
    a, b, d, e = ((c >= edge).astype(I32) for edge in (64, 96, 112, 120))
    return 4 + a + b + d + e, 64 * a + 32 * b + 16 * d + 8 * e


def ones_where(cond):
    return jnp.where(cond, 1.0, 0.0).astype(BF16)


def identity(n):
    return ones_where(iota((n, n), 0) == iota((n, n), 1))


def fill_spread(spt):
    @pl.loop(0, TOK // TILE)
    def _(j):
        for block in range(4):
            t = iota((TILE, 128), 0) + j * TILE
            c = iota((TILE, 128), 1)
            spt[pl.ds(j * TILE, TILE), 128 * block:128 * block + 128] = ones_where(covers(t, c, block))


def fill_pool(sp):
    @pl.loop(0, TOK // TILE)
    def _(j):
        for block in range(4):
            t = iota((128, TILE), 1) + j * TILE
            c = iota((128, TILE), 0)
            sp[128 * block:128 * block + 128, pl.ds(pl.multiple_of(j * TILE, TILE), TILE)] = ones_where(covers(t, c, block))


def pre_kernel(tok, seg, weight, vecs, a1_out, fine, coarse, acc, acc_ids):
    j = pl.program_id(0)
    h = lax.axis_index("head")
    v = tok[...].astype(F32)
    center = v - jnp.mean(v, axis=-1, keepdims=True)
    inverse = lax.rsqrt(jnp.mean(center * center, axis=-1, keepdims=True) + EPS)
    a1 = (center * inverse * vecs[0:1, :] + vecs[1:2, :]).astype(BF16)
    a1_out[...] = a1
    for part in range(3):
        r = (mm(a1, weight[part]) + vecs[2 + part:3 + part, :]).astype(BF16)
        if part == 0:
            r = r * jnp.array(0.125, BF16)
        fine[:, D * part:D * part + D] = r
    ids = seg[:, pl.ds(pl.multiple_of(h * TOK + j * TILE, TILE), TILE)].astype(F32)
    ids_b = jnp.broadcast_to(ids, (128, TILE)).astype(BF16)
    sq_b = jnp.broadcast_to(ids * ids, (128, TILE)).astype(BF16)
    fine[:, 3 * D:3 * D + 128] = mm_bt(identity(TILE), ids_b).astype(BF16)
    c, t = iota((192, TILE), 0), iota((192, TILE), 1)
    near = ones_where(jnp.where(c < 128, t >> 1, (t >> 2) + 128) == c)
    x = fine[:, 0:3 * D]
    r = mm(near, x)
    lab = labels_of(mm_bt(near, ids_b), mm_bt(near, sq_b), jnp.where(iota((192, 128), 0) < 128, 2.0, 4.0))
    at1, at2 = pl.multiple_of(j * 128, 128), pl.multiple_of(512 + j * 64, 64)
    coarse[pl.ds(at1, 128), 0:2 * D] = (r[0:128, 0:2 * D] * 0.5).astype(BF16)
    coarse[pl.ds(at1, 128), 2 * D:3 * D] = r[0:128, 2 * D:].astype(BF16)
    coarse[pl.ds(at1, 128), 3 * D:] = lab[0:128].astype(BF16)
    coarse[pl.ds(at2, 64), 0:2 * D] = (r[128:192, 0:2 * D] * 0.25).astype(BF16)
    coarse[pl.ds(at2, 64), 2 * D:3 * D] = r[128:192, 2 * D:].astype(BF16)
    coarse[pl.ds(at2, 64), 3 * D:] = lab[128:192].astype(BF16)
    tt, cc = iota((128, TILE), 1) + j * TILE, iota((128, TILE), 0)
    far = jnp.concatenate([ones_where(covers(tt, cc, 2)), ones_where(covers(tt, cc, 3))], axis=0)

    @pl.when(j == 0)
    def _():
        acc[...] = jnp.zeros_like(acc)
        acc_ids[...] = jnp.zeros_like(acc_ids)
    acc[...] += mm(far, x)
    acc_ids[:, 0:128] += mm_bt(far, ids_b)
    acc_ids[:, 128:256] += mm_bt(far, sq_b)

    @pl.when(j == TOK // TILE - 1)
    def _():
        row = iota((TILE, 128), 0)
        level, _unused = mixed_levels(row - 128)
        times = jnp.where(row < 128, 8.0, (1 << level).astype(F32))
        lab = labels_of(acc_ids[:, 0:128], acc_ids[:, 128:256], times)
        shrink = 1.0 / times
        for k in range(8):
            coarse[768:1024, 128 * k:128 * k + 128] = (acc[:, 128 * k:128 * k + 128] * shrink).astype(BF16)
        coarse[768:1024, 2 * D:3 * D] = acc[:, 2 * D:].astype(BF16)
        coarse[768:1024, 3 * D:] = lab.astype(BF16)


def labels_of(total, squares, times):
    return jnp.where(times * squares == total * total, total / times, 0.0)


def before_attention(tok, seg, weight, vecs):
    wide = 3 * D + 128
    return pl.pallas_call(
        pre_kernel,
        grid=(TOK // TILE,),
        out_shape=[jax.ShapeDtypeStruct((TOK, D), BF16), jax.ShapeDtypeStruct((TOK, wide), BF16),
                   jax.ShapeDtypeStruct((TOK, wide), BF16)],
        in_specs=[pl.BlockSpec((TILE, D), lambda j: (j, 0)),
                  pl.BlockSpec(seg.shape, lambda j: (0, 0)),
                  pl.BlockSpec((3, D, D), lambda j: (0, 0, 0), pipeline_mode=pl.Buffered(1)),
                  pl.BlockSpec((16, D), lambda j: (0, 0))],
        out_specs=[pl.BlockSpec((TILE, D), lambda j: (j, 0)), pl.BlockSpec((TILE, wide), lambda j: (j, 0)),
                   pl.BlockSpec((TOK, wide), lambda j: (0, 0))],
        scratch_shapes=[VMEM((TILE, 3 * D), F32), VMEM((TILE, 256), F32)],
        compiler_params=pltpu.CompilerParams(dimension_semantics=("arbitrary",), vmem_limit_bytes=60 << 20),
        name="before_attention",
    )(tok, seg, weight, vecs)


def row_place():
    h, s = lax.axis_index("head"), lax.axis_index("span")
    return (s % 2) * 4 + h


def row_device(place):
    s = lax.axis_index("span")
    return {"head": place % 4, "span": (s // 2) * 2 + place // 4}


def greet(devices):
    barrier = pltpu.get_barrier_semaphore()
    for d in devices:
        pl.semaphore_signal(barrier, inc=1, device_id=d, device_id_type=MESH)
    pl.semaphore_wait(barrier, len(devices))


def rcopy(src, dst, send, recv, device):
    return pltpu.make_async_remote_copy(src_ref=src, dst_ref=dst, send_sem=send, recv_sem=recv,
                                        device_id=device, device_id_type=MESH)


def edges_kernel(fine, coarse, halo, wide, local, send, recv):
    p = row_place()
    others = [lax.rem(p + d, 8) for d in range(1, 8)]
    greet([row_device(o) for o in others])
    right, left = row_device(others[0]), row_device(others[6])
    lanes = pl.ds(D, 2 * D + 128)
    copies = []
    for l, size in enumerate(LEVEL_SIZE):
        src, at = (fine, 0) if l == 0 else (coarse, COARSE_AT[l])
        copies.append(rcopy(src.at[pl.ds(at + size - 16, 16), lanes], halo.at[0, l], send.at[l], recv.at[l], right))
        copies.append(rcopy(src.at[pl.ds(at, 16), lanes], halo.at[1, l], send.at[7 + l], recv.at[7 + l], left))
    block = coarse.at[pl.ds(1008, 16), lanes]
    for d in range(1, 8):
        copies.append(rcopy(block, wide.at[p], send.at[13 + d], recv.at[13 + d], row_device(others[d - 1])))
    for cp in copies:
        cp.start()
    own = pltpu.make_async_copy(block, wide.at[p], local)
    own.start()
    own.wait()
    for cp in copies:
        cp.wait()


def exchange_edges(fine, coarse):
    lanes = 2 * D + 128
    return pl.pallas_call(
        edges_kernel,
        out_shape=[jax.ShapeDtypeStruct((2, 7, 16, lanes), BF16), jax.ShapeDtypeStruct((8, 16, lanes), BF16)],
        in_specs=[pl.BlockSpec(memory_space=pl.ANY)] * 2,
        out_specs=[pl.BlockSpec(memory_space=pl.ANY)] * 2,
        scratch_shapes=[pltpu.SemaphoreType.DMA, pltpu.SemaphoreType.DMA((21,)), pltpu.SemaphoreType.DMA((21,))],
        compiler_params=pltpu.CompilerParams(collective_id=2, has_side_effects=True),
        name="exchange_edges",
    )(fine, coarse)


def edges_back_kernel(ext, halo, wide, local, send, recv):
    p = row_place()
    others = [lax.rem(p + d, 8) for d in range(1, 8)]
    greet([row_device(o) for o in others])
    right, left = row_device(others[0]), row_device(others[6])
    copies = []
    for l, size in enumerate(LEVEL_SIZE):
        at = EXT_AT[l]
        copies.append(rcopy(ext.at[:, pl.ds(at + 16 + size, 16)], halo.at[0, l], send.at[l], recv.at[l], right))
        copies.append(rcopy(ext.at[:, pl.ds(at, 16)], halo.at[1, l], send.at[7 + l], recv.at[7 + l], left))
    for d in range(1, 8):
        o = others[d - 1]
        copies.append(rcopy(ext.at[:, pl.ds(pl.multiple_of(WIDE_AT + 16 * o, 16), 16)], wide.at[p], send.at[13 + d], recv.at[13 + d], row_device(o)))
    for cp in copies:
        cp.start()
    own = pltpu.make_async_copy(ext.at[:, pl.ds(pl.multiple_of(WIDE_AT + 16 * p, 16), 16)], wide.at[p], local)
    own.start()
    own.wait()
    for cp in copies:
        cp.wait()


def return_edges(ext):
    return pl.pallas_call(
        edges_back_kernel,
        out_shape=[jax.ShapeDtypeStruct((2, 7, 2, 16, D), BF16), jax.ShapeDtypeStruct((8, 2, 16, D), BF16)],
        in_specs=[pl.BlockSpec(memory_space=pl.ANY)],
        out_specs=[pl.BlockSpec(memory_space=pl.ANY)] * 2,
        scratch_shapes=[pltpu.SemaphoreType.DMA, pltpu.SemaphoreType.DMA((21,)), pltpu.SemaphoreType.DMA((21,))],
        compiler_params=pltpu.CompilerParams(collective_id=3, has_side_effects=True),
        name="return_edges",
    )(ext)


def build_ext(dst, x0, xc, halo, wide, first=None, last=None):
    def put(at, v):
        dst[at:at + v.shape[0], :] = v.astype(dst.dtype)

    for l, size in enumerate(LEVEL_SIZE):
        at = EXT_AT[l]
        a, b = halo[0, l], halo[1, l]
        if first is not None:
            a, b = a.astype(F32) * first, b.astype(F32) * last
        put(at, a)
        put(at + 16, x0[...] if l == 0 else xc[COARSE_AT[l]:COARSE_AT[l] + size, :])
        put(at + 16 + size, b)
    for e in range(8):
        put(WIDE_AT + 16 * e, wide[e])


def fill_bias(bias, bias_mixed, lx, l0, lc, hl, rl):
    p = row_place()
    build_ext(lx, l0, lc, hl, rl, jnp.where(p > 0, 1.0, 0.0), jnp.where(p < 7, 1.0, 0.0))

    def matching(at, size, q):
        kl = lx[pl.ds(at, size), :]
        ql = jnp.transpose(q.astype(F32))[0:1, :]
        return (kl == ql) & (kl != 0.0)

    r, c = iota((160, 128), 0), iota((160, 128), 1)
    near = jnp.abs((r >> 4) - 1 - (c >> 4)) <= 1
    far = near & (jnp.abs((r >> 3) - 2 - (c >> 3)) >= 2)
    same = (r - 16) == c

    @pl.loop(0, 8)
    def _(i):
        at = pl.multiple_of(128 * i, 16)
        ok = matching(at, 160, l0[pl.ds(at, 128), :]) & near | same
        bias[pl.ds(pl.multiple_of(160 * i, 16), 160), :] = jnp.where(ok, 0.0, NEG)

    @pl.loop(8, 15)
    def _(i):
        q = lc[pl.ds(pl.multiple_of(128 * (i - 8), 16), 128), :]
        ok = matching(tile_at(i), 160, q) & far
        bias[pl.ds(pl.multiple_of(160 * i, 16), 160), :] = jnp.where(ok, 0.0, NEG)

    r, c = iota((336, 128), 0), iota((336, 128), 1)
    inner = (r >= 96).astype(I32) + (r >= 160).astype(I32)
    start = jnp.where(inner == 0, 0, jnp.where(inner == 1, 96, 160))
    e, k = (r - 208) >> 4, (r - 208) & 15
    upper = (k >= 8).astype(I32)
    level_k = jnp.where(r < 208, 4 + inner, 7 + upper)
    pos_k = jnp.where(r < 208, r - start - 16, jnp.where(k < 8, e * 8 + k, e * 4 + k - 8))
    level_q, start_q = mixed_levels(c)
    pos_q = c - start_q + jnp.where(level_q == 7, p * 8, jnp.where(level_q == 8, p * 4, 0))
    shape = (level_k == level_q) & (jnp.abs((pos_k >> 4) - (pos_q >> 4)) <= 1) & (jnp.abs((pos_k >> 3) - (pos_q >> 3)) >= 2)
    ok = matching(2048, 336, lc[896:1024, :]) & shape
    bias_mixed[...] = jnp.where(ok, 0.0, NEG)


def tile_at(i):
    level = (i >= 8).astype(I32) + (i >= 12).astype(I32) + (i >= 14).astype(I32)
    return pl.multiple_of(128 * i + 32 * level, 16)


def tile_times(i):
    level = (i >= 8).astype(I32) + (i >= 12).astype(I32) + (i >= 14).astype(I32)
    return (1 << level).astype(F32)


def mixed_times(shape):
    level, _unused = mixed_levels(iota(shape, len(shape) - 1))
    return (1 << level).astype(F32)


def head_masks(rows):
    lane = iota((rows, 128), 1)
    return ones_where(lane < 64), ones_where(lane >= 64)


def by_head(x, masks):
    return jnp.concatenate([x * masks[0], x * masks[1]], axis=0)


def own_blocks(x):
    return jnp.concatenate([x[0:64, 0:128], x[64:128, 128:256]], axis=0)


def twice(x):
    return jnp.concatenate([x, x], axis=1)


def coarse_columns(ref, j):
    pair = pl.multiple_of(1536 + 128 * (j // 2), 128)
    return jnp.concatenate([ref[:, pl.ds(pl.multiple_of(1024 + 128 * j, 128), 128)], ref[:, pl.ds(pair, 128)],
                            ref[:, 1792:2048]], axis=1)


def attention_kernel(q0, k0, v0, l0, qc, kc, vc, lc, hk, hv, hl, rk, rv, rl, ao_out, iz_out,
                     kx, vx, qx, bias, bias_mixed, lx, spt, nz):
    g = pl.program_id(0)

    @pl.when(g == 0)
    def _():
        fill_bias(bias, bias_mixed, lx, l0, lc, hl, rl)
        fill_spread(spt)
    build_ext(kx, k0, kc, hk, rk)
    build_ext(vx, v0, vc, hv, rv)
    qx[0:1024, :] = q0[...]
    qx[1024:2048, :] = qc[...]
    masks = head_masks(128)

    def tile(at, size, i, b, times):
        kw, vw = kx[pl.ds(at, size), :], vx[pl.ds(at, size), :]
        q = by_head(qx[pl.ds(pl.multiple_of(128 * i, 128), 128), :], masks)
        e = jnp.exp(mm_bt(kw, q) + twice(b))
        z = jnp.sum(e, axis=0, keepdims=True) * times
        n = own_blocks(mm_at(vw, e.astype(BF16)))
        zb = jnp.concatenate([jnp.broadcast_to(z[:, 0:128], (64, 128)), jnp.broadcast_to(z[:, 128:256], (64, 128))], axis=0)
        cols = pl.ds(pl.multiple_of(128 * i, 128), 128)
        nz[0:128, cols] = n.astype(BF16)
        nz[128:256, cols] = zb.astype(BF16)

    def body(i, carry):
        tile(tile_at(i), 160, i, bias[pl.ds(pl.multiple_of(160 * i, 16), 160), :], tile_times(i))
        return carry
    lax.fori_loop(0, 15, body, 0)
    tile(2048, 336, 15, bias_mixed[...], twice(mixed_times((1, 128))))
    eye = identity(TILE)

    @pl.loop(0, TOK // TILE)
    def _(j):
        rows = pl.ds(pl.multiple_of(j * TILE, TILE), TILE)
        r = mm_bt(eye, nz[:, rows]) + mm_bt(spt[rows, :], coarse_columns(nz, j))
        inverse = 1.0 / r[:, 128:256]
        iz_out[rows, :] = inverse
        ao_out[rows, :] = (r[:, 0:128] * inverse).astype(BF16)


def pair_specs():
    def cols(shift):
        return pl.BlockSpec((TOK, 128), lambda g, shift=shift: (0, g + shift))
    label = pl.BlockSpec((TOK, 128), lambda g: (0, 12))
    each = [cols(0), cols(4), cols(8), label]
    halo = [pl.BlockSpec((2, 7, 16, 128), lambda g, s=s: (0, 0, 0, g + s)) for s in (0, 4)]
    halo.append(pl.BlockSpec((2, 7, 16, 128), lambda g: (0, 0, 0, 8)))
    wide = [pl.BlockSpec((8, 16, 128), lambda g, s=s: (0, 0, g + s)) for s in (0, 4)]
    wide.append(pl.BlockSpec((8, 16, 128), lambda g: (0, 0, 8)))
    return each + each + halo + wide


def attention(fine, coarse, halo, wide):
    out = pl.BlockSpec((TOK, 128), lambda g: (0, g))
    return pl.pallas_call(
        attention_kernel,
        grid=(4,),
        out_shape=[jax.ShapeDtypeStruct((TOK, D), BF16), jax.ShapeDtypeStruct((TOK, D), F32)],
        in_specs=pair_specs(),
        out_specs=[out, out],
        scratch_shapes=[VMEM((EXT, 128), BF16), VMEM((EXT, 128), BF16), VMEM((2048, 128), BF16),
                        VMEM((15 * 160, 128), F32), VMEM((336, 128), F32), VMEM((EXT, 128), F32),
                        VMEM((TOK, 512), BF16), VMEM((256, 2048), BF16)],
        compiler_params=pltpu.CompilerParams(dimension_semantics=("arbitrary",), vmem_limit_bytes=60 << 20),
        name="attention",
    )(*([fine] * 4 + [coarse] * 4 + [halo] * 3 + [wide] * 3))


def attention_back_kernel(q0, k0, v0, l0, qc, kc, vc, lc, hk, hv, hl, rk, rv, rl, ao, iz, da, dq_out, ext_out,
                          kx, vx, qx, gx, bias, bias_mixed, lx, spt, sp, rm, dk, dv, dqt):
    g = pl.program_id(0)

    @pl.when(g == 0)
    def _():
        fill_bias(bias, bias_mixed, lx, l0, lc, hl, rl)
        fill_spread(spt)
        fill_pool(sp)
    build_ext(kx, k0, kc, hk, rk)
    build_ext(vx, v0, vc, hv, rv)
    qx[0:1024, :] = q0[...]
    qx[1024:2048, :] = qc[...]
    heads = ones_where(iota((16, 128), 0) == (iota((16, 128), 1) >> 6))

    @pl.loop(0, TOK // TILE)
    def _(j):
        rows = pl.ds(pl.multiple_of(j * TILE, TILE), TILE)
        gf = da[rows, :].astype(F32) * iz[rows, :]
        gx[rows, :] = gf.astype(BF16)
        high, low = split(gf * ao[rows, :].astype(F32))
        rm[:, rows] = mm_bt(heads, high) + mm_bt(heads, low)

    def pooled(c_rows, t_rows, dst):
        s = sp[c_rows, t_rows]
        gx[dst, :] = mm(s, gx[t_rows, :]).astype(BF16)
        high, low = split(rm[:, t_rows])
        return mm_bt(high, s) + mm_bt(low, s)

    @pl.loop(0, 4)
    def _(j):
        dst = pl.ds(pl.multiple_of(1024 + 128 * j, 128), 128)
        rm[:, dst] = pooled(pl.ds(0, 128), pl.ds(pl.multiple_of(j * 256, 256), 256), dst) * 2.0

    for j in range(2):
        dst = pl.ds(1536 + 128 * j, 128)
        rm[:, dst] = pooled(pl.ds(128, 128), pl.ds(j * 512, 512), dst) * 4.0
    rm[:, pl.ds(1792, 128)] = pooled(pl.ds(256, 128), pl.ds(0, 1024), pl.ds(1792, 128)) * 8.0
    rm[:, pl.ds(1920, 128)] = pooled(pl.ds(384, 128), pl.ds(0, 1024), pl.ds(1920, 128)) * mixed_times((16, 128))
    dk[...] = jnp.zeros_like(dk)
    dv[...] = jnp.zeros_like(dv)
    masks = head_masks(128)

    def tile(at, size, i, b, shrink):
        keys = pl.ds(at, size)
        cols = pl.ds(pl.multiple_of(128 * i, 128), 128)
        kw, vw = kx[keys, :], vx[keys, :]
        q, gg = by_head(qx[cols, :], masks), by_head(gx[cols, :], masks)
        e = jnp.exp(mm_bt(kw, q) + twice(b))
        rest = jnp.concatenate([rm[0:1, cols], rm[1:2, cols]], axis=1)
        ds = (e * (mm_bt(vw, gg) - rest)).astype(BF16)
        dk[keys, :] += mm(ds, q)
        dv[keys, :] += mm(e.astype(BF16), gg)
        dqt[:, cols] = (own_blocks(mm_at(kw, ds)) * shrink).astype(BF16)

    def body(i, carry):
        tile(tile_at(i), 160, i, bias[pl.ds(pl.multiple_of(160 * i, 16), 160), :], 0.125 / tile_times(i))
        return carry
    lax.fori_loop(0, 15, body, 0)
    tile(2048, 336, 15, bias_mixed[...], 0.125 / mixed_times((1, 128)))
    eye = identity(TILE)

    @pl.loop(0, TOK // TILE)
    def _(j):
        rows = pl.ds(pl.multiple_of(j * TILE, TILE), TILE)
        dq_out[rows, :] = (mm_bt(eye, dqt[:, rows]) + mm_bt(spt[rows, :], coarse_columns(dqt, j))).astype(BF16)
    ext_out[0] = dk[...].astype(BF16)
    ext_out[1] = dv[...].astype(BF16)


def attention_back(fine, coarse, halo, wide, ao, iz, da):
    pair = pl.BlockSpec((TOK, 128), lambda g: (0, g))
    ext = pl.BlockSpec((2, EXT, 128), lambda g: (0, 0, g))
    return pl.pallas_call(
        attention_back_kernel,
        grid=(4,),
        out_shape=[jax.ShapeDtypeStruct((TOK, D), BF16), jax.ShapeDtypeStruct((2, EXT, D), BF16)],
        in_specs=pair_specs() + [pair, pair, pair],
        out_specs=[pair, ext],
        scratch_shapes=[VMEM((EXT, 128), BF16), VMEM((EXT, 128), BF16), VMEM((2048, 128), BF16), VMEM((2048, 128), BF16),
                        VMEM((15 * 160, 128), F32), VMEM((336, 128), F32), VMEM((EXT, 128), F32),
                        VMEM((TOK, 512), BF16), VMEM((512, TOK), BF16), VMEM((16, 2048), F32),
                        VMEM((EXT, 128), F32), VMEM((EXT, 128), F32), VMEM((128, 2048), BF16)],
        compiler_params=pltpu.CompilerParams(dimension_semantics=("arbitrary",), vmem_limit_bytes=60 << 20),
        name="attention_back",
    )(*([fine] * 4 + [coarse] * 4 + [halo] * 3 + [wide] * 3 + [ao, iz, da]))


C0 = 0.7978845608028654
C1 = 0.044715


def middle_kernel(tok, ao, cot, wo, w1, w2, vecs, b1, out, dh1_out, da_out, gwo, gw1, gw2, gvec, gb1,
                  awo, aw1, aw2, avec, ab1):
    j = pl.program_id(0)

    @pl.when(j == 0)
    def _():
        awo[...] = jnp.zeros_like(awo)
        aw1[...] = jnp.zeros_like(aw1)
        aw2[...] = jnp.zeros_like(aw2)
        avec[...] = jnp.zeros_like(avec)
        ab1[...] = jnp.zeros_like(ab1)
    mixed = ao[...]
    h1 = tok[...].astype(F32) + mm(mixed, wo[...]) + vecs[5:6, :]
    center = h1 - jnp.mean(h1, axis=-1, keepdims=True)
    inverse = lax.rsqrt(jnp.mean(center * center, axis=-1, keepdims=True) + EPS)
    xh = center * inverse
    gain = vecs[6:7, :]
    a2 = (xh * gain + vecs[7:8, :]).astype(BF16)
    dy = cot[...]
    y = h1 + vecs[8:9, :]
    da2 = jnp.zeros((TILE, D), F32)
    for k in range(FF // D):
        cols = slice(D * k, D * k + D)
        u = mm(a2, w1[:, cols]) + b1[:, cols]
        u2 = u * u
        th = jnp.tanh(u * (C0 + (C0 * C1) * u2))
        half = 0.5 * (1.0 + th)
        g = (u * half).astype(BF16)
        slope = half + 0.5 * u * (1.0 - th * th) * (C0 + (3.0 * C0 * C1) * u2)
        y = y + mm(g, w2[cols, :])
        du = (mm_bt(dy, w2[cols, :]) * slope).astype(BF16)
        aw2[cols, :] += mm_at(g, dy)
        aw1[:, cols] += mm_at(a2, du)
        ab1[:, cols] += jnp.sum(du.astype(F32), axis=0, keepdims=True)
        da2 = da2 + mm_bt(du, w1[:, cols])
    out[...] = y.astype(BF16)
    dyf = dy.astype(F32)
    e = da2 * gain
    dh1 = dyf + inverse * (e - jnp.mean(e, axis=-1, keepdims=True) - xh * jnp.mean(e * xh, axis=-1, keepdims=True))
    dh1_out[...] = dh1
    db = dh1.astype(BF16)
    awo[...] += mm_at(mixed, db)
    da_out[...] = mm_bt(db, wo[...]).astype(BF16)
    avec[5:6, :] += jnp.sum(db.astype(F32), axis=0, keepdims=True)
    avec[6:7, :] += jnp.sum(da2 * xh, axis=0, keepdims=True)
    avec[7:8, :] += jnp.sum(da2, axis=0, keepdims=True)
    avec[8:9, :] += jnp.sum(dyf, axis=0, keepdims=True)

    @pl.when(j == TOK // TILE - 1)
    def _():
        gwo[...] = awo[...].astype(BF16)
        gw1[...] = aw1[...].astype(BF16)
        gw2[...] = aw2[...].astype(BF16)
        gvec[...] = avec[...]
        gb1[...] = ab1[...]


def whole(shape):
    return pl.BlockSpec(shape, lambda j: (0,) * len(shape), pipeline_mode=pl.Buffered(1))


def middle(tok, ao, cot, wo, w1, w2, vecs, b1):
    tile = pl.BlockSpec((TILE, D), lambda j: (j, 0))
    S = jax.ShapeDtypeStruct
    return pl.pallas_call(
        middle_kernel,
        grid=(TOK // TILE,),
        out_shape=[S((TOK, D), BF16), S((TOK, D), F32), S((TOK, D), BF16), S((D, D), BF16), S((D, FF), BF16), S((FF, D), BF16),
                   S((16, D), F32), S((1, FF), F32)],
        in_specs=[tile, tile, tile, whole((D, D)), whole((D, FF)), whole((FF, D)), whole((16, D)), whole((1, FF))],
        out_specs=[tile, tile, tile, whole((D, D)), whole((D, FF)), whole((FF, D)), whole((16, D)), whole((1, FF))],
        scratch_shapes=[VMEM((D, D), F32), VMEM((D, FF), F32), VMEM((FF, D), F32), VMEM((16, D), F32), VMEM((1, FF), F32)],
        compiler_params=pltpu.CompilerParams(dimension_semantics=("arbitrary",), vmem_limit_bytes=60 << 20),
        name="middle",
    )(tok, ao, cot, wo, w1, w2, vecs, b1)


def post_kernel(tok, a1, dq, ext, halo, wide, dh1, weight, vecs, out, gw, gvec, spt, kv, kvc, aw, avec):
    j = pl.program_id(0)

    @pl.when(j == 0)
    def _():
        fill_spread(spt)
        aw[...] = jnp.zeros_like(aw)
        avec[...] = jnp.zeros_like(avec)
        for half in range(2):
            lanes = slice(D * half, D * half + D)
            for l, size in enumerate(LEVEL_SIZE):
                at = EXT_AT[l] + 16
                dst, to = (kv, 0) if l == 0 else (kvc, COARSE_AT[l])
                shrink = 0.5 ** l if half == 0 else 1.0
                first, last = halo[0, l, half].astype(F32), halo[1, l, half].astype(F32)
                if size == 16:
                    v = ext[half, at:at + 16, :].astype(F32) + first + last
                    dst[to:to + 16, lanes] = (v * shrink).astype(BF16)
                    continue
                dst[to:to + 16, lanes] = ((ext[half, at:at + 16, :].astype(F32) + first) * shrink).astype(BF16)
                end = to + size - 16
                dst[end:end + 16, lanes] = ((ext[half, at + size - 16:at + size, :].astype(F32) + last) * shrink).astype(BF16)
                if size > 32:
                    dst[to + 16:end, lanes] = ext[half, at + 16:at + size - 16, :] * jnp.array(shrink, BF16)
            v = wide[0, half].astype(F32)
            for e in range(1, 8):
                v = v + wide[e, half].astype(F32)
            if half == 0:
                v = v * jnp.where(iota((16, D), 0) < 8, 0.5 ** 7, 0.5 ** 8)
            kvc[1008:1024, lanes] = v.astype(BF16)

    rows = pl.ds(pl.multiple_of(j * TILE, TILE), TILE)
    s = spt[rows, :]
    x1 = kvc[pl.ds(pl.multiple_of(j * 128, 128), 128), :]
    x2 = kvc[pl.ds(pl.multiple_of(512 + 128 * (j // 2), 128), 128), :]
    x3 = kvc[768:1024, :]
    dkv = (kv[rows, :].astype(F32) + mm(s[:, 0:128], x1) + mm(s[:, 128:256], x2) + mm(s[:, 256:512], x3)).astype(BF16)
    parts = (dq[...], dkv[:, 0:D], dkv[:, D:2 * D])
    a = a1[...]
    da1 = jnp.zeros((TILE, D), F32)
    for c in range(3):
        aw[c] += mm_at(a, parts[c])
        avec[2 + c:3 + c, :] += jnp.sum(parts[c].astype(F32), axis=0, keepdims=True)
        da1 = da1 + mm_bt(parts[c], weight[c])
    v = tok[...].astype(F32)
    center = v - jnp.mean(v, axis=-1, keepdims=True)
    inverse = lax.rsqrt(jnp.mean(center * center, axis=-1, keepdims=True) + EPS)
    xh = center * inverse
    e = da1 * vecs[0:1, :]
    dv = inverse * (e - jnp.mean(e, axis=-1, keepdims=True) - xh * jnp.mean(e * xh, axis=-1, keepdims=True))
    out[...] = (dh1[...] + dv).astype(BF16)
    avec[0:1, :] += jnp.sum(da1 * xh, axis=0, keepdims=True)
    avec[1:2, :] += jnp.sum(da1, axis=0, keepdims=True)

    @pl.when(j == TOK // TILE - 1)
    def _():
        gw[...] = aw[...].astype(BF16)
        gvec[...] = avec[...]


def after_attention(tok, a1, dq, ext, halo, wide, dh1, weight, vecs):
    tile = pl.BlockSpec((TILE, D), lambda j: (j, 0))
    S = jax.ShapeDtypeStruct
    return pl.pallas_call(
        post_kernel,
        grid=(TOK // TILE,),
        out_shape=[S((TOK, D), BF16), S((3, D, D), BF16), S((8, D), F32)],
        in_specs=[tile, tile, tile, whole((2, EXT, D)), whole((2, 7, 2, 16, D)), whole((8, 2, 16, D)), tile, whole((3, D, D)), whole((16, D))],
        out_specs=[tile, whole((3, D, D)), whole((8, D))],
        scratch_shapes=[VMEM((TOK, 512), BF16), VMEM((TOK, 2 * D), BF16), VMEM((TOK, 2 * D), BF16), VMEM((3, D, D), F32), VMEM((8, D), F32)],
        compiler_params=pltpu.CompilerParams(dimension_semantics=("arbitrary",), vmem_limit_bytes=60 << 20),
        name="after_attention",
    )(tok, a1, dq, ext, halo, wide, dh1, weight, vecs)


def where_am_i():
    h = lax.axis_index("head")
    s = lax.axis_index("span")
    return h, s, s // 4, (s // 2) % 2, s % 2


def peers_of(h, s, y, x, c):
    zs = [lax.rem(h + d, 4) for d in (1, 2, 3)]
    px = {"span": y * 4 + (1 - x) * 2 + c}
    py = {"span": (1 - y) * 4 + x * 2 + c}
    pc = {"span": y * 4 + x * 2 + 1 - c}
    return zs, px, py, pc


def gather_kernel(n, orders, *refs):
    ins, outs = refs[:n], refs[n:2 * n]
    lsem, ssem, rsem = refs[2 * n:]
    h, s, y, x, c = where_am_i()
    zs, px, py, pc = peers_of(h, s, y, x, c)
    greet([{"head": z} for z in zs] + [px, py, pc])
    pend = []
    zc = []
    for i in range(n):
        own = pltpu.make_async_copy(ins[i], outs[i].at[h, y, x, c], lsem.at[i])
        own.start()
        cs = []
        for k, z in enumerate(zs):
            cp = rcopy(ins[i], outs[i].at[h, y, x, c], ssem.at[i, k], rsem.at[i, k], {"head": z})
            cp.start()
            cs.append(cp)
        zc.append((own, cs))
    s2 = []
    for i in range(n):
        own, cs = zc[i]
        own.wait()
        for cp in cs:
            cp.wait()
        dev = px if orders[i] == 0 else py
        src = outs[i].at[:, y, x, c]
        cp = rcopy(src, src, ssem.at[i, 3], rsem.at[i, 3], dev)
        cp.start()
        s2.append(cp)
    s3 = []
    for i in range(n):
        s2[i].wait()
        if orders[i] == 0:
            src, dev = outs[i].at[:, y, :, c], py
        else:
            src, dev = outs[i].at[:, :, x, c], px
        cp = rcopy(src, src, ssem.at[i, 4], rsem.at[i, 4], dev)
        cp.start()
        s3.append(cp)
    s4 = []
    for i in range(n):
        s3[i].wait()
        src = outs[i].at[:, :, :, c]
        cp = rcopy(src, src, ssem.at[i, 5], rsem.at[i, 5], pc)
        cp.start()
        s4.append(cp)
    for cp in s4:
        cp.wait()


def gather_all(shards, orders, cid=0, space=pl.ANY):
    n = len(shards)
    return pl.pallas_call(
        functools.partial(gather_kernel, n, orders),
        out_shape=[jax.ShapeDtypeStruct((4, 2, 2, 2) + a.shape, a.dtype) for a in shards],
        in_specs=[pl.BlockSpec(memory_space=pl.ANY)] * n,
        out_specs=[pl.BlockSpec(memory_space=space)] * n,
        scratch_shapes=[pltpu.SemaphoreType.DMA((n,)), pltpu.SemaphoreType.DMA((n, 6)), pltpu.SemaphoreType.DMA((n, 6))],
        compiler_params=pltpu.CompilerParams(collective_id=cid, has_side_effects=True),
        name="gather_params",
    )(*shards)


def scatter_kernel(n, orders, *refs):
    ins, outs = refs[:n], refs[n:2 * n]
    a = 2 * n
    r1, r2, r3, r4 = (refs[a + k * n:a + (k + 1) * n] for k in range(4))
    ssem, rsem = refs[a + 4 * n:]
    h, s, y, x, c = where_am_i()
    zs, px, py, pc = peers_of(h, s, y, x, c)
    greet([{"head": z} for z in zs] + [px, py, pc])
    cs = []
    for i in range(n):
        cp = rcopy(ins[i].at[:, :, :, 1 - c], r1[i], ssem.at[i, 0], rsem.at[i, 0], pc)
        cp.start()
        cs.append(cp)
    s2 = []
    for i in range(n):
        cs[i].wait()

        @pl.loop(0, 4)
        def _(hh):
            for yy in range(2):
                for xx in range(2):
                    r1[i][hh, yy, xx] = (r1[i][hh, yy, xx].astype(F32) + ins[i][hh, yy, xx, c].astype(F32)).astype(r1[i].dtype)
        if orders[i] == 0:
            src, dev = r1[i].at[:, :, 1 - x], px
        else:
            src, dev = r1[i].at[:, 1 - y], py
        cp = rcopy(src, r2[i], ssem.at[i, 1], rsem.at[i, 1], dev)
        cp.start()
        s2.append(cp)
    s3 = []
    for i in range(n):
        s2[i].wait()

        @pl.loop(0, 4)
        def _(hh):
            for v in range(2):
                mine = r1[i][hh, v, x] if orders[i] == 0 else r1[i][hh, y, v]
                r2[i][hh, v] = (r2[i][hh, v].astype(F32) + mine.astype(F32)).astype(r2[i].dtype)
        if orders[i] == 0:
            src, dev = r2[i].at[:, 1 - y], py
        else:
            src, dev = r2[i].at[:, 1 - x], px
        cp = rcopy(src, r3[i], ssem.at[i, 2], rsem.at[i, 2], dev)
        cp.start()
        s3.append(cp)
    s4 = []
    for i in range(n):
        s3[i].wait()
        me = y if orders[i] == 0 else x

        @pl.loop(0, 4)
        def _(hh):
            r3[i][hh] = (r3[i][hh].astype(F32) + r2[i][hh, me].astype(F32)).astype(r3[i].dtype)
        zz = []
        for k, z in enumerate(zs):
            cp = rcopy(r3[i].at[z], r4[i].at[k], ssem.at[i, 3 + k], rsem.at[i, 3 + k], {"head": z})
            cp.start()
            zz.append(cp)
        s4.append(zz)
    for i in range(n):
        for cp in s4[i]:
            cp.wait()
        acc = r3[i][h].astype(F32)
        for k in range(3):
            acc = acc + r4[i][k].astype(F32)
        outs[i][...] = acc


def scatter_all(grads, orders, cid=1):
    n = len(grads)
    sh = [g.shape[4:] for g in grads]
    V = pltpu.VMEM
    return pl.pallas_call(
        functools.partial(scatter_kernel, n, orders),
        out_shape=[jax.ShapeDtypeStruct(s, F32) for s in sh],
        in_specs=[pl.BlockSpec(memory_space=pltpu.VMEM)] * n,
        out_specs=[pl.BlockSpec(memory_space=pltpu.VMEM)] * n,
        scratch_shapes=[V((4, 2, 2) + s, g.dtype) for s, g in zip(sh, grads)]
        + [V((4, 2) + s, g.dtype) for s, g in zip(sh, grads)]
        + [V((4,) + s, g.dtype) for s, g in zip(sh, grads)]
        + [V((3,) + s, g.dtype) for s, g in zip(sh, grads)]
        + [pltpu.SemaphoreType.DMA((n, 6)), pltpu.SemaphoreType.DMA((n, 6))],
        compiler_params=pltpu.CompilerParams(collective_id=cid, has_side_effects=True, vmem_limit_bytes=60 << 20),
        name="scatter_grads",
    )(*grads)


BOTH = ("head", "span")


def pack_vectors(first_gain, first_shift, project_bias, output_bias, second_gain, second_shift, reduce_bias, expand_bias):
    a = jnp.stack([first_gain, first_shift, project_bias[0], project_bias[1], project_bias[2], output_bias, second_gain, second_shift])
    b = jnp.pad(reduce_bias[None, :], ((0, 7), (0, 0)))
    return jnp.concatenate([a, b, expand_bias.reshape(8, 8), jnp.zeros((8, 88), F32)], axis=1)


def unpack_vectors(g):
    vecs = g[:, :, 0:32].reshape(32, 8, 2, 16).transpose(2, 1, 0, 3).reshape(16, D)
    return vecs, g[:, :, 32:40].reshape(1, FF)


def pack_gradients(vec, b1):
    a = vec[0:8].reshape(8, 32, 16).transpose(1, 0, 2)
    b = jnp.pad(vec[8].reshape(32, 1, 16), ((0, 0), (0, 7), (0, 0)))
    return jnp.concatenate([a, b, b1.reshape(32, 8, 8), jnp.zeros((32, 8, 88), F32)], axis=2)


def shards(tokens, segment_ids, first_gain, first_shift, project_weight, project_bias, output_weight, output_bias,
           second_gain, second_shift, expand_weight, expand_bias, reduce_weight, reduce_bias, cotangent):
    tok, cot = tokens[0], cotangent[0]
    near = lax.axis_size("head") == 4 and lax.axis_size("span") == 8
    if near:
        packed = pack_vectors(first_gain, first_shift, project_bias, output_bias, second_gain, second_shift, reduce_bias, expand_bias)
        wq, wo, w1, w2, vec = gather_all([project_weight.reshape(48, D), output_weight, expand_weight, reduce_weight, packed], ORDERS)
        wq = wq.reshape(32, 3, 16, D).transpose(1, 0, 2, 3).reshape(3, D, D)
        wo, w1, w2 = wo.reshape(D, D), w1.reshape(D, FF), w2.reshape(FF, D)
        vecs, b1 = unpack_vectors(vec.reshape(32, 8, 128))
    else:
        def full(v, axis=0):
            return lax.all_gather(v, BOTH, axis=axis, tiled=True)
        wq, wo, w1, w2 = full(project_weight, 1), full(output_weight), full(expand_weight), full(reduce_weight)
        rows = [full(first_gain), full(first_shift), *full(project_bias, 1), full(output_bias), full(second_gain), full(second_shift), full(reduce_bias)]
        vecs = jnp.pad(jnp.stack(rows), ((0, 7), (0, 0)))
        b1 = full(expand_bias)[None]
    a1, fine, coarse = before_attention(tok, segment_ids, wq, vecs)
    halo, wide = exchange_edges(fine, coarse)
    ao, iz = attention(fine, coarse, halo, wide)
    out, dh1, da, gwo, gw1, gw2, gvec, gb1 = middle(tok, ao, cot, wo, w1, w2, vecs, b1)
    dq, ext = attention_back(fine, coarse, halo, wide, ao, iz, da)
    halo_b, wide_b = return_edges(ext)
    dtok, gwq, gvec_b = after_attention(tok, a1, dq, ext, halo_b, wide_b, dh1, wq, vecs)
    vec = jnp.concatenate([gvec_b[0:5], gvec[5:9]], axis=0)
    if near:
        grid = (4, 2, 2, 2)
        sums = scatter_all([gwq.reshape(3, 32, 16, D).transpose(1, 0, 2, 3).reshape(grid + (48, D)), gwo.reshape(grid + (16, D)),
                            gw1.reshape(grid + (16, FF)), gw2.reshape(grid + (64, D)), pack_gradients(vec, gb1).reshape(grid + (8, 128))], ORDERS)
        gwq, gwo, gw1, gw2, packed = sums
        gwq = gwq.reshape(3, 16, D)
        row = [packed[r, 0:16] for r in range(8)]
        small = (row[0], row[1], packed[2:5, 0:16], row[5], row[6], row[7], packed[:, 32:40].reshape(64), packed[0, 16:32])
    else:
        def part(v, axis=0):
            return lax.psum_scatter(v.astype(F32), BOTH, scatter_dimension=axis, tiled=True)
        gwq, gwo, gw1, gw2 = part(gwq, 1), part(gwo), part(gw1), part(gw2)
        small = (part(vec[0]), part(vec[1]), part(vec[2:5], 1), part(vec[5]), part(vec[6]), part(vec[7]), part(gb1[0]), part(vec[8]))
    return (out[None], dtok[None], small[0], small[1], gwq, small[2], gwo, small[3], small[4], small[5], gw1, small[6], gw2, small[7])


ORDERS = (1, 0, 0, 1, 0)


def solution(mesh):
    token, row, matrix = P("span", "head", None), P(BOTH), P(BOTH, None)
    three, bias = P(None, BOTH, None), P(None, BOTH)
    params = (row, row, three, bias, matrix, row, row, row, matrix, row, matrix, row)
    return jax.shard_map(shards, mesh=mesh, in_specs=(token, P("span", None)) + params + (token,),
                         out_specs=(token, token) + params, check_vma=False)
```

```python
import functools
import jax
import jax.numpy as jnp
from jax import lax
from jax.experimental import pallas as pl
from jax.experimental.pallas import tpu as pltpu
from jax.sharding import PartitionSpec as P

F32, BF16, I32 = jnp.float32, jnp.bfloat16, jnp.int32
MESH = pl.DeviceIdType.MESH
VMEM = pltpu.VMEM
NEG = -1e30
EPS = 1e-5
TOK = 1024
TILE = 256
D = 512
FF = 2048
EXT = 2384
LEVEL_SIZE = (1024, 512, 256, 128, 64, 32, 16)
COARSE_AT = (None, 0, 512, 768, 896, 960, 992)
EXT_AT = (0, 1056, 1600, 1888, 2048, 2144, 2208)
WIDE_AT = 2256
TRANS_B = (((1,), (1,)), ((), ()))
TRANS_A = (((0,), (0,)), ((), ()))


def mm(a, b):
    return jnp.dot(a, b, preferred_element_type=F32)


def mm_bt(a, b):
    return lax.dot_general(a, b, TRANS_B, preferred_element_type=F32)


def mm_at(a, b):
    return lax.dot_general(a, b, TRANS_A, preferred_element_type=F32)


def iota(shape, dim):
    return lax.broadcasted_iota(I32, shape, dim)


def split(v):
    high = v.astype(BF16)
    return high, (v - high.astype(F32)).astype(BF16)


def covers(t, c, block):
    if block == 0:
        return ((t & 255) >> 1) == c
    if block == 1:
        return ((t & 511) >> 2) == c
    if block == 2:
        return (t >> 3) == c
    level, start = mixed_levels(c)
    return (jnp.right_shift(t, level) == c - start) & (c < 124)


def mixed_levels(c):
    a, b, d, e = ((c >= edge).astype(I32) for edge in (64, 96, 112, 120))
    return 4 + a + b + d + e, 64 * a + 32 * b + 16 * d + 8 * e


def ones_where(cond):
    return jnp.where(cond, 1.0, 0.0).astype(BF16)


def identity(n):
    return ones_where(iota((n, n), 0) == iota((n, n), 1))


def fill_spread(spt):
    @pl.loop(0, TOK // TILE)
    def _(j):
        for block in range(4):
            t = iota((TILE, 128), 0) + j * TILE
            c = iota((TILE, 128), 1)
            spt[pl.ds(j * TILE, TILE), 128 * block:128 * block + 128] = ones_where(covers(t, c, block))


def fill_pool(sp):
    @pl.loop(0, TOK // TILE)
    def _(j):
        for block in range(4):
            t = iota((128, TILE), 1) + j * TILE
            c = iota((128, TILE), 0)
            sp[128 * block:128 * block + 128, pl.ds(pl.multiple_of(j * TILE, TILE), TILE)] = ones_where(covers(t, c, block))


def pre_kernel(tok, seg, weight, vecs, a1_out, fine, coarse, acc, acc_ids):
    j = pl.program_id(0)
    h = lax.axis_index("head")
    v = tok[...].astype(F32)
    center = v - jnp.mean(v, axis=-1, keepdims=True)
    inverse = lax.rsqrt(jnp.mean(center * center, axis=-1, keepdims=True) + EPS)
    a1 = (center * inverse * vecs[0:1, :] + vecs[1:2, :]).astype(BF16)
    a1_out[...] = a1
    for part in range(3):
        r = (mm(a1, weight[part]) + vecs[2 + part:3 + part, :]).astype(BF16)
        if part == 0:
            r = r * jnp.array(0.125, BF16)
        fine[:, D * part:D * part + D] = r
    ids = seg[:, pl.ds(pl.multiple_of(h * TOK + j * TILE, TILE), TILE)].astype(F32)
    ids_b = jnp.broadcast_to(ids, (128, TILE)).astype(BF16)
    sq_b = jnp.broadcast_to(ids * ids, (128, TILE)).astype(BF16)
    fine[:, 3 * D:3 * D + 128] = mm_bt(identity(TILE), ids_b).astype(BF16)
    c, t = iota((192, TILE), 0), iota((192, TILE), 1)
    near = ones_where(jnp.where(c < 128, t >> 1, (t >> 2) + 128) == c)
    x = fine[:, 0:3 * D]
    r = mm(near, x)
    lab = labels_of(mm_bt(near, ids_b), mm_bt(near, sq_b), jnp.where(iota((192, 128), 0) < 128, 2.0, 4.0))
    at1, at2 = pl.multiple_of(j * 128, 128), pl.multiple_of(512 + j * 64, 64)
    coarse[pl.ds(at1, 128), 0:2 * D] = (r[0:128, 0:2 * D] * 0.5).astype(BF16)
    coarse[pl.ds(at1, 128), 2 * D:3 * D] = r[0:128, 2 * D:].astype(BF16)
    coarse[pl.ds(at1, 128), 3 * D:] = lab[0:128].astype(BF16)
    coarse[pl.ds(at2, 64), 0:2 * D] = (r[128:192, 0:2 * D] * 0.25).astype(BF16)
    coarse[pl.ds(at2, 64), 2 * D:3 * D] = r[128:192, 2 * D:].astype(BF16)
    coarse[pl.ds(at2, 64), 3 * D:] = lab[128:192].astype(BF16)
    tt, cc = iota((128, TILE), 1) + j * TILE, iota((128, TILE), 0)
    far = jnp.concatenate([ones_where(covers(tt, cc, 2)), ones_where(covers(tt, cc, 3))], axis=0)

    @pl.when(j == 0)
    def _():
        acc[...] = jnp.zeros_like(acc)
        acc_ids[...] = jnp.zeros_like(acc_ids)
    acc[...] += mm(far, x)
    acc_ids[:, 0:128] += mm_bt(far, ids_b)
    acc_ids[:, 128:256] += mm_bt(far, sq_b)

    @pl.when(j == TOK // TILE - 1)
    def _():
        row = iota((TILE, 128), 0)
        level, _unused = mixed_levels(row - 128)
        times = jnp.where(row < 128, 8.0, (1 << level).astype(F32))
        lab = labels_of(acc_ids[:, 0:128], acc_ids[:, 128:256], times)
        shrink = 1.0 / times
        for k in range(8):
            coarse[768:1024, 128 * k:128 * k + 128] = (acc[:, 128 * k:128 * k + 128] * shrink).astype(BF16)
        coarse[768:1024, 2 * D:3 * D] = acc[:, 2 * D:].astype(BF16)
        coarse[768:1024, 3 * D:] = lab.astype(BF16)


def labels_of(total, squares, times):
    return jnp.where(times * squares == total * total, total / times, 0.0)


def before_attention(tok, seg, weight, vecs):
    wide = 3 * D + 128
    return pl.pallas_call(
        pre_kernel,
        grid=(TOK // TILE,),
        out_shape=[jax.ShapeDtypeStruct((TOK, D), BF16), jax.ShapeDtypeStruct((TOK, wide), BF16),
                   jax.ShapeDtypeStruct((TOK, wide), BF16)],
        in_specs=[pl.BlockSpec((TILE, D), lambda j: (j, 0)),
                  pl.BlockSpec(seg.shape, lambda j: (0, 0)),
                  pl.BlockSpec((3, D, D), lambda j: (0, 0, 0), pipeline_mode=pl.Buffered(1)),
                  pl.BlockSpec((16, D), lambda j: (0, 0))],
        out_specs=[pl.BlockSpec((TILE, D), lambda j: (j, 0)), pl.BlockSpec((TILE, wide), lambda j: (j, 0)),
                   pl.BlockSpec((TOK, wide), lambda j: (0, 0))],
        scratch_shapes=[VMEM((TILE, 3 * D), F32), VMEM((TILE, 256), F32)],
        compiler_params=pltpu.CompilerParams(dimension_semantics=("arbitrary",), vmem_limit_bytes=60 << 20),
        name="before_attention",
    )(tok, seg, weight, vecs)


def row_place():
    h, s = lax.axis_index("head"), lax.axis_index("span")
    return (s % 2) * 4 + h


def row_device(place):
    s = lax.axis_index("span")
    return {"head": place % 4, "span": (s // 2) * 2 + place // 4}


def greet(devices):
    barrier = pltpu.get_barrier_semaphore()
    for d in devices:
        pl.semaphore_signal(barrier, inc=1, device_id=d, device_id_type=MESH)
    pl.semaphore_wait(barrier, len(devices))


def rcopy(src, dst, send, recv, device):
    return pltpu.make_async_remote_copy(src_ref=src, dst_ref=dst, send_sem=send, recv_sem=recv,
                                        device_id=device, device_id_type=MESH)


def edges_kernel(fine, coarse, halo, wide, local, send, recv):
    p = row_place()
    others = [lax.rem(p + d, 8) for d in range(1, 8)]
    greet([row_device(o) for o in others])
    right, left = row_device(others[0]), row_device(others[6])
    lanes = pl.ds(D, 2 * D + 128)
    copies = []
    for l, size in enumerate(LEVEL_SIZE):
        src, at = (fine, 0) if l == 0 else (coarse, COARSE_AT[l])
        copies.append(rcopy(src.at[pl.ds(at + size - 16, 16), lanes], halo.at[0, l], send.at[l], recv.at[l], right))
        copies.append(rcopy(src.at[pl.ds(at, 16), lanes], halo.at[1, l], send.at[7 + l], recv.at[7 + l], left))
    block = coarse.at[pl.ds(1008, 16), lanes]
    for d in range(1, 8):
        copies.append(rcopy(block, wide.at[p], send.at[13 + d], recv.at[13 + d], row_device(others[d - 1])))
    for cp in copies:
        cp.start()
    own = pltpu.make_async_copy(block, wide.at[p], local)
    own.start()
    own.wait()
    for cp in copies:
        cp.wait()


def exchange_edges(fine, coarse):
    lanes = 2 * D + 128
    return pl.pallas_call(
        edges_kernel,
        out_shape=[jax.ShapeDtypeStruct((2, 7, 16, lanes), BF16), jax.ShapeDtypeStruct((8, 16, lanes), BF16)],
        in_specs=[pl.BlockSpec(memory_space=pl.ANY)] * 2,
        out_specs=[pl.BlockSpec(memory_space=pl.ANY)] * 2,
        scratch_shapes=[pltpu.SemaphoreType.DMA, pltpu.SemaphoreType.DMA((21,)), pltpu.SemaphoreType.DMA((21,))],
        compiler_params=pltpu.CompilerParams(collective_id=2, has_side_effects=True),
        name="exchange_edges",
    )(fine, coarse)


def edges_back_kernel(ext, halo, wide, local, send, recv):
    p = row_place()
    others = [lax.rem(p + d, 8) for d in range(1, 8)]
    greet([row_device(o) for o in others])
    right, left = row_device(others[0]), row_device(others[6])
    copies = []
    for l, size in enumerate(LEVEL_SIZE):
        at = EXT_AT[l]
        copies.append(rcopy(ext.at[:, pl.ds(at + 16 + size, 16)], halo.at[0, l], send.at[l], recv.at[l], right))
        copies.append(rcopy(ext.at[:, pl.ds(at, 16)], halo.at[1, l], send.at[7 + l], recv.at[7 + l], left))
    for d in range(1, 8):
        o = others[d - 1]
        copies.append(rcopy(ext.at[:, pl.ds(pl.multiple_of(WIDE_AT + 16 * o, 16), 16)], wide.at[p], send.at[13 + d], recv.at[13 + d], row_device(o)))
    for cp in copies:
        cp.start()
    own = pltpu.make_async_copy(ext.at[:, pl.ds(pl.multiple_of(WIDE_AT + 16 * p, 16), 16)], wide.at[p], local)
    own.start()
    own.wait()
    for cp in copies:
        cp.wait()


def return_edges(ext):
    return pl.pallas_call(
        edges_back_kernel,
        out_shape=[jax.ShapeDtypeStruct((2, 7, 2, 16, D), BF16), jax.ShapeDtypeStruct((8, 2, 16, D), BF16)],
        in_specs=[pl.BlockSpec(memory_space=pl.ANY)],
        out_specs=[pl.BlockSpec(memory_space=pl.ANY)] * 2,
        scratch_shapes=[pltpu.SemaphoreType.DMA, pltpu.SemaphoreType.DMA((21,)), pltpu.SemaphoreType.DMA((21,))],
        compiler_params=pltpu.CompilerParams(collective_id=3, has_side_effects=True),
        name="return_edges",
    )(ext)


def build_ext(dst, x0, xc, halo, wide, first=None, last=None):
    def put(at, v):
        dst[at:at + v.shape[0], :] = v.astype(dst.dtype)

    for l, size in enumerate(LEVEL_SIZE):
        at = EXT_AT[l]
        a, b = halo[0, l], halo[1, l]
        if first is not None:
            a, b = a.astype(F32) * first, b.astype(F32) * last
        put(at, a)
        put(at + 16, x0[...] if l == 0 else xc[COARSE_AT[l]:COARSE_AT[l] + size, :])
        put(at + 16 + size, b)
    for e in range(8):
        put(WIDE_AT + 16 * e, wide[e])


def fill_bias(bias, bias_mixed, lx, l0, lc, hl, rl):
    p = row_place()
    build_ext(lx, l0, lc, hl, rl, jnp.where(p > 0, 1.0, 0.0), jnp.where(p < 7, 1.0, 0.0))

    def matching(at, size, q):
        kl = lx[pl.ds(at, size), :]
        ql = jnp.transpose(q.astype(F32))[0:1, :]
        return (kl == ql) & (kl != 0.0)

    r, c = iota((160, 128), 0), iota((160, 128), 1)
    near = jnp.abs((r >> 4) - 1 - (c >> 4)) <= 1
    far = near & (jnp.abs((r >> 3) - 2 - (c >> 3)) >= 2)
    same = (r - 16) == c

    @pl.loop(0, 8)
    def _(i):
        at = pl.multiple_of(128 * i, 16)
        ok = matching(at, 160, l0[pl.ds(at, 128), :]) & near | same
        bias[pl.ds(pl.multiple_of(160 * i, 16), 160), :] = jnp.where(ok, 0.0, NEG)

    @pl.loop(8, 15)
    def _(i):
        q = lc[pl.ds(pl.multiple_of(128 * (i - 8), 16), 128), :]
        ok = matching(tile_at(i), 160, q) & far
        bias[pl.ds(pl.multiple_of(160 * i, 16), 160), :] = jnp.where(ok, 0.0, NEG)

    r, c = iota((336, 128), 0), iota((336, 128), 1)
    inner = (r >= 96).astype(I32) + (r >= 160).astype(I32)
    start = jnp.where(inner == 0, 0, jnp.where(inner == 1, 96, 160))
    e, k = (r - 208) >> 4, (r - 208) & 15
    upper = (k >= 8).astype(I32)
    level_k = jnp.where(r < 208, 4 + inner, 7 + upper)
    pos_k = jnp.where(r < 208, r - start - 16, jnp.where(k < 8, e * 8 + k, e * 4 + k - 8))
    level_q, start_q = mixed_levels(c)
    pos_q = c - start_q + jnp.where(level_q == 7, p * 8, jnp.where(level_q == 8, p * 4, 0))
    shape = (level_k == level_q) & (jnp.abs((pos_k >> 4) - (pos_q >> 4)) <= 1) & (jnp.abs((pos_k >> 3) - (pos_q >> 3)) >= 2)
    ok = matching(2048, 336, lc[896:1024, :]) & shape
    bias_mixed[...] = jnp.where(ok, 0.0, NEG)


def tile_at(i):
    level = (i >= 8).astype(I32) + (i >= 12).astype(I32) + (i >= 14).astype(I32)
    return pl.multiple_of(128 * i + 32 * level, 16)


def tile_times(i):
    level = (i >= 8).astype(I32) + (i >= 12).astype(I32) + (i >= 14).astype(I32)
    return (1 << level).astype(F32)


def mixed_times(shape):
    level, _unused = mixed_levels(iota(shape, len(shape) - 1))
    return (1 << level).astype(F32)


def head_masks(rows):
    lane = iota((rows, 128), 1)
    return ones_where(lane < 64), ones_where(lane >= 64)


def by_head(x, masks):
    return jnp.concatenate([x * masks[0], x * masks[1]], axis=0)


def own_blocks(x):
    return jnp.concatenate([x[0:64, 0:128], x[64:128, 128:256]], axis=0)


def twice(x):
    return jnp.concatenate([x, x], axis=1)


def coarse_columns(ref, j):
    pair = pl.multiple_of(1536 + 128 * (j // 2), 128)
    return jnp.concatenate([ref[:, pl.ds(pl.multiple_of(1024 + 128 * j, 128), 128)], ref[:, pl.ds(pair, 128)],
                            ref[:, 1792:2048]], axis=1)


def attention_kernel(n, orders, q0, k0, v0, l0, qc, kc, vc, lc, hk, hv, hl, rk, rv, rl, *refs):
    ins, (ao_out, iz_out), outs = refs[:n], refs[n:n + 2], refs[n + 2:2 * n + 2]
    kx, vx, qx, bias, bias_mixed, lx, spt, nz, *sems = refs[2 * n + 2:]
    g = pl.program_id(0)
    steps = []
    if n:
        steps = gather_steps(ins, outs, orders, *sems)
        pl.when(g == 0)(greet_all)
        for k in range(4):
            pl.when(g == k)(steps[k])

    @pl.when(g == 0)
    def _():
        fill_bias(bias, bias_mixed, lx, l0, lc, hl, rl)
        fill_spread(spt)
    build_ext(kx, k0, kc, hk, rk)
    build_ext(vx, v0, vc, hv, rv)
    qx[0:1024, :] = q0[...]
    qx[1024:2048, :] = qc[...]
    masks = head_masks(128)

    def tile(at, size, i, b, times):
        kw, vw = kx[pl.ds(at, size), :], vx[pl.ds(at, size), :]
        q = by_head(qx[pl.ds(pl.multiple_of(128 * i, 128), 128), :], masks)
        e = jnp.exp(mm_bt(kw, q) + twice(b))
        z = jnp.sum(e, axis=0, keepdims=True) * times
        n = own_blocks(mm_at(vw, e.astype(BF16)))
        zb = jnp.concatenate([jnp.broadcast_to(z[:, 0:128], (64, 128)), jnp.broadcast_to(z[:, 128:256], (64, 128))], axis=0)
        cols = pl.ds(pl.multiple_of(128 * i, 128), 128)
        nz[0:128, cols] = n.astype(BF16)
        nz[128:256, cols] = zb.astype(BF16)

    def body(i, carry):
        tile(tile_at(i), 160, i, bias[pl.ds(pl.multiple_of(160 * i, 16), 160), :], tile_times(i))
        return carry
    lax.fori_loop(0, 15, body, 0, unroll=5)
    tile(2048, 336, 15, bias_mixed[...], twice(mixed_times((1, 128))))
    eye = identity(TILE)

    @pl.loop(0, TOK // TILE)
    def _(j):
        rows = pl.ds(pl.multiple_of(j * TILE, TILE), TILE)
        r = mm_bt(eye, nz[:, rows]) + mm_bt(spt[rows, :], coarse_columns(nz, j))
        inverse = 1.0 / r[:, 128:256]
        iz_out[rows, :] = inverse
        ao_out[rows, :] = (r[:, 0:128] * inverse).astype(BF16)
    if n:
        pl.when(g == 3)(steps[4])


def pair_specs():
    def cols(shift):
        return pl.BlockSpec((TOK, 128), lambda g, shift=shift: (0, g + shift))
    label = pl.BlockSpec((TOK, 128), lambda g: (0, 12))
    each = [cols(0), cols(4), cols(8), label]
    halo = [pl.BlockSpec((2, 7, 16, 128), lambda g, s=s: (0, 0, 0, g + s)) for s in (0, 4)]
    halo.append(pl.BlockSpec((2, 7, 16, 128), lambda g: (0, 0, 0, 8)))
    wide = [pl.BlockSpec((8, 16, 128), lambda g, s=s: (0, 0, g + s)) for s in (0, 4)]
    wide.append(pl.BlockSpec((8, 16, 128), lambda g: (0, 0, 8)))
    return each + each + halo + wide


def attention(fine, coarse, halo, wide, parts, orders):
    out = pl.BlockSpec((TOK, 128), lambda g: (0, g))
    n = len(parts)
    anywhere = pl.BlockSpec(memory_space=pl.ANY)
    sems = [pltpu.SemaphoreType.DMA((n,)), pltpu.SemaphoreType.DMA((n, 6)), pltpu.SemaphoreType.DMA((n, 6))] if n else []
    remote = dict(collective_id=4, has_side_effects=True) if n else {}
    return pl.pallas_call(
        functools.partial(attention_kernel, n, orders),
        grid=(4,),
        out_shape=[jax.ShapeDtypeStruct((TOK, D), BF16), jax.ShapeDtypeStruct((TOK, D), F32)]
        + [jax.ShapeDtypeStruct((4, 2, 2, 2) + a.shape, a.dtype) for a in parts],
        in_specs=pair_specs() + [anywhere] * n,
        out_specs=[out, out] + [anywhere] * n,
        scratch_shapes=[VMEM((EXT, 128), BF16), VMEM((EXT, 128), BF16), VMEM((2048, 128), BF16),
                        VMEM((15 * 160, 128), F32), VMEM((336, 128), F32), VMEM((EXT, 128), F32),
                        VMEM((TOK, 512), BF16), VMEM((256, 2048), BF16)] + sems,
        compiler_params=pltpu.CompilerParams(dimension_semantics=("arbitrary",), vmem_limit_bytes=60 << 20, **remote),
        name="attention",
    )(*([fine] * 4 + [coarse] * 4 + [halo] * 3 + [wide] * 3), *parts)


def attention_back_kernel(q0, k0, v0, l0, qc, kc, vc, lc, hk, hv, hl, rk, rv, rl, ao, iz, da, dq_out, ext_out,
                          kx, vx, qx, gx, bias, bias_mixed, lx, spt, sp, rm, dk, dv, dqt):
    g = pl.program_id(0)

    @pl.when(g == 0)
    def _():
        fill_bias(bias, bias_mixed, lx, l0, lc, hl, rl)
        fill_spread(spt)
        fill_pool(sp)
    build_ext(kx, k0, kc, hk, rk)
    build_ext(vx, v0, vc, hv, rv)
    qx[0:1024, :] = q0[...]
    qx[1024:2048, :] = qc[...]
    heads = ones_where(iota((16, 128), 0) == (iota((16, 128), 1) >> 6))

    @pl.loop(0, TOK // TILE)
    def _(j):
        rows = pl.ds(pl.multiple_of(j * TILE, TILE), TILE)
        gf = da[rows, :].astype(F32) * iz[rows, :]
        gx[rows, :] = gf.astype(BF16)
        high, low = split(gf * ao[rows, :].astype(F32))
        rm[:, rows] = mm_bt(heads, high) + mm_bt(heads, low)

    def pooled(c_rows, t_rows, dst):
        s = sp[c_rows, t_rows]
        gx[dst, :] = mm(s, gx[t_rows, :]).astype(BF16)
        high, low = split(rm[:, t_rows])
        return mm_bt(high, s) + mm_bt(low, s)

    @pl.loop(0, 4)
    def _(j):
        dst = pl.ds(pl.multiple_of(1024 + 128 * j, 128), 128)
        rm[:, dst] = pooled(pl.ds(0, 128), pl.ds(pl.multiple_of(j * 256, 256), 256), dst) * 2.0

    for j in range(2):
        dst = pl.ds(1536 + 128 * j, 128)
        rm[:, dst] = pooled(pl.ds(128, 128), pl.ds(j * 512, 512), dst) * 4.0
    rm[:, pl.ds(1792, 128)] = pooled(pl.ds(256, 128), pl.ds(0, 1024), pl.ds(1792, 128)) * 8.0
    rm[:, pl.ds(1920, 128)] = pooled(pl.ds(384, 128), pl.ds(0, 1024), pl.ds(1920, 128)) * mixed_times((16, 128))
    dk[...] = jnp.zeros_like(dk)
    dv[...] = jnp.zeros_like(dv)
    masks = head_masks(128)

    def tile(at, size, i, b, shrink):
        keys = pl.ds(at, size)
        cols = pl.ds(pl.multiple_of(128 * i, 128), 128)
        kw, vw = kx[keys, :], vx[keys, :]
        q, gg = by_head(qx[cols, :], masks), by_head(gx[cols, :], masks)
        e = jnp.exp(mm_bt(kw, q) + twice(b))
        rest = jnp.concatenate([rm[0:1, cols], rm[1:2, cols]], axis=1)
        ds = (e * (mm_bt(vw, gg) - rest)).astype(BF16)
        dk[keys, :] += mm(ds, q)
        dv[keys, :] += mm(e.astype(BF16), gg)
        dqt[:, cols] = (own_blocks(mm_at(kw, ds)) * shrink).astype(BF16)

    def body(i, carry):
        tile(tile_at(i), 160, i, bias[pl.ds(pl.multiple_of(160 * i, 16), 160), :], 0.125 / tile_times(i))
        return carry
    lax.fori_loop(0, 15, body, 0, unroll=5)
    tile(2048, 336, 15, bias_mixed[...], 0.125 / mixed_times((1, 128)))
    eye = identity(TILE)

    @pl.loop(0, TOK // TILE)
    def _(j):
        rows = pl.ds(pl.multiple_of(j * TILE, TILE), TILE)
        dq_out[rows, :] = (mm_bt(eye, dqt[:, rows]) + mm_bt(spt[rows, :], coarse_columns(dqt, j))).astype(BF16)
    ext_out[0] = dk[...].astype(BF16)
    ext_out[1] = dv[...].astype(BF16)


def attention_back(fine, coarse, halo, wide, ao, iz, da):
    pair = pl.BlockSpec((TOK, 128), lambda g: (0, g))
    ext = pl.BlockSpec((2, EXT, 128), lambda g: (0, 0, g))
    return pl.pallas_call(
        attention_back_kernel,
        grid=(4,),
        out_shape=[jax.ShapeDtypeStruct((TOK, D), BF16), jax.ShapeDtypeStruct((2, EXT, D), BF16)],
        in_specs=pair_specs() + [pair, pair, pair],
        out_specs=[pair, ext],
        scratch_shapes=[VMEM((EXT, 128), BF16), VMEM((EXT, 128), BF16), VMEM((2048, 128), BF16), VMEM((2048, 128), BF16),
                        VMEM((15 * 160, 128), F32), VMEM((336, 128), F32), VMEM((EXT, 128), F32),
                        VMEM((TOK, 512), BF16), VMEM((512, TOK), BF16), VMEM((16, 2048), F32),
                        VMEM((EXT, 128), F32), VMEM((EXT, 128), F32), VMEM((128, 2048), BF16)],
        compiler_params=pltpu.CompilerParams(dimension_semantics=("arbitrary",), vmem_limit_bytes=60 << 20),
        name="attention_back",
    )(*([fine] * 4 + [coarse] * 4 + [halo] * 3 + [wide] * 3 + [ao, iz, da]))


C0 = 0.7978845608028654
C1 = 0.044715


def middle_kernel(tok, ao, cot, wo, w1, w2, vecs, b1, out, dh1_out, da_out, gwo, gw1, gw2, gvec, gb1,
                  awo, aw1, aw2, avec, ab1):
    j = pl.program_id(0)

    @pl.when(j == 0)
    def _():
        awo[...] = jnp.zeros_like(awo)
        aw1[...] = jnp.zeros_like(aw1)
        aw2[...] = jnp.zeros_like(aw2)
        avec[...] = jnp.zeros_like(avec)
        ab1[...] = jnp.zeros_like(ab1)
    mixed = ao[...]
    h1 = tok[...].astype(F32) + mm(mixed, wo[...]) + vecs[5:6, :]
    center = h1 - jnp.mean(h1, axis=-1, keepdims=True)
    inverse = lax.rsqrt(jnp.mean(center * center, axis=-1, keepdims=True) + EPS)
    xh = center * inverse
    gain = vecs[6:7, :]
    a2 = (xh * gain + vecs[7:8, :]).astype(BF16)
    dy = cot[...]
    y = h1 + vecs[8:9, :]
    da2 = jnp.zeros((TILE, D), F32)
    for k in range(FF // D):
        cols = slice(D * k, D * k + D)
        u = mm(a2, w1[:, cols]) + b1[:, cols]
        u2 = u * u
        th = jnp.tanh(u * (C0 + (C0 * C1) * u2))
        half = 0.5 * (1.0 + th)
        g = (u * half).astype(BF16)
        slope = half + 0.5 * u * (1.0 - th * th) * (C0 + (3.0 * C0 * C1) * u2)
        y = y + mm(g, w2[cols, :])
        du = (mm_bt(dy, w2[cols, :]) * slope).astype(BF16)
        aw2[cols, :] += mm_at(g, dy)
        aw1[:, cols] += mm_at(a2, du)
        ab1[:, cols] += jnp.sum(du.astype(F32), axis=0, keepdims=True)
        da2 = da2 + mm_bt(du, w1[:, cols])
    out[...] = y.astype(BF16)
    dyf = dy.astype(F32)
    e = da2 * gain
    dh1 = dyf + inverse * (e - jnp.mean(e, axis=-1, keepdims=True) - xh * jnp.mean(e * xh, axis=-1, keepdims=True))
    dh1_out[...] = dh1
    db = dh1.astype(BF16)
    awo[...] += mm_at(mixed, db)
    da_out[...] = mm_bt(db, wo[...]).astype(BF16)
    avec[5:6, :] += jnp.sum(db.astype(F32), axis=0, keepdims=True)
    avec[6:7, :] += jnp.sum(da2 * xh, axis=0, keepdims=True)
    avec[7:8, :] += jnp.sum(da2, axis=0, keepdims=True)
    avec[8:9, :] += jnp.sum(dyf, axis=0, keepdims=True)

    @pl.when(j == TOK // TILE - 1)
    def _():
        gwo[...] = awo[...].astype(BF16)
        gw1[...] = aw1[...].astype(BF16)
        gw2[...] = aw2[...].astype(BF16)
        gvec[...] = avec[...]
        gb1[...] = ab1[...]


def whole(shape):
    return pl.BlockSpec(shape, lambda j: (0,) * len(shape), pipeline_mode=pl.Buffered(1))


def middle(tok, ao, cot, wo, w1, w2, vecs, b1):
    tile = pl.BlockSpec((TILE, D), lambda j: (j, 0))
    S = jax.ShapeDtypeStruct
    return pl.pallas_call(
        middle_kernel,
        grid=(TOK // TILE,),
        out_shape=[S((TOK, D), BF16), S((TOK, D), F32), S((TOK, D), BF16), S((D, D), BF16), S((D, FF), BF16), S((FF, D), BF16),
                   S((16, D), F32), S((1, FF), F32)],
        in_specs=[tile, tile, tile, whole((D, D)), whole((D, FF)), whole((FF, D)), whole((16, D)), whole((1, FF))],
        out_specs=[tile, tile, tile, whole((D, D)), whole((D, FF)), whole((FF, D)), whole((16, D)), whole((1, FF))],
        scratch_shapes=[VMEM((D, D), F32), VMEM((D, FF), F32), VMEM((FF, D), F32), VMEM((16, D), F32), VMEM((1, FF), F32)],
        compiler_params=pltpu.CompilerParams(dimension_semantics=("arbitrary",), vmem_limit_bytes=60 << 20),
        name="middle",
    )(tok, ao, cot, wo, w1, w2, vecs, b1)


def post_kernel(tok, a1, dq, ext, halo, wide, dh1, weight, vecs, out, gw, gvec, spt, kv, kvc, aw, avec):
    j = pl.program_id(0)

    @pl.when(j == 0)
    def _():
        fill_spread(spt)
        aw[...] = jnp.zeros_like(aw)
        avec[...] = jnp.zeros_like(avec)
        for half in range(2):
            lanes = slice(D * half, D * half + D)
            for l, size in enumerate(LEVEL_SIZE):
                at = EXT_AT[l] + 16
                dst, to = (kv, 0) if l == 0 else (kvc, COARSE_AT[l])
                shrink = 0.5 ** l if half == 0 else 1.0
                first, last = halo[0, l, half].astype(F32), halo[1, l, half].astype(F32)
                if size == 16:
                    v = ext[half, at:at + 16, :].astype(F32) + first + last
                    dst[to:to + 16, lanes] = (v * shrink).astype(BF16)
                    continue
                dst[to:to + 16, lanes] = ((ext[half, at:at + 16, :].astype(F32) + first) * shrink).astype(BF16)
                end = to + size - 16
                dst[end:end + 16, lanes] = ((ext[half, at + size - 16:at + size, :].astype(F32) + last) * shrink).astype(BF16)
                if size > 32:
                    dst[to + 16:end, lanes] = ext[half, at + 16:at + size - 16, :] * jnp.array(shrink, BF16)
            v = wide[0, half].astype(F32)
            for e in range(1, 8):
                v = v + wide[e, half].astype(F32)
            if half == 0:
                v = v * jnp.where(iota((16, D), 0) < 8, 0.5 ** 7, 0.5 ** 8)
            kvc[1008:1024, lanes] = v.astype(BF16)

    rows = pl.ds(pl.multiple_of(j * TILE, TILE), TILE)
    s = spt[rows, :]
    x1 = kvc[pl.ds(pl.multiple_of(j * 128, 128), 128), :]
    x2 = kvc[pl.ds(pl.multiple_of(512 + 128 * (j // 2), 128), 128), :]
    x3 = kvc[768:1024, :]
    dkv = (kv[rows, :].astype(F32) + mm(s[:, 0:128], x1) + mm(s[:, 128:256], x2) + mm(s[:, 256:512], x3)).astype(BF16)
    parts = (dq[...], dkv[:, 0:D], dkv[:, D:2 * D])
    a = a1[...]
    da1 = jnp.zeros((TILE, D), F32)
    for c in range(3):
        aw[c] += mm_at(a, parts[c])
        avec[2 + c:3 + c, :] += jnp.sum(parts[c].astype(F32), axis=0, keepdims=True)
        da1 = da1 + mm_bt(parts[c], weight[c])
    v = tok[...].astype(F32)
    center = v - jnp.mean(v, axis=-1, keepdims=True)
    inverse = lax.rsqrt(jnp.mean(center * center, axis=-1, keepdims=True) + EPS)
    xh = center * inverse
    e = da1 * vecs[0:1, :]
    dv = inverse * (e - jnp.mean(e, axis=-1, keepdims=True) - xh * jnp.mean(e * xh, axis=-1, keepdims=True))
    out[...] = (dh1[...] + dv).astype(BF16)
    avec[0:1, :] += jnp.sum(da1 * xh, axis=0, keepdims=True)
    avec[1:2, :] += jnp.sum(da1, axis=0, keepdims=True)

    @pl.when(j == TOK // TILE - 1)
    def _():
        gw[...] = aw[...].astype(BF16)
        gvec[...] = avec[...]


def after_attention(tok, a1, dq, ext, halo, wide, dh1, weight, vecs):
    tile = pl.BlockSpec((TILE, D), lambda j: (j, 0))
    S = jax.ShapeDtypeStruct
    return pl.pallas_call(
        post_kernel,
        grid=(TOK // TILE,),
        out_shape=[S((TOK, D), BF16), S((3, D, D), BF16), S((8, D), F32)],
        in_specs=[tile, tile, tile, whole((2, EXT, D)), whole((2, 7, 2, 16, D)), whole((8, 2, 16, D)), tile, whole((3, D, D)), whole((16, D))],
        out_specs=[tile, whole((3, D, D)), whole((8, D))],
        scratch_shapes=[VMEM((TOK, 512), BF16), VMEM((TOK, 2 * D), BF16), VMEM((TOK, 2 * D), BF16), VMEM((3, D, D), F32), VMEM((8, D), F32)],
        compiler_params=pltpu.CompilerParams(dimension_semantics=("arbitrary",), vmem_limit_bytes=60 << 20),
        name="after_attention",
    )(tok, a1, dq, ext, halo, wide, dh1, weight, vecs)


def where_am_i():
    h = lax.axis_index("head")
    s = lax.axis_index("span")
    return h, s, s // 4, (s // 2) % 2, s % 2


def peers_of(h, s, y, x, c):
    zs = [lax.rem(h + d, 4) for d in (1, 2, 3)]
    px = {"span": y * 4 + (1 - x) * 2 + c}
    py = {"span": (1 - y) * 4 + x * 2 + c}
    pc = {"span": y * 4 + x * 2 + 1 - c}
    return zs, px, py, pc


def gather_steps(ins, outs, orders, lsem, ssem, rsem):
    h, s, y, x, c = where_am_i()
    zs, px, py, pc = peers_of(h, s, y, x, c)
    n = len(ins)

    def own(i):
        return pltpu.make_async_copy(ins[i], outs[i].at[h, y, x, c], lsem.at[i])

    def along_z(i, k):
        return rcopy(ins[i], outs[i].at[h, y, x, c], ssem.at[i, k], rsem.at[i, k], {"head": zs[k]})

    def second(i):
        src = outs[i].at[:, y, x, c]
        return rcopy(src, src, ssem.at[i, 3], rsem.at[i, 3], py if orders[i] else px)

    def third(i):
        src = outs[i].at[:, :, x, c] if orders[i] else outs[i].at[:, y, :, c]
        return rcopy(src, src, ssem.at[i, 4], rsem.at[i, 4], px if orders[i] else py)

    def fourth(i):
        src = outs[i].at[:, :, :, c]
        return rcopy(src, src, ssem.at[i, 5], rsem.at[i, 5], pc)

    def step0():
        for i in range(n):
            own(i).start()
            for k in range(3):
                along_z(i, k).start()

    def step1():
        for i in range(n):
            own(i).wait()
            for k in range(3):
                along_z(i, k).wait()
            second(i).start()

    def step2():
        for i in range(n):
            second(i).wait()
            third(i).start()

    def step3():
        for i in range(n):
            third(i).wait()
            fourth(i).start()

    def step4():
        for i in range(n):
            fourth(i).wait()
    return step0, step1, step2, step3, step4


def greet_all():
    h, s, y, x, c = where_am_i()
    zs, px, py, pc = peers_of(h, s, y, x, c)
    greet([{"head": z} for z in zs] + [px, py, pc])


def gather_kernel(n, orders, *refs):
    greet_all()
    for step in gather_steps(refs[:n], refs[n:2 * n], orders, *refs[2 * n:]):
        step()


def gather_all(shards, orders, cid=0, space=pl.ANY):
    n = len(shards)
    return pl.pallas_call(
        functools.partial(gather_kernel, n, orders),
        out_shape=[jax.ShapeDtypeStruct((4, 2, 2, 2) + a.shape, a.dtype) for a in shards],
        in_specs=[pl.BlockSpec(memory_space=pl.ANY)] * n,
        out_specs=[pl.BlockSpec(memory_space=space)] * n,
        scratch_shapes=[pltpu.SemaphoreType.DMA((n,)), pltpu.SemaphoreType.DMA((n, 6)), pltpu.SemaphoreType.DMA((n, 6))],
        compiler_params=pltpu.CompilerParams(collective_id=cid, has_side_effects=True),
        name="gather_params",
    )(*shards)


def scatter_kernel(n, orders, *refs):
    ins, outs = refs[:n], refs[n:2 * n]
    a = 2 * n
    r1, r2, r3, r4 = (refs[a + k * n:a + (k + 1) * n] for k in range(4))
    ssem, rsem = refs[a + 4 * n:]
    h, s, y, x, c = where_am_i()
    zs, px, py, pc = peers_of(h, s, y, x, c)
    greet([{"head": z} for z in zs] + [px, py, pc])
    cs = []
    for i in range(n):
        cp = rcopy(ins[i].at[:, :, :, 1 - c], r1[i], ssem.at[i, 0], rsem.at[i, 0], pc)
        cp.start()
        cs.append(cp)
    s2 = []
    for i in range(n):
        cs[i].wait()

        @pl.loop(0, 4)
        def _(hh):
            for yy in range(2):
                for xx in range(2):
                    r1[i][hh, yy, xx] = (r1[i][hh, yy, xx].astype(F32) + ins[i][hh, yy, xx, c].astype(F32)).astype(r1[i].dtype)
        if orders[i] == 0:
            src, dev = r1[i].at[:, :, 1 - x], px
        else:
            src, dev = r1[i].at[:, 1 - y], py
        cp = rcopy(src, r2[i], ssem.at[i, 1], rsem.at[i, 1], dev)
        cp.start()
        s2.append(cp)
    s3 = []
    for i in range(n):
        s2[i].wait()

        @pl.loop(0, 4)
        def _(hh):
            for v in range(2):
                mine = r1[i][hh, v, x] if orders[i] == 0 else r1[i][hh, y, v]
                r2[i][hh, v] = (r2[i][hh, v].astype(F32) + mine.astype(F32)).astype(r2[i].dtype)
        if orders[i] == 0:
            src, dev = r2[i].at[:, 1 - y], py
        else:
            src, dev = r2[i].at[:, 1 - x], px
        cp = rcopy(src, r3[i], ssem.at[i, 2], rsem.at[i, 2], dev)
        cp.start()
        s3.append(cp)
    s4 = []
    for i in range(n):
        s3[i].wait()
        me = y if orders[i] == 0 else x

        @pl.loop(0, 4)
        def _(hh):
            r3[i][hh] = (r3[i][hh].astype(F32) + r2[i][hh, me].astype(F32)).astype(r3[i].dtype)
        zz = []
        for k, z in enumerate(zs):
            cp = rcopy(r3[i].at[z], r4[i].at[k], ssem.at[i, 3 + k], rsem.at[i, 3 + k], {"head": z})
            cp.start()
            zz.append(cp)
        s4.append(zz)
    for i in range(n):
        for cp in s4[i]:
            cp.wait()
        acc = r3[i][h].astype(F32)
        for k in range(3):
            acc = acc + r4[i][k].astype(F32)
        outs[i][...] = acc


def scatter_all(grads, orders, cid=1):
    n = len(grads)
    sh = [g.shape[4:] for g in grads]
    V = pltpu.VMEM
    return pl.pallas_call(
        functools.partial(scatter_kernel, n, orders),
        out_shape=[jax.ShapeDtypeStruct(s, F32) for s in sh],
        in_specs=[pl.BlockSpec(memory_space=pltpu.VMEM)] * n,
        out_specs=[pl.BlockSpec(memory_space=pltpu.VMEM)] * n,
        scratch_shapes=[V((4, 2, 2) + s, g.dtype) for s, g in zip(sh, grads)]
        + [V((4, 2) + s, g.dtype) for s, g in zip(sh, grads)]
        + [V((4,) + s, g.dtype) for s, g in zip(sh, grads)]
        + [V((3,) + s, g.dtype) for s, g in zip(sh, grads)]
        + [pltpu.SemaphoreType.DMA((n, 6)), pltpu.SemaphoreType.DMA((n, 6))],
        compiler_params=pltpu.CompilerParams(collective_id=cid, has_side_effects=True, vmem_limit_bytes=60 << 20),
        name="scatter_grads",
    )(*grads)


BOTH = ("head", "span")


def pack_vectors(first_gain, first_shift, project_bias, output_bias, second_gain, second_shift, reduce_bias, expand_bias):
    a = jnp.stack([first_gain, first_shift, project_bias[0], project_bias[1], project_bias[2], output_bias, second_gain, second_shift])
    b = jnp.pad(reduce_bias[None, :], ((0, 7), (0, 0)))
    return jnp.concatenate([a, b, expand_bias.reshape(8, 8), jnp.zeros((8, 88), F32)], axis=1)


def unpack_vectors(g):
    vecs = g[:, :, 0:32].reshape(32, 8, 2, 16).transpose(2, 1, 0, 3).reshape(16, D)
    return vecs, g[:, :, 32:40].reshape(1, FF)


def pack_gradients(vec, b1):
    a = vec[0:8].reshape(8, 32, 16).transpose(1, 0, 2)
    b = jnp.pad(vec[8].reshape(32, 1, 16), ((0, 0), (0, 7), (0, 0)))
    return jnp.concatenate([a, b, b1.reshape(32, 8, 8), jnp.zeros((32, 8, 88), F32)], axis=2)


def shards(tokens, segment_ids, first_gain, first_shift, project_weight, project_bias, output_weight, output_bias,
           second_gain, second_shift, expand_weight, expand_bias, reduce_weight, reduce_bias, cotangent):
    tok, cot = tokens[0], cotangent[0]
    near = lax.axis_size("head") == 4 and lax.axis_size("span") == 8
    if near:
        packed = pack_vectors(first_gain, first_shift, project_bias, output_bias, second_gain, second_shift, reduce_bias, expand_bias)
        wq, vec = gather_all([project_weight.reshape(48, D), packed], (1, 0))
        parts = [output_weight, expand_weight, reduce_weight]
        wq = wq.reshape(32, 3, 16, D).transpose(1, 0, 2, 3).reshape(3, D, D)
        vecs, b1 = unpack_vectors(vec.reshape(32, 8, 128))
    else:
        def full(v, axis=0):
            return lax.all_gather(v, BOTH, axis=axis, tiled=True)
        wq, wo, w1, w2 = full(project_weight, 1), full(output_weight), full(expand_weight), full(reduce_weight)
        rows = [full(first_gain), full(first_shift), *full(project_bias, 1), full(output_bias), full(second_gain), full(second_shift), full(reduce_bias)]
        vecs = jnp.pad(jnp.stack(rows), ((0, 7), (0, 0)))
        b1 = full(expand_bias)[None]
        parts = []
    a1, fine, coarse = before_attention(tok, segment_ids, wq, vecs)
    halo, wide = exchange_edges(fine, coarse)
    ao, iz, *weights = attention(fine, coarse, halo, wide, parts, (0, 0, 1))
    if near:
        wo, w1, w2 = weights[0].reshape(D, D), weights[1].reshape(D, FF), weights[2].reshape(FF, D)
    out, dh1, da, gwo, gw1, gw2, gvec, gb1 = middle(tok, ao, cot, wo, w1, w2, vecs, b1)
    dq, ext = attention_back(fine, coarse, halo, wide, ao, iz, da)
    halo_b, wide_b = return_edges(ext)
    dtok, gwq, gvec_b = after_attention(tok, a1, dq, ext, halo_b, wide_b, dh1, wq, vecs)
    vec = jnp.concatenate([gvec_b[0:5], gvec[5:9]], axis=0)
    if near:
        grid = (4, 2, 2, 2)
        sums = scatter_all([gwq.reshape(3, 32, 16, D).transpose(1, 0, 2, 3).reshape(grid + (48, D)), gwo.reshape(grid + (16, D)),
                            gw1.reshape(grid + (16, FF)), gw2.reshape(grid + (64, D)), pack_gradients(vec, gb1).reshape(grid + (8, 128))], ORDERS)
        gwq, gwo, gw1, gw2, packed = sums
        gwq = gwq.reshape(3, 16, D)
        row = [packed[r, 0:16] for r in range(8)]
        small = (row[0], row[1], packed[2:5, 0:16], row[5], row[6], row[7], packed[:, 32:40].reshape(64), packed[0, 16:32])
    else:
        def part(v, axis=0):
            return lax.psum_scatter(v.astype(F32), BOTH, scatter_dimension=axis, tiled=True)
        gwq, gwo, gw1, gw2 = part(gwq, 1), part(gwo), part(gw1), part(gw2)
        small = (part(vec[0]), part(vec[1]), part(vec[2:5], 1), part(vec[5]), part(vec[6]), part(vec[7]), part(gb1[0]), part(vec[8]))
    return (out[None], dtok[None], small[0], small[1], gwq, small[2], gwo, small[3], small[4], small[5], gw1, small[6], gw2, small[7])


ORDERS = (1, 0, 0, 1, 0)


def solution(mesh):
    token, row, matrix = P("span", "head", None), P(BOTH), P(BOTH, None)
    three, bias = P(None, BOTH, None), P(None, BOTH)
    params = (row, row, three, bias, matrix, row, row, row, matrix, row, matrix, row)
    return jax.shard_map(shards, mesh=mesh, in_specs=(token, P("span", None)) + params + (token,),
                         out_specs=(token, token) + params, check_vma=False)
```

```python
import functools
import jax
import jax.numpy as jnp
from jax import lax
from jax.experimental import pallas as pl
from jax.experimental.pallas import tpu as pltpu
from jax.sharding import PartitionSpec as P

F32, BF16, I32 = jnp.float32, jnp.bfloat16, jnp.int32
MESH = pl.DeviceIdType.MESH
VMEM = pltpu.VMEM
NEG = -1e30
EPS = 1e-5
TOK = 1024
TILE = 256
D = 512
FF = 2048
EXT = 2384
SIZES = (1024, 512, 256, 128, 64, 32, 16)
EXT_AT = (0, 1056, 1600, 1888, 2048, 2144, 2208)
WIDE_AT = 2256
TRANS_B = (((1,), (1,)), ((), ()))
TRANS_A = (((0,), (0,)), ((), ()))


def mm(a, b):
    return jnp.dot(a, b, preferred_element_type=F32)


def mm_bt(a, b):
    return lax.dot_general(a, b, TRANS_B, preferred_element_type=F32)


def mm_at(a, b):
    return lax.dot_general(a, b, TRANS_A, preferred_element_type=F32)


def iota(shape, dim):
    return lax.broadcasted_iota(I32, shape, dim)


def split(v):
    high = v.astype(BF16)
    return high, (v - high.astype(F32)).astype(BF16)


def covers(t, c, block):
    if block == 0:
        return ((t & 255) >> 1) == c
    if block == 1:
        return ((t & 511) >> 2) == c
    if block == 2:
        return (t >> 3) == c
    level, start = mixed_levels(c)
    return (jnp.right_shift(t, level) == c - start) & (c < 124)


def mixed_levels(c):
    a, b, d, e = ((c >= edge).astype(I32) for edge in (64, 96, 112, 120))
    return 4 + a + b + d + e, 64 * a + 32 * b + 16 * d + 8 * e


def ones_where(cond):
    return jnp.where(cond, 1.0, 0.0).astype(BF16)


def identity(n):
    return ones_where(iota((n, n), 0) == iota((n, n), 1))


def fill_spread(spt):
    @pl.loop(0, TOK // TILE)
    def _(j):
        for block in range(4):
            t = iota((TILE, 128), 0) + j * TILE
            c = iota((TILE, 128), 1)
            spt[pl.ds(j * TILE, TILE), 128 * block:128 * block + 128] = ones_where(covers(t, c, block))


def fill_pool(sp):
    @pl.loop(0, TOK // TILE)
    def _(j):
        for block in range(4):
            t = iota((128, TILE), 1) + j * TILE
            c = iota((128, TILE), 0)
            sp[128 * block:128 * block + 128, pl.ds(pl.multiple_of(j * TILE, TILE), TILE)] = ones_where(covers(t, c, block))


TILES = TOK // TILE
LABEL = 2 * D
WIDE = 2 * D + 128
BIAS_MIXED = 15 * 160
BIASES = BIAS_MIXED + 336


def tile_level(i):
    return 0 if i < 8 else 1 if i < 12 else 2 if i < 14 else 3


def tile_at(i):
    return 2048 if i == 15 else 128 * i + 32 * tile_level(i)


def tile_keys(i):
    return 336 if i == 15 else 160


def tile_times(i):
    if i < 15:
        return float(2 ** tile_level(i))
    level, _unused = mixed_levels(iota((1, 128), 1))
    return (1 << level).astype(F32)


INNER = (1, 2, 3, 4, 5, 6, 9, 10)
OUTER = (0, 7, 8, 11, 12, 13, 14, 15)


def labels_of(total, squares, times):
    return jnp.where(times * squares == total * total, total / times, 0.0)


def head_masks(rows):
    lane = iota((rows, 128), 1)
    return ones_where(lane < 64), ones_where(lane >= 64)


def by_head(x, masks):
    return jnp.concatenate([x * masks[0], x * masks[1]], axis=0)


def own_blocks(x):
    return jnp.concatenate([x[0:64, 0:128], x[64:128, 128:256]], axis=0)


def twice(x):
    return jnp.concatenate([x, x], axis=1)


def two_rows(a, b):
    row = iota((16, a.shape[1]), 0)
    return jnp.where(row == 0, a, jnp.where(row == 1, b, 0.0))


def lanes_of(g, base=0):
    return pl.ds(pl.multiple_of(base + g * 128, 128), 128)


def coarse_cols(ref, base, j):
    return jnp.concatenate([ref[:, base + 128 * j:base + 128 * j + 128],
                            ref[:, base + 512 + 128 * (j // 2):base + 640 + 128 * (j // 2)],
                            ref[:, base + 768:base + 1024]], axis=1)


def coarse_blocks():
    return ([(128 * j, 0, 256 * j, 256) for j in range(4)] + [(512 + 128 * j, 1, 512 * j, 512) for j in range(2)]
            + [(768, 2, 0, 1024), (896, 3, 0, 1024)])


def where_am_i():
    h = lax.axis_index("head")
    s = lax.axis_index("span")
    return h, s, s // 4, (s // 2) % 2, s % 2


class Peers:
    def __init__(self, near):
        h, s = lax.axis_index("head"), lax.axis_index("span")
        odd = s % 2
        self.place = odd * 4 + h
        self.odd = odd
        self.h = h
        other = s + 1 - 2 * odd
        self.z_index = [lax.rem(h + d, 4) for d in (1, 2, 3)]
        self.zs = [{"head": z} for z in self.z_index]
        self.core = {"span": other}
        opposite = {"head": 3 - h, "span": other}
        step = 1 - 2 * odd
        self.right = {"head": lax.rem(h + 1, 4), "span": s + step * ((h + 1) // 4)}
        self.left = {"head": lax.rem(h + 3, 4), "span": s + step * (1 - (h + 3) // 4)}
        self.greeted = self.zs + [self.core, opposite]
        if near:
            y, x = s // 4, (s // 2) % 2
            self.y, self.x, self.c = y, x, odd
            self.px = {"span": y * 4 + (1 - x) * 2 + odd}
            self.py = {"span": (1 - y) * 4 + x * 2 + odd}
            self.greeted += [self.px, self.py]


def greet(devices):
    barrier = pltpu.get_barrier_semaphore()
    for d in devices:
        pl.semaphore_signal(barrier, inc=1, device_id=d, device_id_type=MESH)
    pl.semaphore_wait(barrier, len(devices))


def rcopy(src, dst, send, recv, device):
    return pltpu.make_async_remote_copy(src_ref=src, dst_ref=dst, send_sem=send, recv_sem=recv,
                                        device_id=device, device_id_type=MESH)


class Gather:
    def __init__(self, me, shard, full, swap, local, send, recv):
        self.me, self.shard, self.full, self.swap, self.local, self.send, self.recv = me, shard, full, swap, local, send, recv

    def own(self):
        m = self.me
        return pltpu.make_async_copy(self.shard, self.full(m.h, m.y, m.x, m.c), self.local)

    def hop(self, k):
        m, a = self.me, slice(None)
        if k < 3:
            return rcopy(self.shard, self.full(m.h, m.y, m.x, m.c), self.send.at[k], self.recv.at[k], m.zs[k])
        if k == 3:
            ref, dev = self.full(a, m.y, m.x, m.c), m.py if self.swap else m.px
        elif k == 4:
            ref, dev = (self.full(a, a, m.x, m.c), m.px) if self.swap else (self.full(a, m.y, a, m.c), m.py)
        else:
            ref, dev = self.full(a, a, a, m.c), m.core
        return rcopy(ref, ref, self.send.at[k], self.recv.at[k], dev)

    def start(self, stage):
        if stage == 0:
            self.own().start()
            for k in range(3):
                self.hop(k).start()
        else:
            self.hop(2 + stage).start()

    def wait(self, stage):
        if stage == 0:
            self.own().wait()
            for k in range(3):
                self.hop(k).wait()
        else:
            self.hop(2 + stage).wait()


class Scatter:
    def __init__(self, me, grad, mine, swap, bufs, send, recv):
        self.me, self.grad, self.mine, self.swap, self.bufs, self.send, self.recv = me, grad, mine, swap, bufs, send, recv

    def hops(self, stage):
        m, s, r = self.me, self.send, self.recv
        r1, r2, r3, r4 = self.bufs
        if stage == 0:
            return [rcopy(self.grad(1 - m.c), r1, s.at[0], r.at[0], m.core)]
        if stage == 1:
            src, dev = (r1.at[:, 1 - m.y], m.py) if self.swap else (r1.at[:, :, 1 - m.x], m.px)
            return [rcopy(src, r2, s.at[1], r.at[1], dev)]
        if stage == 2:
            src, dev = (r2.at[:, 1 - m.x], m.px) if self.swap else (r2.at[:, 1 - m.y], m.py)
            return [rcopy(src, r3, s.at[2], r.at[2], dev)]
        return [rcopy(r3.at[m.z_index[k]], r4.at[k], s.at[3 + k], r.at[3 + k], m.zs[k]) for k in range(3)]

    def start(self, stage):
        for cp in self.hops(stage):
            cp.start()

    def wait(self, stage):
        for cp in self.hops(stage):
            cp.wait()

    def add(self, stage):
        m = self.me
        r1, r2, r3, r4 = self.bufs

        def into(dst, key, other):
            dst[key] = (dst[key].astype(F32) + other.astype(F32)).astype(dst.dtype)
        if stage == 0:
            @pl.loop(0, 4)
            def _(hh):
                for yy in range(2):
                    for xx in range(2):
                        into(r1, (hh, yy, xx), self.mine(hh, yy, xx))
        elif stage == 1:
            @pl.loop(0, 4)
            def _(hh):
                for v in range(2):
                    into(r2, (hh, v), r1[hh, m.y, v] if self.swap else r1[hh, v, m.x])
        else:
            @pl.loop(0, 4)
            def _(hh):
                into(r3, (hh,), r2[hh, m.x if self.swap else m.y])

    def result(self):
        r1, r2, r3, r4 = self.bufs
        acc = r3[self.me.h].astype(F32)
        for k in range(3):
            acc = acc + r4[k].astype(F32)
        return acc


def scatter_bufs(shape, dtype):
    return [VMEM((4, 2, 2) + shape, dtype), VMEM((4, 2) + shape, dtype), VMEM((4,) + shape, dtype), VMEM((3,) + shape, dtype)]


def split3(v):
    high, rest = split(v)
    mid = rest
    low = (v - high.astype(F32) - mid.astype(F32)).astype(BF16)
    return high, mid, low


def mm_exact(v, ones):
    a, b, c = split3(v)
    return mm(a, ones) + mm(b, ones) + mm(c, ones)


def small_rows(vt, g1, s1, pb, ob, g2, s2, rb, eb):
    vt[...] = jnp.zeros_like(vt)
    for r, ref in enumerate((g1, s1, None, None, None, ob, g2, s2)):
        vt[r:r + 1, 0:16] = pb[r - 2:r - 1, :] if ref is None else ref[...]
    vt[0:1, 16:32] = rb[...]
    for r in range(8):
        vt[r:r + 1, 32:40] = eb[0:1, 8 * r:8 * r + 8]


def unpack_small(gathered, vecs, b1):
    v = gathered[...].reshape(256, 128)
    row, n = iota((256, D), 0), iota((256, D), 1)
    lane, col = iota((128, D), 0), iota((128, D), 1)
    mine = (row >> 3) == (n >> 4)
    for half in range(2):
        x = mm_exact(v, ones_where(lane == (col & 15) + 16 * half))
        vecs[8 * half:8 * half + 8, :] = jnp.sum(jnp.where(mine, x, 0.0).reshape(32, 8, D), axis=0)
    x = mm_exact(v, ones_where(lane == (col & 7) + 32))
    for q in range(4):
        ok = ((row >> 3) == ((n + 512 * q) >> 6)) & ((row & 7) == ((n >> 3) & 7))
        b1[0:1, D * q:D * q + D] = jnp.sum(jnp.where(ok, x, 0.0), axis=0, keepdims=True)


def fill_bias(bias, kvx, labq, place, tiles):
    def matching(i):
        kl = kvx[tile_at(i):tile_at(i) + tile_keys(i), LABEL:WIDE].astype(F32)
        return (kl == labq[i:i + 1, :]) & (kl != 0.0)

    r, c = iota((160, 128), 0), iota((160, 128), 1)
    near = jnp.abs((r >> 4) - 1 - (c >> 4)) <= 1
    far = near & (jnp.abs((r >> 3) - 2 - (c >> 3)) >= 2)
    same = (r - 16) == c
    for i in tiles:
        if i == 15:
            continue
        ok = matching(i) & near | same if i < 8 else matching(i) & far
        bias[160 * i:160 * i + 160, :] = jnp.where(ok, 0.0, NEG)
    if 15 not in tiles:
        return
    r, c = iota((336, 128), 0), iota((336, 128), 1)
    inner = (r >= 96).astype(I32) + (r >= 160).astype(I32)
    start = jnp.where(inner == 0, 0, jnp.where(inner == 1, 96, 160))
    e, k = (r - 208) >> 4, (r - 208) & 15
    upper = (k >= 8).astype(I32)
    level_k = jnp.where(r < 208, 4 + inner, 7 + upper)
    pos_k = jnp.where(r < 208, r - start - 16, jnp.where(k < 8, e * 8 + k, e * 4 + k - 8))
    level_q, start_q = mixed_levels(c)
    pos_q = c - start_q + jnp.where(level_q == 7, place * 8, jnp.where(level_q == 8, place * 4, 0))
    shape = (level_k == level_q) & (jnp.abs((pos_k >> 4) - (pos_q >> 4)) <= 1) & (jnp.abs((pos_k >> 3) - (pos_q >> 3)) >= 2)
    bias[BIAS_MIXED:BIASES, :] = jnp.where(matching(15) & shape, 0.0, NEG)


def bias_of(bias, i):
    return twice(bias[160 * i:160 * i + 160, :] if i < 15 else bias[BIAS_MIXED:BIASES, :])


def forward_kernel(near, *refs):
    refs = list(refs)

    def take(n):
        out = refs[:n]
        del refs[:n]
        return out
    tok, seg = take(2)
    if near:
        wq_in, = take(1)
        small = take(8)
        ffn_in = take(3)
    else:
        wq, vecs = take(2)
    kvx_o, qx_o, bias_o, a1_o, ao_o, iz_o, sp_o, spt_o = take(8)
    if near:
        wq_o, vecs_o, b1_o = take(3)
        ffn_o = take(3)
    kvx, qx, bias, a1, ao, iz, sp, spt, xh, labq, n0, nc, z0, out_sem, e_send, e_recv = take(16)
    if near:
        wq, vecs, b1, vt, vg, local, send, recv = take(8)
    me = Peers(near)
    place = me.place
    outs = []

    def emit(src, dst):
        cp = pltpu.make_async_copy(src, dst, out_sem.at[len(outs)])
        cp.start()
        outs.append(cp)

    for l, size in enumerate(SIZES):
        kvx[EXT_AT[l]:EXT_AT[l] + 16, :] = jnp.zeros((16, WIDE), BF16)
        kvx[EXT_AT[l] + 16 + size:EXT_AT[l] + 32 + size, :] = jnp.zeros((16, WIDE), BF16)
    if near:
        small_rows(vt, *small)
    greet(me.greeted)
    if near:
        lane = (pl.ds(0, 256), pl.ds(256, 256))
        first = [Gather(me, vt, lambda h, y, x, c: vg.at[h, y, x, c], False, local.at[0], send.at[0], recv.at[0])]
        for k in range(2):
            first.append(Gather(me, wq_in.at[:, :, lane[k]], lambda h, y, x, c, k=k: wq.at[:, h, y, x, c, :, lane[k]], k == 1,
                                local.at[1 + k], send.at[1 + k], recv.at[1 + k]))
        later = [Gather(me, ffn_in[k], lambda h, y, x, c, k=k: ffn_o[k].at[h, y, x, c], k == 2,
                        local.at[3 + k], send.at[3 + k], recv.at[3 + k]) for k in range(3)]

    def advance(group, stage):
        if near:
            for a in (first if group == 0 else later):
                if stage >= 0:
                    a.wait(stage)
                if stage < 3:
                    a.start(stage + 1)

    advance(0, -1)
    fill_pool(sp)
    fill_spread(spt)
    emit(sp, sp_o)
    emit(spt, spt_o)
    advance(0, 0)
    advance(1, -1)
    ids = seg[:, pl.ds(pl.multiple_of(me.h * TOK, TOK), TOK)].astype(F32)
    ids_b = jnp.broadcast_to(ids, (128, TOK)).astype(BF16)
    sq_b = jnp.broadcast_to(ids * ids, (128, TOK)).astype(BF16)
    eye = identity(TILE)
    for j in range(TILES):
        kvx[16 + TILE * j:16 + TILE * j + TILE, LABEL:WIDE] = mm_bt(eye, ids_b[:, TILE * j:TILE * j + TILE]).astype(BF16)
    for i in range(8):
        labq[i:i + 1, :] = ids[:, 128 * i:128 * i + 128]
    wide_at = pl.multiple_of(WIDE_AT + 16 * place, 16)

    def put_coarse(b, value, cols):
        at, block, _t, _n = coarse_blocks()[b]
        if block < 3:
            level = block + 1
            row = EXT_AT[level] + 16 + at - (0, 512, 768)[block]
            kvx[row:row + 128, cols] = value
        else:
            for level, a, n in ((4, 0, 64), (5, 64, 32), (6, 96, 16)):
                kvx[EXT_AT[level] + 16:EXT_AT[level] + 16 + n, cols] = value[a:a + n]
            kvx[pl.ds(wide_at, 16), cols] = value[112:128]

    for b, (at, block, t, n) in enumerate(coarse_blocks()):
        s = sp[128 * block:128 * block + 128, t:t + n]
        rows_level, _unused = mixed_levels(iota((128, 128), 0))
        cols_level, _unused = mixed_levels(iota((8, 128), 1))
        times_r = (1 << rows_level).astype(F32) if block == 3 else float(2 ** (block + 1))
        times_c = (1 << cols_level).astype(F32) if block == 3 else float(2 ** (block + 1))
        lab = labels_of(mm_bt(s, ids_b[:, t:t + n]), mm_bt(s, sq_b[:, t:t + n]), times_r)
        put_coarse(b, lab.astype(BF16), slice(LABEL, WIDE))
        row = labels_of(mm_bt(ids_b[0:8, t:t + n], s), mm_bt(sq_b[0:8, t:t + n], s), times_c)
        labq[8 + b:9 + b, :] = row[0:1, :]
    fill_bias(bias, kvx, labq, place, INNER)
    advance(0, 1)
    for j in range(TILES):
        v = tok[TILE * j:TILE * j + TILE, :].astype(F32)
        center = v - jnp.mean(v, axis=-1, keepdims=True)
        xh[TILE * j:TILE * j + TILE, :] = center * lax.rsqrt(jnp.mean(center * center, axis=-1, keepdims=True) + EPS)
    advance(0, 2)
    advance(1, 0)
    if near:
        first[0].wait(3)
        unpack_small(vg, vecs, b1)
        emit(vecs, vecs_o)
        emit(b1, b1_o)
    for j in range(TILES):
        rows = slice(TILE * j, TILE * j + TILE)
        a1[rows, :] = (xh[rows, :] * vecs[0:1, :] + vecs[1:2, :]).astype(BF16)
    emit(a1, a1_o)
    if near:
        first[1].wait(3)
        first[2].wait(3)
        emit(wq, wq_o)
    for c in range(3):
        w = wq[c].reshape(D, D)
        for j in range(TILES):
            r = (mm(a1[TILE * j:TILE * j + TILE, :], w) + vecs[2 + c:3 + c, :]).astype(BF16)
            if c == 0:
                qx[TILE * j:TILE * j + TILE, :] = r * jnp.array(0.125, BF16)
            else:
                kvx[16 + TILE * j:16 + TILE * j + TILE, D * (c - 1):D * c] = r
    for b, (at, block, t, n) in enumerate(coarse_blocks()):
        s = sp[128 * block:128 * block + 128, t:t + n]
        if block == 3:
            level, _unused = mixed_levels(iota((128, D), 0))
            shrink = 1.0 / (1 << level).astype(F32)
        else:
            shrink = 0.5 ** (block + 1)
        qx[1024 + at:1024 + at + 128, :] = (mm(s, qx[t:t + n, :]) * shrink).astype(BF16)
        put_coarse(b, (mm(s, kvx[16 + t:16 + t + n, 0:D]) * shrink).astype(BF16), slice(0, D))
        put_coarse(b, mm(s, kvx[16 + t:16 + t + n, D:2 * D]).astype(BF16), slice(D, 2 * D))
    to_right, to_left = [], []
    for l, size in enumerate(SIZES):
        at = EXT_AT[l]
        to_right.append(rcopy(kvx.at[pl.ds(at + size, 16)], kvx.at[pl.ds(at, 16)], e_send.at[l], e_recv.at[l], me.right))
        to_left.append(rcopy(kvx.at[pl.ds(at + 16, 16)], kvx.at[pl.ds(at + 16 + size, 16)], e_send.at[7 + l], e_recv.at[7 + l], me.left))
    own_wide = kvx.at[pl.ds(wide_at, 16)]
    wide_z = [rcopy(own_wide, own_wide, e_send.at[14 + k], e_recv.at[14 + k], me.zs[k]) for k in range(3)]
    four = kvx.at[pl.ds(pl.multiple_of(WIDE_AT + 64 * me.odd, 16), 64)]
    wide_core = rcopy(four, four, e_send.at[17], e_recv.at[17], me.core)
    not_last, not_first = place < 7, place > 0

    @pl.when(not_last)
    def _():
        for cp in to_right:
            cp.start()

    @pl.when(not_first)
    def _():
        for cp in to_left:
            cp.start()
    for cp in wide_z:
        cp.start()
    emit(qx, qx_o)
    masks = head_masks(128)

    def tile(g, i):
        keys = slice(tile_at(i), tile_at(i) + tile_keys(i))
        kw, vw = kvx[keys, lanes_of(g)], kvx[keys, lanes_of(g, D)]
        q = by_head(qx[128 * i:128 * i + 128, lanes_of(g)], masks)
        e = jnp.exp(mm_bt(kw, q) + bias_of(bias, i))
        times = tile_times(i)
        z = jnp.sum(e, axis=0, keepdims=True)
        z0_, z1_ = z[:, 0:128] * times, z[:, 128:256] * times
        n = own_blocks(mm_at(vw, e.astype(BF16)))
        if i < 8:
            cols = slice(128 * i, 128 * i + 128)
            n0[g, :, cols] = n
            z0[g, 0:1, cols] = z0_
            z0[g, 1:2, cols] = z1_
        else:
            cols = slice(128 * i - 1024, 128 * i - 896)
            high, low = split(two_rows(z0_, z1_))
            nc[g, :, cols] = jnp.concatenate([n.astype(BF16), high, low], axis=0)

    def run(tiles, lo, hi):
        @pl.loop(lo, hi)
        def _(g):
            for i in tiles:
                tile(g, i)
    run(INNER, 0, 1)
    advance(1, 1)
    for cp in wide_z:
        cp.wait()
    wide_core.start()
    run(INNER, 1, 4)
    advance(1, 2)

    @pl.when(not_last)
    def _():
        for cp in to_right:
            cp.wait_send()
        for cp in to_left:
            cp.wait_recv()

    @pl.when(not_first)
    def _():
        for cp in to_left:
            cp.wait_send()
        for cp in to_right:
            cp.wait_recv()
    wide_core.wait()
    emit(kvx, kvx_o)
    fill_bias(bias, kvx, labq, place, OUTER)
    emit(bias, bias_o)

    @pl.loop(0, 4)
    def _(g):
        for i in OUTER:
            tile(g, i)
        c_ref = nc.at[g]
        for j in range(TILES):
            cols = slice(TILE * j, TILE * j + TILE)
            r = mm(coarse_cols(c_ref, 0, j), sp[:, cols])
            n = n0[g, :, cols] + r[0:128]
            i0 = 1.0 / (z0[g, 0:1, cols] + r[128:129] + r[144:145])
            i1 = 1.0 / (z0[g, 1:2, cols] + r[129:130] + r[145:146])
            iz[g, 0:1, cols] = i0
            iz[g, 1:2, cols] = i1
            ao[pl.ds(pl.multiple_of(g * 128, 128), 64), cols] = (n[0:64] * i0).astype(BF16)
            ao[pl.ds(pl.multiple_of(g * 128 + 64, 64), 64), cols] = (n[64:128] * i1).astype(BF16)
    emit(ao, ao_o)
    emit(iz, iz_o)
    if near:
        for a in later:
            a.wait(3)
    for cp in outs:
        cp.wait()


ANY = pl.BlockSpec(memory_space=pl.ANY)
IN_VMEM = pl.BlockSpec(memory_space=pltpu.VMEM)
S = jax.ShapeDtypeStruct
SEM = pltpu.SemaphoreType.DMA


def forward(near, tok, seg, *params):
    grid = (4, 2, 2, 2)
    shapes = [S((EXT, WIDE), BF16), S((2048, D), BF16), S((BIASES, 128), F32), S((TOK, D), BF16), S((D, TOK), BF16),
              S((4, 2, TOK), F32), S((512, TOK), BF16), S((TOK, 512), BF16)]
    scratch = [VMEM(s.shape, s.dtype) for s in shapes] + [
        VMEM((TOK, D), F32), VMEM((16, 128), F32), VMEM((4, 128, TOK), F32), VMEM((4, 160, TOK), BF16), VMEM((4, 2, TOK), F32),
        SEM((16,)), SEM((18,)), SEM((18,))]
    if near:
        shapes += [S((3,) + grid + (16, D), BF16), S((16, D), F32), S((1, FF), F32)]
        shapes += [S(grid + a.shape, a.dtype) for a in params[9:]]
        scratch += [VMEM((3,) + grid + (16, D), BF16), VMEM((16, D), F32), VMEM((1, FF), F32), VMEM((8, 128), F32),
                    VMEM(grid + (8, 128), F32), SEM((6,)), SEM((6, 6)), SEM((6, 6))]
        specs = [IN_VMEM] * 9 + [ANY] * 3
    else:
        specs = [IN_VMEM] * 2
    return pl.pallas_call(
        functools.partial(forward_kernel, near),
        out_shape=shapes,
        in_specs=[IN_VMEM, IN_VMEM] + specs,
        out_specs=[ANY] * len(shapes),
        scratch_shapes=scratch,
        compiler_params=pltpu.CompilerParams(collective_id=0, has_side_effects=True, vmem_limit_bytes=60 << 20),
        name="forward",
    )(tok, seg, *params)


C0 = 0.7978845608028654
C1 = 0.044715


def middle_kernel(tok, ao, cot, wo, w1, w2, vecs, b1, out, dh1_out, da_out, gwo, gw1, gw2, gvec, gb1,
                  awo, aw1, aw2, avec, ab1):
    j = pl.program_id(0)

    @pl.when(j == 0)
    def _():
        awo[...] = jnp.zeros_like(awo)
        aw1[...] = jnp.zeros_like(aw1)
        aw2[...] = jnp.zeros_like(aw2)
        avec[...] = jnp.zeros_like(avec)
        ab1[...] = jnp.zeros_like(ab1)
    mixed = ao[...]
    h1 = tok[...].astype(F32) + mm_at(mixed, wo[...]) + vecs[5:6, :]
    center = h1 - jnp.mean(h1, axis=-1, keepdims=True)
    inverse = lax.rsqrt(jnp.mean(center * center, axis=-1, keepdims=True) + EPS)
    xh = center * inverse
    gain = vecs[6:7, :]
    a2 = (xh * gain + vecs[7:8, :]).astype(BF16)
    dy = cot[...]
    y = h1 + vecs[8:9, :]
    da2 = jnp.zeros((TILE, D), F32)
    for k in range(FF // D):
        cols = slice(D * k, D * k + D)
        u = mm(a2, w1[:, cols]) + b1[:, cols]
        u2 = u * u
        th = jnp.tanh(u * (C0 + (C0 * C1) * u2))
        half = 0.5 * (1.0 + th)
        g = (u * half).astype(BF16)
        slope = half + 0.5 * u * (1.0 - th * th) * (C0 + (3.0 * C0 * C1) * u2)
        y = y + mm(g, w2[cols, :])
        du = (mm_bt(dy, w2[cols, :]) * slope).astype(BF16)
        aw2[cols, :] += mm_at(g, dy)
        aw1[:, cols] += mm_at(a2, du)
        ab1[:, cols] += jnp.sum(du.astype(F32), axis=0, keepdims=True)
        da2 = da2 + mm_bt(du, w1[:, cols])
    out[...] = y.astype(BF16)
    dyf = dy.astype(F32)
    e = da2 * gain
    dh1 = dyf + inverse * (e - jnp.mean(e, axis=-1, keepdims=True) - xh * jnp.mean(e * xh, axis=-1, keepdims=True))
    dh1_out[...] = dh1
    db = dh1.astype(BF16)
    awo[...] += mm(mixed, db)
    da_out[...] = mm_bt(wo[...], db).astype(BF16)
    avec[5:6, :] += jnp.sum(db.astype(F32), axis=0, keepdims=True)
    avec[6:7, :] += jnp.sum(da2 * xh, axis=0, keepdims=True)
    avec[7:8, :] += jnp.sum(da2, axis=0, keepdims=True)
    avec[8:9, :] += jnp.sum(dyf, axis=0, keepdims=True)

    @pl.when(j == TOK // TILE - 1)
    def _():
        gwo[...] = awo[...].astype(BF16)
        gw1[...] = aw1[...].astype(BF16)
        gw2[...] = aw2[...].astype(BF16)
        gvec[...] = avec[...]
        gb1[...] = ab1[...]


def whole(shape):
    return pl.BlockSpec(shape, lambda j: (0,) * len(shape), pipeline_mode=pl.Buffered(1))


def middle(tok, ao, cot, wo, w1, w2, vecs, b1):
    tile = pl.BlockSpec((TILE, D), lambda j: (j, 0))
    flat = pl.BlockSpec((D, TILE), lambda j: (0, j))
    return pl.pallas_call(
        middle_kernel,
        grid=(TOK // TILE,),
        out_shape=[S((TOK, D), BF16), S((TOK, D), F32), S((D, TOK), BF16), S((D, D), BF16), S((D, FF), BF16), S((FF, D), BF16),
                   S((16, D), F32), S((1, FF), F32)],
        in_specs=[tile, flat, tile, whole((D, D)), whole((D, FF)), whole((FF, D)), whole((16, D)), whole((1, FF))],
        out_specs=[tile, tile, flat, whole((D, D)), whole((D, FF)), whole((FF, D)), whole((16, D)), whole((1, FF))],
        scratch_shapes=[VMEM((D, D), F32), VMEM((D, FF), F32), VMEM((FF, D), F32), VMEM((16, D), F32), VMEM((1, FF), F32)],
        compiler_params=pltpu.CompilerParams(dimension_semantics=("arbitrary",), vmem_limit_bytes=60 << 20),
        name="middle",
    )(tok, ao, cot, wo, w1, w2, vecs, b1)


def pack_small(rows, b1):
    row, n = iota((256, D), 0), iota((256, D), 1)
    lane, col = iota((128, D), 0), iota((128, D), 1)
    mine = (row >> 3) == (n >> 4)

    def moved(v, ok, ones):
        total = None
        for part in split3(jnp.where(ok, v, 0.0)):
            r = mm_bt(part, ones)
            total = r if total is None else total + r
        return total
    eight = jnp.broadcast_to(rows[0:8][None], (32, 8, D)).reshape(256, D)
    out = moved(eight, mine, ones_where(lane == (col & 15)))
    out = out + moved(jnp.broadcast_to(rows[8:9], (256, D)), mine & ((row & 7) == 0), ones_where(lane == (col & 15) + 16))
    last = ones_where(lane == (col & 7) + 32)
    for q in range(4):
        ok = ((row >> 3) == ((n + 512 * q) >> 6)) & ((row & 7) == ((n >> 3) & 7))
        out = out + moved(jnp.broadcast_to(b1[0:1, D * q:D * q + D], (256, D)), ok, last)
    return out.reshape(4, 2, 2, 2, 8, 128)


def backward_kernel(near, *refs):
    refs = list(refs)

    def take(n):
        out = refs[:n]
        del refs[:n]
        return out
    ins = take(13)
    gffn, (gvec, gb1) = take(3), take(2)
    tok_o, gq_o = take(2)
    small_o = take(8 if near else 1)
    gffn_o = take(3 if near else 0)
    kvx, qx, bias, a1, ao, iz, sp, spt, da, tok, dh1, wq, vecs = take(13)
    gr, rm, dqt, dkv, dq, edge, e_got, w_send, w_got, w_mid, aw, avec, tok_s, in_sem, out_sem, e_send, e_recv = take(17)
    if near:
        gq, gv, f_mine, f_sem, send, recv = take(6)
        bufs = [take(4) for _ in range(6)]
    me = Peers(near)
    place = me.place
    loads = {}
    targets = (da, ao, iz, sp, kvx, qx, bias, spt, a1, tok, dh1, wq, vecs)
    names = ("da", "ao", "iz", "sp", "kvx", "qx", "bias", "spt", "a1", "tok", "dh1", "wq", "vecs")
    for k, name in enumerate(names):
        loads[name] = pltpu.make_async_copy(ins[k], targets[k], in_sem.at[k])
        loads[name].start()
    greet(me.greeted)
    mine_copies = []
    if near:
        lane = (pl.ds(0, 256), pl.ds(256, 256))
        ffn = []
        for k in range(3):
            cp = pltpu.make_async_copy(gffn[k].at[:, :, :, me.c], f_mine[k], f_sem.at[k])
            cp.start()
            mine_copies.append(cp)
            ffn.append(Scatter(me, lambda c, k=k: gffn[k].at[:, :, :, c], lambda h, y, x, k=k: f_mine[k][h, y, x], k == 2,
                               bufs[k], send.at[k], recv.at[k]))
        last = [Scatter(me, lambda c: gv.at[:, :, :, c], lambda h, y, x: gv[h, y, x, me.c], False, bufs[3], send.at[3], recv.at[3])]
        for k in range(2):
            last.append(Scatter(me, lambda c, k=k: gq.at[:, :, :, c, :, :, lane[k]],
                                lambda h, y, x, k=k: gq[h, y, x, me.c, :, :, 256 * k:256 * k + 256], k == 1,
                                bufs[4 + k], send.at[4 + k], recv.at[4 + k]))

    def advance(group, stage):
        for a in group:
            if stage >= 0:
                a.wait(stage)
                a.add(stage)
            a.start(stage + 1)

    if near:
        advance(ffn, -1)
    for name in ("da", "ao", "iz", "sp"):
        loads[name].wait()
    masks = head_masks(128)

    @pl.loop(0, 4)
    def _(g):
        lo, hi = pl.ds(pl.multiple_of(g * 128, 128), 64), pl.ds(pl.multiple_of(g * 128 + 64, 64), 64)
        for j in range(TILES):
            cols = slice(TILE * j, TILE * j + TILE)
            g0 = da[lo, cols].astype(F32) * iz[g, 0:1, cols]
            g1 = da[hi, cols].astype(F32) * iz[g, 1:2, cols]
            r0 = jnp.sum(g0 * ao[lo, cols].astype(F32), axis=0, keepdims=True)
            r1 = jnp.sum(g1 * ao[hi, cols].astype(F32), axis=0, keepdims=True)
            rm[g, 0:1, cols] = r0
            rm[g, 1:2, cols] = r1
            high, low = split(two_rows(r0, r1))
            gr[g, :, cols] = jnp.concatenate([g0.astype(BF16), g1.astype(BF16), high, low], axis=0)
        for b, (at, block, t, n) in enumerate(coarse_blocks()):
            x = mm_bt(gr[g, :, t:t + n], sp[128 * block:128 * block + 128, t:t + n])
            cols = slice(1024 + at, 1152 + at)
            gr[g, 0:128, cols] = x[0:128].astype(BF16)
            times = tile_times(8 + b)
            rm[g, 0:1, cols] = (x[128:129] + x[144:145]) * times
            rm[g, 1:2, cols] = (x[129:130] + x[145:146]) * times
    dkv[...] = jnp.zeros_like(dkv)
    for name in ("kvx", "qx", "bias"):
        loads[name].wait()
    zero = jnp.zeros((64, 128), BF16)

    def tile(g, i):
        keys = slice(tile_at(i), tile_at(i) + tile_keys(i))
        cols = slice(128 * i, 128 * i + 128)
        kw, vw = kvx[keys, lanes_of(g)], kvx[keys, lanes_of(g, D)]
        q = by_head(qx[cols, lanes_of(g)], masks)
        gt = gr[g, 0:128, cols]
        gb = jnp.concatenate([jnp.concatenate([gt[0:64], zero], axis=1), jnp.concatenate([zero, gt[64:128]], axis=1)], axis=0)
        e = jnp.exp(mm_bt(kw, q) + bias_of(bias, i))
        rest = jnp.concatenate([rm[g, 0:1, cols], rm[g, 1:2, cols]], axis=1)
        ds = (e * (mm(vw, gb) - rest)).astype(BF16)
        dkv[keys, lanes_of(g)] += mm(ds, q)
        dkv[keys, lanes_of(g, D)] += mm_bt(e.astype(BF16), gb)
        dqt[g, :, cols] = (own_blocks(mm_at(kw, ds)) * (0.125 / tile_times(i))).astype(BF16)

    def run(tiles, lo, hi):
        @pl.loop(lo, hi)
        def _(g):
            for i in tiles:
                tile(g, i)
    run(OUTER, 0, 4)
    for l, size in enumerate(SIZES):
        edge[0, l] = dkv[EXT_AT[l] + 16 + size:EXT_AT[l] + 32 + size, :].astype(BF16)
        edge[1, l] = dkv[EXT_AT[l]:EXT_AT[l] + 16, :].astype(BF16)
    half_at = pl.multiple_of(WIDE_AT + 64 * (1 - me.odd), 16)
    w_send[...] = dkv[pl.ds(half_at, 64), :].astype(BF16)
    to_right = rcopy(edge.at[0], e_got.at[0], e_send.at[0], e_recv.at[0], me.right)
    to_left = rcopy(edge.at[1], e_got.at[1], e_send.at[1], e_recv.at[1], me.left)
    wide_core = rcopy(w_send, w_mid, e_send.at[2], e_recv.at[2], me.core)
    not_last, not_first = place < 7, place > 0
    wide_core.start()

    @pl.when(not_last)
    def _():
        to_right.start()

    @pl.when(not_first)
    def _():
        to_left.start()
    if near:
        for cp in mine_copies:
            cp.wait()
        advance(ffn, 0)
    run(INNER, 0, 2)
    wide_core.wait()
    own_at = pl.multiple_of(WIDE_AT + 64 * me.odd, 16)
    w_mid[...] = (w_mid[...].astype(F32) + dkv[pl.ds(own_at, 64), :]).astype(BF16)
    wide_z = [rcopy(w_mid.at[pl.ds(pl.multiple_of(16 * me.z_index[k], 16), 16)], w_got.at[k], e_send.at[3 + k], e_recv.at[3 + k], me.zs[k])
              for k in range(3)]
    for cp in wide_z:
        cp.start()
    if near:
        advance(ffn, 1)
    run(INNER, 2, 4)

    @pl.loop(0, 4)
    def _(g):
        d_ref = dqt.at[g]
        eye = identity(TILE)
        for j in range(TILES):
            cols = slice(TILE * j, TILE * j + TILE)
            r = d_ref[:, cols].astype(F32) + mm(coarse_cols(d_ref, 1024, j), sp[:, cols])
            dq[cols, lanes_of(g)] = mm_bt(eye, r.astype(BF16)).astype(BF16)
    for cp in wide_z:
        cp.wait()

    @pl.when(not_last)
    def _():
        to_right.wait_send()
        to_left.wait_recv()
        for l, size in enumerate(SIZES):
            rows = slice(EXT_AT[l] + size, EXT_AT[l] + 16 + size)
            dkv[rows, :] += e_got[1, l].astype(F32)

    @pl.when(not_first)
    def _():
        to_left.wait_send()
        to_right.wait_recv()
        for l, size in enumerate(SIZES):
            rows = slice(EXT_AT[l] + 16, EXT_AT[l] + 32)
            dkv[rows, :] += e_got[0, l].astype(F32)
    v = w_mid[pl.ds(pl.multiple_of(16 * me.h, 16), 16), :].astype(F32)
    for k in range(3):
        v = v + w_got[k].astype(F32)
    wide_row, wide_lane = iota((16, 2 * D), 0), iota((16, 2 * D), 1)
    w_own = (v * jnp.where(wide_lane >= D, 1.0, jnp.where(wide_row < 8, 0.5 ** 7, 0.5 ** 8))).astype(BF16)
    lane_all = iota((1, 2 * D), 1)

    def coarse_rows(at, n, level):
        return (dkv[at:at + n, :] * jnp.where(lane_all < D, 0.5 ** level, 1.0)).astype(BF16)
    for name in ("spt", "a1", "tok", "dh1", "wq", "vecs"):
        loads[name].wait()
    top = jnp.concatenate([coarse_rows(EXT_AT[3] + 16, 128, 3), coarse_rows(EXT_AT[4] + 16, 64, 4), coarse_rows(EXT_AT[5] + 16, 32, 5),
                           coarse_rows(EXT_AT[6] + 16, 16, 6), w_own], axis=0)
    avec[...] = jnp.zeros_like(avec)
    aw[...] = jnp.zeros_like(aw)
    if near:
        avec[5:9, :] = gvec[5:9, :]
        advance(ffn, 2)
    for j in range(TILES):
        rows = slice(TILE * j, TILE * j + TILE)
        x = jnp.concatenate([coarse_rows(EXT_AT[1] + 16 + 128 * j, 128, 1), coarse_rows(EXT_AT[2] + 16 + 128 * (j // 2), 128, 2), top], axis=0)
        d = (dkv[16 + TILE * j:16 + TILE * j + TILE, :] + mm(spt[rows, :], x)).astype(BF16)
        parts = (dq[rows, :], d[:, 0:D], d[:, D:2 * D])
        a = a1[rows, :]
        da1 = jnp.zeros((TILE, D), F32)
        for c in range(3):
            aw[c] += mm_at(a, parts[c])
            avec[2 + c:3 + c, :] += jnp.sum(parts[c].astype(F32), axis=0, keepdims=True)
            da1 = da1 + mm_bt(parts[c], wq[c].reshape(D, D))
        v = tok[rows, :].astype(F32)
        center = v - jnp.mean(v, axis=-1, keepdims=True)
        inverse = lax.rsqrt(jnp.mean(center * center, axis=-1, keepdims=True) + EPS)
        n = center * inverse
        e = da1 * vecs[0:1, :]
        dv = inverse * (e - jnp.mean(e, axis=-1, keepdims=True) - n * jnp.mean(e * n, axis=-1, keepdims=True))
        tok_s[rows, :] = (dh1[rows, :] + dv).astype(BF16)
        avec[0:1, :] += jnp.sum(da1 * n, axis=0, keepdims=True)
        avec[1:2, :] += jnp.sum(da1, axis=0, keepdims=True)
    done = pltpu.make_async_copy(tok_s, tok_o, out_sem.at[0])
    done.start()
    if not near:
        gq_o[...] = aw[...].astype(BF16)
        small_o[0][...] = avec[...]
        done.wait()
        return
    for c in range(3):
        gq[:, :, :, :, c] = aw[c].astype(BF16).reshape(4, 2, 2, 2, 16, D)
    for a in last[1:]:
        a.start(0)
    gv[...] = pack_small(avec[...], gb1)
    last[0].start(0)
    for a in ffn:
        a.wait(3)
    for k in range(3):
        gffn_o[k][...] = ffn[k].result()
    for stage in range(3):
        for a in last:
            a.wait(stage)
            a.add(stage)
            a.start(stage + 1)
    for a in last:
        a.wait(3)
    gq_o[:, :, 0:256] = last[1].result()
    gq_o[:, :, 256:512] = last[2].result()
    t = last[0].result()
    for k, r in enumerate((0, 1, None, 5, 6, 7)):
        if r is None:
            small_o[k][...] = t[2:5, 0:16]
        else:
            small_o[k][...] = t[r:r + 1, 0:16]
    small_o[6][...] = t[:, 32:40]
    small_o[7][...] = t[0:1, 16:32]
    done.wait()


def backward(near, saved, wq, vecs, tok, da, dh1, gffn, gvec, gb1):
    kvx, qx, bias, a1, ao, iz, sp, spt = saved
    grid = (4, 2, 2, 2)
    vm = [VMEM(v.shape, v.dtype) for v in (kvx, qx, bias, a1, ao, iz, sp, spt, da, tok, dh1, wq, vecs)]
    scratch = vm + [VMEM((4, 160, 2048), BF16), VMEM((4, 2, 2048), F32), VMEM((4, 128, 2048), BF16), VMEM((EXT, 2 * D), F32),
                    VMEM((TOK, D), BF16), VMEM((2, 7, 16, 2 * D), BF16), VMEM((2, 7, 16, 2 * D), BF16), VMEM((64, 2 * D), BF16),
                    VMEM((3, 16, 2 * D), BF16), VMEM((64, 2 * D), BF16), VMEM((3, D, D), F32), VMEM((16, D), F32), VMEM((TOK, D), BF16),
                    SEM((13,)), SEM((1,)), SEM((6,)), SEM((6,))]
    if near:
        gffn = [g.reshape(grid + (g.shape[0] // 32, g.shape[1])) for g in gffn]
        shapes = [S((TOK, D), BF16), S((3, 16, D), F32)]
        shapes += [S((1, 16), F32), S((1, 16), F32), S((3, 16), F32), S((1, 16), F32), S((1, 16), F32), S((1, 16), F32), S((8, 8), F32), S((1, 16), F32)]
        shapes += [S(g.shape[4:], F32) for g in gffn]
        pieces = [(g.shape[4:], BF16) for g in gffn] + [((8, 128), F32), ((3, 16, 256), BF16), ((3, 16, 256), BF16)]
        scratch += [VMEM(grid + (3, 16, D), BF16), VMEM(grid + (8, 128), F32), [VMEM((4, 2, 2) + g.shape[4:], BF16) for g in gffn], SEM((3,)),
                    SEM((6, 6)), SEM((6, 6))]
        for shape, kind in pieces:
            scratch += scatter_bufs(shape, kind)
    else:
        gffn = gffn[0:3]
        shapes = [S((TOK, D), BF16), S((3, D, D), BF16), S((16, D), F32)]
    ordered = (da, ao, iz, sp, kvx, qx, bias, spt, a1, tok, dh1, wq, vecs)
    return pl.pallas_call(
        functools.partial(backward_kernel, near),
        out_shape=shapes,
        in_specs=[ANY] * 16 + [IN_VMEM] * 2,
        out_specs=[ANY] + [IN_VMEM] * (len(shapes) - 1),
        scratch_shapes=scratch,
        compiler_params=pltpu.CompilerParams(collective_id=1, has_side_effects=True, vmem_limit_bytes=62 << 20),
        name="backward",
    )(*ordered, *gffn, gvec, gb1)


BOTH = ("head", "span")


def shards(tokens, segment_ids, first_gain, first_shift, project_weight, project_bias, output_weight, output_bias,
           second_gain, second_shift, expand_weight, expand_bias, reduce_weight, reduce_bias, cotangent):
    tok, cot = tokens[0], cotangent[0]
    near = lax.axis_size("head") == 4 and lax.axis_size("span") == 8
    if near:
        vectors = (first_gain, first_shift, project_bias, output_bias, second_gain, second_shift, reduce_bias, expand_bias)
        vectors = [v if v.ndim == 2 else v[None] for v in vectors]
        *saved, wq, vecs, b1, wo, w1, w2 = forward(True, tok, segment_ids, project_weight, *vectors, output_weight, expand_weight, reduce_weight)
        wo, w1, w2 = wo.reshape(D, D), w1.reshape(D, FF), w2.reshape(FF, D)
    else:
        def full(v, axis=0):
            return lax.all_gather(v, BOTH, axis=axis, tiled=True)
        wq, wo, w1, w2 = full(project_weight, 1), full(output_weight), full(expand_weight), full(reduce_weight)
        rows = [full(first_gain), full(first_shift), *full(project_bias, 1), full(output_bias), full(second_gain), full(second_shift), full(reduce_bias)]
        vecs = jnp.pad(jnp.stack(rows), ((0, 7), (0, 0)))
        b1 = full(expand_bias)[None]
        saved = forward(False, tok, segment_ids, wq, vecs)
    ao = saved[4]
    out, dh1, da, *gffn, gvec, gb1 = middle(tok, ao, cot, wo, w1, w2, vecs, b1)
    dtok, gwq, *rest = backward(near, saved, wq, vecs, tok, da, dh1, gffn, gvec, gb1)
    if near:
        small, (gwo, gw1, gw2) = rest[0:8], rest[8:11]
        small = [v if v.shape[0] == 3 else v.reshape(-1) for v in small]
    else:
        def part(v, axis=0):
            return lax.psum_scatter(v.astype(F32), BOTH, scatter_dimension=axis, tiled=True)
        vec = rest[0]
        gwq, gwo, gw1, gw2 = part(gwq, 1), part(gffn[0]), part(gffn[1]), part(gffn[2])
        small = (part(vec[0]), part(vec[1]), part(vec[2:5], 1), part(gvec[5]), part(gvec[6]), part(gvec[7]), part(gb1[0]), part(gvec[8]))
    return (out[None], dtok[None], small[0], small[1], gwq, small[2], gwo, small[3], small[4], small[5], gw1, small[6], gw2, small[7])


def solution(mesh):
    token, row, matrix = P("span", "head", None), P(BOTH), P(BOTH, None)
    three, bias = P(None, BOTH, None), P(None, BOTH)
    params = (row, row, three, bias, matrix, row, row, row, matrix, row, matrix, row)
    return jax.shard_map(shards, mesh=mesh, in_specs=(token, P("span", None)) + params + (token,),
                         out_specs=(token, token) + params, check_vma=False)
```

```python
import functools
import jax
import jax.numpy as jnp
from jax import lax
from jax.experimental import pallas as pl
from jax.experimental.pallas import tpu as pltpu
from jax.sharding import PartitionSpec as P

F32, BF16, I32 = jnp.float32, jnp.bfloat16, jnp.int32
MESH = pl.DeviceIdType.MESH
VMEM = pltpu.VMEM
NEG = -1e30
EPS = 1e-5
TOK = 1024
TILE = 256
D = 512
FF = 2048
EXT = 2384
SIZES = (1024, 512, 256, 128, 64, 32, 16)
EXT_AT = (0, 1056, 1600, 1888, 2048, 2144, 2208)
WIDE_AT = 2256
TRANS_B = (((1,), (1,)), ((), ()))
TRANS_A = (((0,), (0,)), ((), ()))


def mm(a, b):
    return jnp.dot(a, b, preferred_element_type=F32)


def mm_bt(a, b):
    return lax.dot_general(a, b, TRANS_B, preferred_element_type=F32)


def mm_at(a, b):
    return lax.dot_general(a, b, TRANS_A, preferred_element_type=F32)


def iota(shape, dim):
    return lax.broadcasted_iota(I32, shape, dim)


def split(v):
    high = v.astype(BF16)
    return high, (v - high.astype(F32)).astype(BF16)


def covers(t, c, block):
    if block == 0:
        return ((t & 255) >> 1) == c
    if block == 1:
        return ((t & 511) >> 2) == c
    if block == 2:
        return (t >> 3) == c
    level, start = mixed_levels(c)
    return (jnp.right_shift(t, level) == c - start) & (c < 124)


def mixed_levels(c):
    a, b, d, e = ((c >= edge).astype(I32) for edge in (64, 96, 112, 120))
    return 4 + a + b + d + e, 64 * a + 32 * b + 16 * d + 8 * e


def ones_where(cond):
    return jnp.where(cond, 1.0, 0.0).astype(BF16)


def identity(n):
    return ones_where(iota((n, n), 0) == iota((n, n), 1))


def fill_spread(spt):
    @pl.loop(0, TOK // TILE)
    def _(j):
        for block in range(4):
            t = iota((TILE, 128), 0) + j * TILE
            c = iota((TILE, 128), 1)
            spt[pl.ds(j * TILE, TILE), 128 * block:128 * block + 128] = ones_where(covers(t, c, block))


def fill_pool(sp):
    @pl.loop(0, TOK // TILE)
    def _(j):
        for block in range(4):
            t = iota((128, TILE), 1) + j * TILE
            c = iota((128, TILE), 0)
            sp[128 * block:128 * block + 128, pl.ds(pl.multiple_of(j * TILE, TILE), TILE)] = ones_where(covers(t, c, block))


TILES = TOK // TILE
BIAS_MIXED = 15 * 160
BIASES = BIAS_MIXED + 336


def tile_level(i):
    return 0 if i < 8 else 1 if i < 12 else 2 if i < 14 else 3


def tile_at(i):
    return 2048 if i == 15 else 128 * i + 32 * tile_level(i)


def tile_keys(i):
    return 336 if i == 15 else 160


def tile_times(i):
    if i < 15:
        return float(2 ** tile_level(i))
    level, _unused = mixed_levels(iota((1, 128), 1))
    return (1 << level).astype(F32)


INNER = (1, 2, 3, 4, 5, 6, 9, 10)
OUTER = (0, 7, 8, 11, 12, 13, 14, 15)


def labels_of(total, squares, times):
    return jnp.where(times * squares == total * total, total / times, 0.0)


def head_masks(rows):
    lane = iota((rows, 128), 1)
    return ones_where(lane < 64), ones_where(lane >= 64)


def by_head(x, masks):
    return jnp.concatenate([x * masks[0], x * masks[1]], axis=0)


def own_blocks(x):
    return jnp.concatenate([x[0:64, 0:128], x[64:128, 128:256]], axis=0)


def twice(x):
    return jnp.concatenate([x, x], axis=1)


def two_rows(a, b):
    row = iota((16, a.shape[1]), 0)
    return jnp.where(row == 0, a, jnp.where(row == 1, b, 0.0))


def lanes_of(g, base=0):
    return pl.ds(pl.multiple_of(base + g * 128, 128), 128)


def coarse_cols(ref, base, j):
    return jnp.concatenate([ref[:, base + 128 * j:base + 128 * j + 128],
                            ref[:, base + 512 + 128 * (j // 2):base + 640 + 128 * (j // 2)],
                            ref[:, base + 768:base + 1024]], axis=1)


def coarse_blocks():
    return ([(128 * j, 0, 256 * j, 256) for j in range(4)] + [(512 + 128 * j, 1, 512 * j, 512) for j in range(2)]
            + [(768, 2, 0, 1024), (896, 3, 0, 1024)])


def near_rows(side):
    o, i = iota((96, 128), 0), iota((96, 128), 1)
    level = (o >> 4) + 1
    block = i >> 4
    fine = jnp.maximum(block - 1, 0)
    value_out, value_in = (o >> 3) & 1, jnp.where(block < 2, block, (i >> 3) & 1)
    width, size = jnp.left_shift(1, fine), jnp.left_shift(1, level)
    if side == 0:
        start = ((o & 7) - 8) * size
        at = jnp.where(block < 2, (i & 15) - 16, (i & 7) - 16) * width
    else:
        start = (o & 7) * size
        at = jnp.where(block < 2, i & 15, (i & 7) + 8) * width
    inside = (value_out == value_in) & (at >= start) & (at + width <= start + size)
    share = jnp.where(value_out == 1, 1.0, width.astype(F32) / size.astype(F32))
    return jnp.where(inside, share, 0.0).astype(BF16)


def wide_rows(value):
    r, i = iota((128, 128), 0), iota((128, 128), 1)
    k, j = r & 15, (i & 15) - 8 * value
    own = ((r >> 4) == (i >> 4)) & (j >= 0) & (j < 8)
    fine, rough = own & (k < 8) & (j == k), own & (k >= 8) & (k < 12) & ((j >> 1) == k - 8)
    return jnp.where(fine, 1.0, jnp.where(rough, 1.0 if value else 0.5, 0.0)).astype(BF16)


def far_and_near(side, far, near):
    return jnp.concatenate([far, near] if side == 0 else [near, far], axis=0)


def border(side, l):
    return EXT_AT[l] + (16 + SIZES[l] if side else 0)


def own_border(side, l):
    return EXT_AT[l] + (SIZES[l] if side else 16)


def pick_far(side, rows):
    return rows[0:8] if side else rows[8:16]


def column_of(row, n):
    spread = jnp.where(iota((n, n), 0) == iota((n, n), 1), jnp.broadcast_to(row, (n, n)), 0.0)
    return jnp.broadcast_to(jnp.sum(spread, axis=1, keepdims=True), (n, 128)).astype(BF16)


def where_am_i():
    h = lax.axis_index("head")
    s = lax.axis_index("span")
    return h, s, s // 4, (s // 2) % 2, s % 2


class Peers:
    def __init__(self, near):
        h, s = lax.axis_index("head"), lax.axis_index("span")
        odd = s % 2
        self.place = odd * 4 + h
        self.odd = odd
        self.h = h
        other = s + 1 - 2 * odd
        self.z_index = [lax.rem(h + d, 4) for d in (1, 2, 3)]
        self.zs = [{"head": z} for z in self.z_index]
        self.core = {"span": other}
        opposite = {"head": 3 - h, "span": other}
        step = 1 - 2 * odd
        self.right = {"head": lax.rem(h + 1, 4), "span": s + step * ((h + 1) // 4)}
        self.left = {"head": lax.rem(h + 3, 4), "span": s + step * (1 - (h + 3) // 4)}
        self.greeted = self.zs + [self.core, opposite]
        if near:
            y, x = s // 4, (s // 2) % 2
            self.y, self.x, self.c = y, x, odd
            self.s = s
            self.px = {"span": y * 4 + (1 - x) * 2 + odd}
            self.py = {"span": (1 - y) * 4 + x * 2 + odd}
            self.s_index = [lax.rem(s + d, 8) for d in range(1, 8)]
            self.spans = [{"span": o} for o in self.s_index]
            self.greeted = self.zs + self.spans + [opposite]


def greet(devices):
    barrier = pltpu.get_barrier_semaphore()
    for d in devices:
        pl.semaphore_signal(barrier, inc=1, device_id=d, device_id_type=MESH)
    pl.semaphore_wait(barrier, len(devices))


def rcopy(src, dst, send, recv, device):
    return pltpu.make_async_remote_copy(src_ref=src, dst_ref=dst, send_sem=send, recv_sem=recv,
                                        device_id=device, device_id_type=MESH)


class Gather:
    def __init__(self, me, shard, full, swap, local, send, recv):
        self.me, self.shard, self.full, self.swap, self.local, self.send, self.recv = me, shard, full, swap, local, send, recv

    def own(self):
        m = self.me
        return pltpu.make_async_copy(self.shard, self.full(m.h, m.y, m.x, m.c), self.local)

    def hop(self, k):
        m, a = self.me, slice(None)
        if k < 3:
            return rcopy(self.shard, self.full(m.h, m.y, m.x, m.c), self.send.at[k], self.recv.at[k], m.zs[k])
        if k == 3:
            ref, dev = self.full(a, m.y, m.x, m.c), m.py if self.swap else m.px
        elif k == 4:
            ref, dev = (self.full(a, a, m.x, m.c), m.px) if self.swap else (self.full(a, m.y, a, m.c), m.py)
        else:
            ref, dev = self.full(a, a, a, m.c), m.core
        return rcopy(ref, ref, self.send.at[k], self.recv.at[k], dev)

    def start(self, stage):
        if stage == 0:
            self.own().start()
            for k in range(3):
                self.hop(k).start()
        else:
            self.hop(2 + stage).start()

    def wait(self, stage):
        if stage == 0:
            self.own().wait()
            for k in range(3):
                self.hop(k).wait()
        else:
            self.hop(2 + stage).wait()


class Scatter:
    def __init__(self, me, grad, mine, swap, bufs, send, recv):
        self.me, self.grad, self.mine, self.swap, self.bufs, self.send, self.recv = me, grad, mine, swap, bufs, send, recv

    def hops(self, stage):
        m, s, r = self.me, self.send, self.recv
        r1, r2, r3, r4 = self.bufs
        if stage == 0:
            return [rcopy(self.grad(1 - m.c), r1, s.at[0], r.at[0], m.core)]
        if stage == 1:
            src, dev = (r1.at[:, 1 - m.y], m.py) if self.swap else (r1.at[:, :, 1 - m.x], m.px)
            return [rcopy(src, r2, s.at[1], r.at[1], dev)]
        if stage == 2:
            src, dev = (r2.at[:, 1 - m.x], m.px) if self.swap else (r2.at[:, 1 - m.y], m.py)
            return [rcopy(src, r3, s.at[2], r.at[2], dev)]
        return [rcopy(r3.at[m.z_index[k]], r4.at[k], s.at[3 + k], r.at[3 + k], m.zs[k]) for k in range(3)]

    def start(self, stage):
        for cp in self.hops(stage):
            cp.start()

    def wait(self, stage):
        for cp in self.hops(stage):
            cp.wait()

    def add(self, stage):
        m = self.me
        r1, r2, r3, r4 = self.bufs

        def into(dst, key, other):
            dst[key] = (dst[key].astype(F32) + other.astype(F32)).astype(dst.dtype)
        if stage == 0:
            @pl.loop(0, 4)
            def _(hh):
                for yy in range(2):
                    for xx in range(2):
                        into(r1, (hh, yy, xx), self.mine(hh, yy, xx))
        elif stage == 1:
            @pl.loop(0, 4)
            def _(hh):
                for v in range(2):
                    into(r2, (hh, v), r1[hh, m.y, v] if self.swap else r1[hh, v, m.x])
        else:
            @pl.loop(0, 4)
            def _(hh):
                into(r3, (hh,), r2[hh, m.x if self.swap else m.y])

    def result(self):
        r1, r2, r3, r4 = self.bufs
        acc = r3[self.me.h].astype(F32)
        for k in range(3):
            acc = acc + r4[k].astype(F32)
        return acc


class SmallGather:
    def __init__(self, me, tile, full, local, send, recv):
        self.me, self.tile, self.full, self.local, self.send, self.recv = me, tile, full, local, send, recv

    def first(self):
        dst = self.full.at[self.me.h, self.me.s]
        return [rcopy(self.tile, dst, self.send.at[k], self.recv.at[k], self.me.zs[k]) for k in range(3)]

    def second(self):
        ref = self.full.at[:, self.me.s]
        return [rcopy(ref, ref, self.send.at[3 + k], self.recv.at[3 + k], self.me.spans[k]) for k in range(7)]

    def own(self):
        return pltpu.make_async_copy(self.tile, self.full.at[self.me.h, self.me.s], self.local)


class SmallScatter:
    def __init__(self, me, grad, got, total, got_z, send, recv):
        self.me, self.grad, self.got, self.total, self.got_z, self.send, self.recv = me, grad, got, total, got_z, send, recv

    def first(self):
        m = self.me
        return [rcopy(self.grad.at[:, m.s_index[k]], self.got.at[k], self.send.at[k], self.recv.at[k], m.spans[k]) for k in range(7)]

    def second(self):
        m = self.me
        return [rcopy(self.total.at[m.z_index[k]], self.got_z.at[k], self.send.at[7 + k], self.recv.at[7 + k], m.zs[k]) for k in range(3)]

    def add(self):
        v = self.grad[:, self.me.s]
        for k in range(7):
            v = v + self.got[k]
        self.total[...] = v

    def result(self):
        v = self.total[self.me.h]
        for k in range(3):
            v = v + self.got_z[k]
        return v


def start_all(copies):
    for cp in copies:
        cp.start()


def wait_all(copies):
    for cp in copies:
        cp.wait()


FFN_SHAPES = ((16, D), (16, FF // 2), (16, FF // 2), (32, D), (32, D))


def ffn_index(k, whole):
    half = (k - 1) % 2
    if k == 0:
        return 0, ()
    if k < 3:
        return 1, (slice(None), whole(FF // 2 * half, FF // 2))
    return 2, (whole(32 * half, 32),)


def ffn_view(refs, k, index):
    which, tail = ffn_index(k, pl.ds)
    return refs[which].at[index + tail]


def ffn_values(refs, k, index):
    which, tail = ffn_index(k, lambda at, n: slice(at, at + n))
    return refs[which][index + tail]


def scatter_bufs(shape, dtype):
    return [VMEM((4, 2, 2) + shape, dtype), VMEM((4, 2) + shape, dtype), VMEM((4,) + shape, dtype), VMEM((3,) + shape, dtype)]


def split3(v):
    high, rest = split(v)
    mid = rest
    low = (v - high.astype(F32) - mid.astype(F32)).astype(BF16)
    return high, mid, low


def mm_exact(v, ones):
    a, b, c = split3(v)
    return mm(a, ones) + mm(b, ones) + mm(c, ones)


def small_rows(vt, g1, s1, pb, ob, g2, s2, rb, eb):
    vt[...] = jnp.zeros_like(vt)
    for r, ref in enumerate((g1, s1, None, None, None, ob, g2, s2)):
        vt[r:r + 1, 0:16] = pb[r - 2:r - 1, :] if ref is None else ref[...]
    vt[0:1, 16:32] = rb[...]
    for r in range(8):
        vt[r:r + 1, 32:40] = eb[0:1, 8 * r:8 * r + 8]


def unpack_small(gathered, vecs, b1):
    v = gathered[...].reshape(256, 128)
    row, n = iota((256, D), 0), iota((256, D), 1)
    lane, col = iota((128, D), 0), iota((128, D), 1)
    mine = (row >> 3) == (n >> 4)
    for half in range(2):
        x = mm_exact(v, ones_where(lane == (col & 15) + 16 * half))
        vecs[8 * half:8 * half + 8, :] = jnp.sum(jnp.where(mine, x, 0.0).reshape(32, 8, D), axis=0)
    x = mm_exact(v, ones_where(lane == (col & 7) + 32))
    for q in range(4):
        ok = ((row >> 3) == ((n + 512 * q) >> 6)) & ((row & 7) == ((n >> 3) & 7))
        b1[0:1, D * q:D * q + D] = jnp.sum(jnp.where(ok, x, 0.0), axis=0, keepdims=True)


def fill_bias(bias, labk, labq, place, tiles):
    def matching(i):
        kl = labk[tile_at(i):tile_at(i) + tile_keys(i), :].astype(F32)
        return (kl == labq[i:i + 1, :]) & (kl != 0.0)

    r, c = iota((160, 128), 0), iota((160, 128), 1)
    near = jnp.abs((r >> 4) - 1 - (c >> 4)) <= 1
    far = near & (jnp.abs((r >> 3) - 2 - (c >> 3)) >= 2)
    same = (r - 16) == c
    for i in tiles:
        if i == 15:
            continue
        ok = matching(i) & near | same if i < 8 else matching(i) & far
        bias[160 * i:160 * i + 160, :] = jnp.where(ok, 0.0, NEG)
    if 15 not in tiles:
        return
    r, c = iota((336, 128), 0), iota((336, 128), 1)
    inner = (r >= 96).astype(I32) + (r >= 160).astype(I32)
    start = jnp.where(inner == 0, 0, jnp.where(inner == 1, 96, 160))
    e, k = (r - 208) >> 4, (r - 208) & 15
    upper = (k >= 8).astype(I32)
    level_k = jnp.where(r < 208, 4 + inner, 7 + upper)
    pos_k = jnp.where(r < 208, r - start - 16, jnp.where(k < 8, e * 8 + k, e * 4 + k - 8))
    level_q, start_q = mixed_levels(c)
    pos_q = c - start_q + jnp.where(level_q == 7, place * 8, jnp.where(level_q == 8, place * 4, 0))
    shape = (level_k == level_q) & (jnp.abs((pos_k >> 4) - (pos_q >> 4)) <= 1) & (jnp.abs((pos_k >> 3) - (pos_q >> 3)) >= 2)
    bias[BIAS_MIXED:BIASES, :] = jnp.where(matching(15) & shape, 0.0, NEG)


def bias_of(bias, i):
    return twice(bias[160 * i:160 * i + 160, :] if i < 15 else bias[BIAS_MIXED:BIASES, :])


def forward_kernel(near, *refs):
    refs = list(refs)

    def take(n):
        out = refs[:n]
        del refs[:n]
        return out
    tok, seg = take(2)
    if near:
        wq_in, = take(1)
        small = take(8)
        ffn_in = take(3)
    else:
        wq, vecs = take(2)
    kvx_o, qx_o, bias_o, a1_o, ao_o, iz_o, sp_o, spt_o = take(8)
    if near:
        wq_o, vecs_o, b1_o = take(3)
        ffn_o = take(3)
    kvx, qx, bias, a1, ao, iz, sp, spt, xh, labq, n0, nc, z0, labk, seg2, msg, got, wbuf, out_sem, e_send, e_recv = take(21)
    if near:
        wq, vecs, b1, vt, vg, local, send, recv, send_v, recv_v = take(10)
    me = Peers(near)
    place = me.place
    outs = []

    def emit(src, dst):
        cp = pltpu.make_async_copy(src, dst, out_sem.at[len(outs)])
        cp.start()
        outs.append(cp)

    got[...] = jnp.zeros_like(got)
    if near:
        small_rows(vt, *small)
    greet(me.greeted)
    ids_core = rcopy(seg, seg2, e_send.at[6], e_recv.at[6], me.core)
    ids_core.start()
    if near:
        small_g = SmallGather(me, vt, vg, local.at[15], send_v, recv_v)
        small_g.own().start()
        start_all(small_g.first())
        first = []
        for k in range(2):
            lanes = pl.ds(256 * k, 256)
            first.append(Gather(me, wq_in.at[:, :, lanes], lambda h, y, x, c, lanes=lanes: wq.at[:, h, y, x, c, :, lanes], k == 1,
                                local.at[k], send.at[k], recv.at[k]))
        later = [Gather(me, ffn_view(ffn_in, k, ()), lambda h, y, x, c, k=k: ffn_view(ffn_o, k, (h, y, x, c)), k in (2, 4),
                        local.at[2 + k], send.at[2 + k], recv.at[2 + k]) for k in range(5)]

    def step(group, stage, *pieces):
        if not near:
            return
        for k in pieces:
            a = (first if group == 0 else later)[k]
            if stage >= 0:
                a.wait(stage)
            if stage < 3:
                a.start(stage + 1)

    step(0, -1, 0, 1)
    fill_pool(sp)
    fill_spread(spt)
    emit(sp, sp_o)
    emit(spt, spt_o)
    if near:
        small_g.own().wait()
        wait_all(small_g.first())
        start_all(small_g.second())
    step(0, 0, 0, 1)
    step(1, -1, 0, 1, 2, 3, 4)
    ids_core.wait()

    def chunk(ref, k):
        return ref[:, pl.ds(pl.multiple_of(TOK * k, TOK), TOK)].astype(F32)
    odd = me.odd.astype(F32)
    ids = chunk(seg, me.h)
    ids_left = jnp.where(me.h > 0, chunk(seg, lax.rem(me.h + 3, 4)), chunk(seg2, 3) * odd)
    ids_right = jnp.where(me.h < 3, chunk(seg, lax.rem(me.h + 1, 4)), chunk(seg2, 0) * (1.0 - odd))
    ids_b = jnp.broadcast_to(ids, (128, TOK)).astype(BF16)
    sq_b = jnp.broadcast_to(ids * ids, (128, TOK)).astype(BF16)
    eye = identity(TILE)
    for j in range(TILES):
        labk[16 + TILE * j:16 + TILE * j + TILE, :] = mm_bt(eye, ids_b[:, TILE * j:TILE * j + TILE]).astype(BF16)
    for i in range(8):
        labq[i:i + 1, :] = ids[:, 128 * i:128 * i + 128]
    row, t = iota((128, TOK), 0), iota((128, TOK), 1)
    level, level_row = row >> 4, iota((1, 128), 1) >> 4
    for side, v in ((0, ids_left), (1, ids_right)):
        base = jnp.right_shift(TOK, level) - 16 if side == 0 else 0
        sel = ones_where(jnp.right_shift(t, level) == base + (row & 15))
        x = mm_bt(two_rows(v, v * v).astype(BF16), sel)
        col = column_of(labels_of(x[0:1], x[1:2], jnp.left_shift(1, level_row).astype(F32)), 128)
        for l in range(7):
            labk[border(side, l):border(side, l) + 16, :] = col[16 * l:16 * l + 16]
    even_ids = [jnp.where(me.odd == 0, chunk(seg, k), chunk(seg2, k)) for k in range(4)]
    odd_ids = [jnp.where(me.odd == 0, chunk(seg2, k), chunk(seg, k)) for k in range(4)]
    all_ids = jnp.concatenate(even_ids + odd_ids, axis=0)
    x = mm_bt(jnp.concatenate([all_ids, all_ids * all_ids], axis=0).astype(BF16), sp[496:512, :])
    lab = labels_of(x[0:8], x[8:16], jnp.where(iota((8, 16), 1) < 8, 128.0, 256.0))
    lab = jnp.broadcast_to(lab[:, None, :], (8, 16, 16)).reshape(128, 16)
    lab = jnp.sum(jnp.where((iota((128, 16), 0) & 15) == iota((128, 16), 1), lab, 0.0), axis=1, keepdims=True)
    labk[WIDE_AT:EXT, :] = jnp.broadcast_to(lab, (128, 128)).astype(BF16)

    def put_coarse(dst, b, value, cols):
        at, block, _t, _n = coarse_blocks()[b]
        if block < 3:
            level = block + 1
            row = EXT_AT[level] + 16 + at - (0, 512, 768)[block]
            dst[row:row + 128, cols] = value
        else:
            for level, a, n in ((4, 0, 64), (5, 64, 32), (6, 96, 16)):
                dst[EXT_AT[level] + 16:EXT_AT[level] + 16 + n, cols] = value[a:a + n]

    for b, (at, block, t, n) in enumerate(coarse_blocks()):
        s = sp[128 * block:128 * block + 128, t:t + n]
        rows_level, _unused = mixed_levels(iota((128, 128), 0))
        cols_level, _unused = mixed_levels(iota((8, 128), 1))
        times_r = (1 << rows_level).astype(F32) if block == 3 else float(2 ** (block + 1))
        times_c = (1 << cols_level).astype(F32) if block == 3 else float(2 ** (block + 1))
        lab = labels_of(mm_bt(s, ids_b[:, t:t + n]), mm_bt(s, sq_b[:, t:t + n]), times_r)
        put_coarse(labk, b, lab.astype(BF16), slice(0, 128))
        row = labels_of(mm_bt(ids_b[0:8, t:t + n], s), mm_bt(sq_b[0:8, t:t + n], s), times_c)
        labq[8 + b:9 + b, :] = row[0:1, :]
    step(0, 1, 0, 1)
    fill_bias(bias, labk, labq, place, range(16))
    emit(bias, bias_o)
    for j in range(TILES):
        v = tok[TILE * j:TILE * j + TILE, :].astype(F32)
        center = v - jnp.mean(v, axis=-1, keepdims=True)
        xh[TILE * j:TILE * j + TILE, :] = center * lax.rsqrt(jnp.mean(center * center, axis=-1, keepdims=True) + EPS)
    if near:
        wait_all(small_g.second())
        unpack_small(vg, vecs, b1)
        emit(vecs, vecs_o)
        emit(b1, b1_o)
    for j in range(TILES):
        rows = slice(TILE * j, TILE * j + TILE)
        a1[rows, :] = (xh[rows, :] * vecs[0:1, :] + vecs[1:2, :]).astype(BF16)
    emit(a1, a1_o)
    step(0, 2, 0, 1)
    step(1, 0, 0, 1, 2, 3, 4)
    step(0, 3, 0, 1)
    if near:
        emit(wq, wq_o)
    for c in range(3):
        w = wq[c].reshape(D, D)
        for j in range(TILES):
            r = (mm(a1[TILE * j:TILE * j + TILE, :], w) + vecs[2 + c:3 + c, :]).astype(BF16)
            if c == 0:
                qx[TILE * j:TILE * j + TILE, :] = r * jnp.array(0.125, BF16)
            else:
                kvx[16 + TILE * j:16 + TILE * j + TILE, D * (c - 1):D * c] = r
    step(1, 1, 0, 1, 2)
    for b, (at, block, t, n) in enumerate(coarse_blocks()):
        s = sp[128 * block:128 * block + 128, t:t + n]
        if block == 3:
            level, _unused = mixed_levels(iota((128, D), 0))
            shrink = 1.0 / (1 << level).astype(F32)
        else:
            shrink = 0.5 ** (block + 1)
        qx[1024 + at:1024 + at + 128, :] = (mm(s, qx[t:t + n, :]) * shrink).astype(BF16)
        kc, vc = mm(s, kvx[16 + t:16 + t + n, 0:D]) * shrink, mm(s, kvx[16 + t:16 + t + n, D:2 * D])
        put_coarse(kvx, b, kc.astype(BF16), slice(0, D))
        put_coarse(kvx, b, vc.astype(BF16), slice(D, 2 * D))
        if block == 3:
            wbuf[place] = jnp.concatenate([kc[112:120], vc[112:120]], axis=0).astype(BF16)
    step(1, 1, 3, 4)
    for side in range(2):
        for l in range(7):
            at = own_border(side, l)
            k16, v16 = kvx[at:at + 16, 0:D], kvx[at:at + 16, D:2 * D]
            if l == 0:
                msg[side, 0], msg[side, 1] = k16, v16
            else:
                far = [pick_far(side, v.astype(F32)) for v in (k16, v16)]
                msg[side, l + 1] = jnp.concatenate(far, axis=0).astype(BF16)
    to_right = rcopy(msg.at[1], got.at[0], e_send.at[0], e_recv.at[0], me.right)
    to_left = rcopy(msg.at[0], got.at[1], e_send.at[1], e_recv.at[1], me.left)
    wide_z = [rcopy(wbuf.at[place], wbuf.at[place], e_send.at[2 + k], e_recv.at[2 + k], me.zs[k]) for k in range(3)]
    four = wbuf.at[pl.ds(4 * me.odd, 4)]
    wide_core = rcopy(four, four, e_send.at[5], e_recv.at[5], me.core)
    not_last, not_first = place < 7, place > 0

    @pl.when(not_last)
    def _():
        to_right.start()

    @pl.when(not_first)
    def _():
        to_left.start()
    for cp in wide_z:
        cp.start()
    emit(qx, qx_o)
    masks = head_masks(128)

    def tile(g, i):
        keys = slice(tile_at(i), tile_at(i) + tile_keys(i))
        kw, vw = kvx[keys, lanes_of(g)], kvx[keys, lanes_of(g, D)]
        q = by_head(qx[128 * i:128 * i + 128, lanes_of(g)], masks)
        e = jnp.exp(mm_bt(kw, q) + bias_of(bias, i))
        times = tile_times(i)
        z = jnp.sum(e, axis=0, keepdims=True)
        z0_, z1_ = z[:, 0:128] * times, z[:, 128:256] * times
        n = own_blocks(mm_at(vw, e.astype(BF16)))
        if i < 8:
            cols = slice(128 * i, 128 * i + 128)
            n0[g, :, cols] = n
            z0[g, 0:1, cols] = z0_
            z0[g, 1:2, cols] = z1_
        else:
            cols = slice(128 * i - 1024, 128 * i - 896)
            high, low = split(two_rows(z0_, z1_))
            nc[g, :, cols] = jnp.concatenate([n.astype(BF16), high, low], axis=0)

    @pl.loop(0, 4)
    def _(g):
        for k in range(4):
            @pl.when(g == k)
            def _():
                if k == 3:
                    step(1, 2, 0, 2)
                if k == 1:
                    wait_all(wide_z)
                    wide_core.start()
        for i in INNER:
            tile(g, i)

    wide_core.wait()
    w = wbuf[...].reshape(128, D)
    kvx[WIDE_AT:EXT, 0:D] = mm(wide_rows(0), w).astype(BF16)
    kvx[WIDE_AT:EXT, D:2 * D] = mm(wide_rows(1), w).astype(BF16)

    @pl.when(not_last)
    def _():
        to_right.wait_send()
        to_left.wait_recv()

    @pl.when(not_first)
    def _():
        to_left.wait_send()
        to_right.wait_recv()
    for side in range(2):
        m = got[side].reshape(128, D)
        closer = mm(near_rows(side), m)
        m = m.astype(F32)
        for l in range(7):
            at = border(side, l)
            if l == 0:
                k16, v16 = m[0:16], m[16:32]
            else:
                a, b = 16 * (l + 1), 16 * (l - 1)
                k16 = far_and_near(side, m[a:a + 8], closer[b:b + 8])
                v16 = far_and_near(side, m[a + 8:a + 16], closer[b + 8:b + 16])
            kvx[at:at + 16, 0:D] = k16.astype(BF16)
            kvx[at:at + 16, D:2 * D] = v16.astype(BF16)
    emit(kvx, kvx_o)

    @pl.loop(0, 4)
    def _(g):
        for k in range(4):
            @pl.when(g == k)
            def _():
                if k > 0:
                    step(1, 2, (None, 1, 4, 3)[k])
        for i in OUTER:
            tile(g, i)
        c_ref = nc.at[g]
        for j in range(TILES):
            cols = slice(TILE * j, TILE * j + TILE)
            r = mm(coarse_cols(c_ref, 0, j), sp[:, cols])
            n = n0[g, :, cols] + r[0:128]
            i0 = 1.0 / (z0[g, 0:1, cols] + r[128:129] + r[144:145])
            i1 = 1.0 / (z0[g, 1:2, cols] + r[129:130] + r[145:146])
            iz[g, 0:1, cols] = i0
            iz[g, 1:2, cols] = i1
            ao[pl.ds(pl.multiple_of(g * 128, 128), 64), cols] = (n[0:64] * i0).astype(BF16)
            ao[pl.ds(pl.multiple_of(g * 128 + 64, 64), 64), cols] = (n[64:128] * i1).astype(BF16)
    emit(ao, ao_o)
    emit(iz, iz_o)
    step(1, 3, 0, 1, 2, 3, 4)
    wait_all(outs)


ANY = pl.BlockSpec(memory_space=pl.ANY)
IN_VMEM = pl.BlockSpec(memory_space=pltpu.VMEM)
S = jax.ShapeDtypeStruct
SEM = pltpu.SemaphoreType.DMA


def forward(near, tok, seg, *params):
    grid = (4, 2, 2, 2)
    shapes = [S((EXT, 2 * D), BF16), S((2048, D), BF16), S((BIASES, 128), F32), S((TOK, D), BF16), S((D, TOK), BF16),
              S((4, 2, TOK), F32), S((512, TOK), BF16), S((TOK, 512), BF16)]
    scratch = [VMEM(s.shape, s.dtype) for s in shapes] + [
        VMEM((TOK, D), F32), VMEM((16, 128), F32), VMEM((4, 128, TOK), F32), VMEM((4, 160, TOK), BF16), VMEM((4, 2, TOK), F32),
        VMEM((EXT, 128), BF16), VMEM(seg.shape, I32), VMEM((2, 8, 16, D), BF16), VMEM((2, 8, 16, D), BF16), VMEM((8, 16, D), BF16),
        SEM((16,)), SEM((7,)), SEM((7,))]
    if near:
        shapes += [S((3,) + grid + (16, D), BF16), S((16, D), F32), S((1, FF), F32)]
        shapes += [S(grid + a.shape, a.dtype) for a in params[9:]]
        scratch += [VMEM((3,) + grid + (16, D), BF16), VMEM((16, D), F32), VMEM((1, FF), F32), VMEM((8, 128), F32),
                    VMEM((4, 8, 8, 128), F32), SEM((16,)), SEM((7, 6)), SEM((7, 6)), SEM((10,)), SEM((10,))]
        specs = [IN_VMEM] * 9 + [ANY] * 3
    else:
        specs = [IN_VMEM] * 2
    return pl.pallas_call(
        functools.partial(forward_kernel, near),
        out_shape=shapes,
        in_specs=[IN_VMEM, IN_VMEM] + specs,
        out_specs=[ANY] * len(shapes),
        scratch_shapes=scratch,
        compiler_params=pltpu.CompilerParams(collective_id=0, has_side_effects=True, vmem_limit_bytes=60 << 20),
        name="forward",
    )(tok, seg, *params)


C0 = 0.7978845608028654
C1 = 0.044715


def middle_kernel(tok, ao, cot, wo, w1, w2, vecs, b1, out, dh1_out, da_out, gwo, gw1, gw2, gvec, gb1,
                  awo, aw1, aw2, avec, ab1):
    j = pl.program_id(0)

    @pl.when(j == 0)
    def _():
        awo[...] = jnp.zeros_like(awo)
        aw1[...] = jnp.zeros_like(aw1)
        aw2[...] = jnp.zeros_like(aw2)
        avec[...] = jnp.zeros_like(avec)
        ab1[...] = jnp.zeros_like(ab1)
    mixed = ao[...]
    h1 = tok[...].astype(F32) + mm_at(mixed, wo[...]) + vecs[5:6, :]
    center = h1 - jnp.mean(h1, axis=-1, keepdims=True)
    inverse = lax.rsqrt(jnp.mean(center * center, axis=-1, keepdims=True) + EPS)
    xh = center * inverse
    gain = vecs[6:7, :]
    a2 = (xh * gain + vecs[7:8, :]).astype(BF16)
    dy = cot[...]
    y = h1 + vecs[8:9, :]
    da2 = jnp.zeros((TILE, D), F32)
    for k in range(FF // D):
        cols = slice(D * k, D * k + D)
        u = mm(a2, w1[:, cols]) + b1[:, cols]
        u2 = u * u
        th = jnp.tanh(u * (C0 + (C0 * C1) * u2))
        half = 0.5 * (1.0 + th)
        g = (u * half).astype(BF16)
        slope = half + 0.5 * u * (1.0 - th * th) * (C0 + (3.0 * C0 * C1) * u2)
        y = y + mm(g, w2[cols, :])
        du = (mm_bt(dy, w2[cols, :]) * slope).astype(BF16)
        aw2[cols, :] += mm_at(g, dy)
        aw1[:, cols] += mm_at(a2, du)
        ab1[:, cols] += jnp.sum(du.astype(F32), axis=0, keepdims=True)
        da2 = da2 + mm_bt(du, w1[:, cols])
    out[...] = y.astype(BF16)
    dyf = dy.astype(F32)
    e = da2 * gain
    dh1 = dyf + inverse * (e - jnp.mean(e, axis=-1, keepdims=True) - xh * jnp.mean(e * xh, axis=-1, keepdims=True))
    dh1_out[...] = dh1
    db = dh1.astype(BF16)
    awo[...] += mm(mixed, db)
    da_out[...] = mm_bt(wo[...], db).astype(BF16)
    avec[5:6, :] += jnp.sum(db.astype(F32), axis=0, keepdims=True)
    avec[6:7, :] += jnp.sum(da2 * xh, axis=0, keepdims=True)
    avec[7:8, :] += jnp.sum(da2, axis=0, keepdims=True)
    avec[8:9, :] += jnp.sum(dyf, axis=0, keepdims=True)

    @pl.when(j == TOK // TILE - 1)
    def _():
        gwo[...] = awo[...].astype(BF16)
        gw1[...] = aw1[...].astype(BF16)
        gw2[...] = aw2[...].astype(BF16)
        gvec[...] = avec[...]
        gb1[...] = ab1[...]


def whole(shape):
    return pl.BlockSpec(shape, lambda j: (0,) * len(shape), pipeline_mode=pl.Buffered(1))


def middle(tok, ao, cot, wo, w1, w2, vecs, b1):
    tile = pl.BlockSpec((TILE, D), lambda j: (j, 0))
    flat = pl.BlockSpec((D, TILE), lambda j: (0, j))
    return pl.pallas_call(
        middle_kernel,
        grid=(TOK // TILE,),
        out_shape=[S((TOK, D), BF16), S((TOK, D), F32), S((D, TOK), BF16), S((D, D), BF16), S((D, FF), BF16), S((FF, D), BF16),
                   S((16, D), F32), S((1, FF), F32)],
        in_specs=[tile, flat, tile, whole((D, D)), whole((D, FF)), whole((FF, D)), whole((16, D)), whole((1, FF))],
        out_specs=[tile, tile, flat, whole((D, D)), whole((D, FF)), whole((FF, D)), whole((16, D)), whole((1, FF))],
        scratch_shapes=[VMEM((D, D), F32), VMEM((D, FF), F32), VMEM((FF, D), F32), VMEM((16, D), F32), VMEM((1, FF), F32)],
        compiler_params=pltpu.CompilerParams(dimension_semantics=("arbitrary",), vmem_limit_bytes=60 << 20),
        name="middle",
    )(tok, ao, cot, wo, w1, w2, vecs, b1)


def pack_small(rows, b1):
    row, n = iota((256, D), 0), iota((256, D), 1)
    lane, col = iota((128, D), 0), iota((128, D), 1)
    mine = (row >> 3) == (n >> 4)

    def moved(v, ok, ones):
        total = None
        for part in split3(jnp.where(ok, v, 0.0)):
            r = mm_bt(part, ones)
            total = r if total is None else total + r
        return total
    eight = jnp.broadcast_to(rows[0:8][None], (32, 8, D)).reshape(256, D)
    out = moved(eight, mine, ones_where(lane == (col & 15)))
    out = out + moved(jnp.broadcast_to(rows[8:9], (256, D)), mine & ((row & 7) == 0), ones_where(lane == (col & 15) + 16))
    last = ones_where(lane == (col & 7) + 32)
    for q in range(4):
        ok = ((row >> 3) == ((n + 512 * q) >> 6)) & ((row & 7) == ((n >> 3) & 7))
        out = out + moved(jnp.broadcast_to(b1[0:1, D * q:D * q + D], (256, D)), ok, last)
    return out.reshape(4, 8, 8, 128)


def backward_kernel(near, *refs):
    refs = list(refs)

    def take(n):
        out = refs[:n]
        del refs[:n]
        return out
    ins = take(13)
    gffn, (gvec, gb1) = take(3), take(2)
    tok_o, gq_o = take(2)
    small_o = take(8 if near else 1)
    gffn_o = take(3 if near else 0)
    kvx, qx, bias, a1, ao, iz, sp, spt, da, tok, dh1, wq, vecs = take(13)
    gr, rm, dqt, dkv, dq, edge, e_got, w_all, w_got, w_mid, gq, avec, tok_s, dall, in_sem, out_sem, e_send, e_recv = take(18)
    if near:
        gv, f_mine, f_sem, send, recv, send_v, recv_v, v_got, v_sum, v_z = take(10)
        bufs = [take(4) for _ in range(11)]
    me = Peers(near)
    place = me.place
    loads = {}
    targets = (da, ao, iz, sp, kvx, qx, bias, spt, a1, tok, dh1, wq, vecs)
    names = ("da", "ao", "iz", "sp", "kvx", "qx", "bias", "spt", "a1", "tok", "dh1", "wq", "vecs")
    for k, name in enumerate(names):
        loads[name] = pltpu.make_async_copy(ins[k], targets[k], in_sem.at[k])
        loads[name].start()
    greet(me.greeted)
    mine_copies = []
    if near:
        for k in range(3):
            cp = pltpu.make_async_copy(gffn[k].at[:, :, :, me.c], f_mine[k], f_sem.at[k])
            cp.start()
            mine_copies.append(cp)
        every = slice(None)
        ffn = [Scatter(me, lambda c, k=k: ffn_view(gffn, k, (every, every, every, c)), lambda h, y, x, k=k: ffn_values(f_mine, k, (h, y, x)),
                       k in (2, 4), bufs[k], send.at[k], recv.at[k]) for k in range(5)]
        last = []
        for k in range(6):
            lo = 256 * (k % 2)
            last.append(Scatter(me, lambda c, k=k, lo=lo: gq.at[k // 2, :, :, :, c, :, pl.ds(lo, 256)],
                                lambda h, y, x, k=k, lo=lo: gq[k // 2, h, y, x, me.c, :, lo:lo + 256], k % 2 == 1,
                                bufs[5 + k], send.at[5 + k], recv.at[5 + k]))
        small_s = SmallScatter(me, gv, v_got, v_sum, v_z, send_v, recv_v)
        for a in ffn:
            a.start(0)

    def put_ffn(k):
        which, tail = ffn_index(k, lambda at, n: slice(at, at + n))
        gffn_o[which][tail or (slice(None),)] = ffn[k].result()

    def put_last(k):
        gq_o[k // 2, :, 256 * (k % 2):256 * (k % 2) + 256] = last[k].result()

    def step(group, stage, *pieces):
        if not near:
            return
        for k in pieces:
            a = (ffn if group == 0 else last)[k]
            a.wait(stage)
            if stage < 3:
                a.add(stage)
                a.start(stage + 1)
            elif group == 0:
                put_ffn(k)
            else:
                put_last(k)

    for name in ("da", "ao", "iz", "sp"):
        loads[name].wait()
    masks = head_masks(128)

    @pl.loop(0, 4)
    def _(g):
        lo, hi = pl.ds(pl.multiple_of(g * 128, 128), 64), pl.ds(pl.multiple_of(g * 128 + 64, 64), 64)
        for j in range(TILES):
            cols = slice(TILE * j, TILE * j + TILE)
            g0 = da[lo, cols].astype(F32) * iz[g, 0:1, cols]
            g1 = da[hi, cols].astype(F32) * iz[g, 1:2, cols]
            r0 = jnp.sum(g0 * ao[lo, cols].astype(F32), axis=0, keepdims=True)
            r1 = jnp.sum(g1 * ao[hi, cols].astype(F32), axis=0, keepdims=True)
            rm[g, 0:1, cols] = r0
            rm[g, 1:2, cols] = r1
            high, low = split(two_rows(r0, r1))
            gr[g, :, cols] = jnp.concatenate([g0.astype(BF16), g1.astype(BF16), high, low], axis=0)
        for b, (at, block, t, n) in enumerate(coarse_blocks()):
            x = mm_bt(gr[g, :, t:t + n], sp[128 * block:128 * block + 128, t:t + n])
            cols = slice(1024 + at, 1152 + at)
            gr[g, 0:128, cols] = x[0:128].astype(BF16)
            times = tile_times(8 + b)
            rm[g, 0:1, cols] = (x[128:129] + x[144:145]) * times
            rm[g, 1:2, cols] = (x[129:130] + x[145:146]) * times
    dkv[...] = jnp.zeros_like(dkv)
    for name in ("kvx", "qx", "bias"):
        loads[name].wait()
    zero = jnp.zeros((64, 128), BF16)

    def tile(g, i):
        keys = slice(tile_at(i), tile_at(i) + tile_keys(i))
        cols = slice(128 * i, 128 * i + 128)
        kw, vw = kvx[keys, lanes_of(g)], kvx[keys, lanes_of(g, D)]
        q = by_head(qx[cols, lanes_of(g)], masks)
        gt = gr[g, 0:128, cols]
        gb = jnp.concatenate([jnp.concatenate([gt[0:64], zero], axis=1), jnp.concatenate([zero, gt[64:128]], axis=1)], axis=0)
        e = jnp.exp(mm_bt(kw, q) + bias_of(bias, i))
        rest = jnp.concatenate([rm[g, 0:1, cols], rm[g, 1:2, cols]], axis=1)
        ds = (e * (mm(vw, gb) - rest)).astype(BF16)
        dkv[keys, lanes_of(g)] += mm(ds, q)
        dkv[keys, lanes_of(g, D)] += mm_bt(e.astype(BF16), gb)
        dqt[g, :, cols] = (own_blocks(mm_at(kw, ds)) * (0.125 / tile_times(i))).astype(BF16)

    if near:
        wait_all(mine_copies)
    step(0, 0, 0, 1, 2, 3, 4)

    @pl.loop(0, 4)
    def _(g):
        for i in OUTER:
            tile(g, i)
    for side in range(2):
        base, closer = [], []
        for l in range(7):
            at = border(side, l)
            k16, v16 = dkv[at:at + 16, 0:D], dkv[at:at + 16, D:2 * D]
            if l == 0:
                base += [k16, v16]
            elif side == 0:
                base += [k16[0:8], v16[0:8]]
                closer += [k16[8:16], v16[8:16]]
            else:
                base += [k16[8:16], v16[8:16]]
                closer += [k16[0:8], v16[0:8]]
        folded = mm_at(near_rows(side), jnp.concatenate(closer, axis=0).astype(BF16))
        edge[side] = (jnp.concatenate(base, axis=0) + folded).astype(BF16).reshape(8, 16, D)
    d_wide = mm_at(wide_rows(0), dkv[WIDE_AT:EXT, 0:D].astype(BF16)) + mm_at(wide_rows(1), dkv[WIDE_AT:EXT, D:2 * D].astype(BF16))
    w_all[...] = d_wide.astype(BF16).reshape(8, 16, D)
    to_right = rcopy(edge.at[1], e_got.at[0], e_send.at[0], e_recv.at[0], me.right)
    to_left = rcopy(edge.at[0], e_got.at[1], e_send.at[1], e_recv.at[1], me.left)
    wide_core = rcopy(w_all.at[pl.ds(4 * (1 - me.odd), 4)], w_mid, e_send.at[2], e_recv.at[2], me.core)
    not_last, not_first = place < 7, place > 0
    wide_core.start()

    @pl.when(not_last)
    def _():
        to_right.start()

    @pl.when(not_first)
    def _():
        to_left.start()
    step(0, 1, 0, 1, 2)

    @pl.loop(0, 2)
    def _(g):
        for i in INNER:
            tile(g, i)
    wide_core.wait()
    for k in range(4):
        w_mid[k] = (w_mid[k].astype(F32) + w_all[4 * me.odd + k].astype(F32)).astype(BF16)
    wide_z = [rcopy(w_mid.at[me.z_index[k]], w_got.at[k], e_send.at[3 + k], e_recv.at[3 + k], me.zs[k]) for k in range(3)]
    start_all(wide_z)

    @pl.loop(2, 4)
    def _(g):
        for i in INNER:
            tile(g, i)
    step(0, 1, 3, 4)

    @pl.loop(0, 4)
    def _(g):
        d_ref = dqt.at[g]
        eye = identity(TILE)
        for j in range(TILES):
            cols = slice(TILE * j, TILE * j + TILE)
            r = d_ref[:, cols].astype(F32) + mm(coarse_cols(d_ref, 1024, j), sp[:, cols])
            dq[cols, lanes_of(g)] = mm_bt(eye, r.astype(BF16)).astype(BF16)
    for name in ("spt", "a1", "tok", "dh1", "wq", "vecs"):
        loads[name].wait()
    avec[...] = jnp.zeros_like(avec)

    def projection_grad(c, d):
        aw = mm_at(a1[...], d).astype(BF16)
        avec[2 + c:3 + c, :] = jnp.sum(d.astype(F32), axis=0, keepdims=True)
        gq[c] = aw.reshape(4, 2, 2, 2, 16, D)
        if near:
            for a in last[2 * c:2 * c + 2]:
                a.start(0)
    projection_grad(0, dq[...])
    step(0, 2, 0, 1, 2)
    for cp in wide_z:
        cp.wait()

    def add_edge(side):
        m = e_got[side].reshape(128, D).astype(F32)
        for l in range(7):
            if l == 0:
                at, n = own_border(side, 0), 16
            else:
                at, n = own_border(side, l) + (0 if side else 8), 8
            a = 16 * (l + 1) if l else 0
            dkv[at:at + n, 0:D] += m[a:a + n]
            dkv[at:at + n, D:2 * D] += m[a + n:a + 2 * n]

    @pl.when(not_last)
    def _():
        to_right.wait_send()
        to_left.wait_recv()
        add_edge(1)

    @pl.when(not_first)
    def _():
        to_left.wait_send()
        to_right.wait_recv()
        add_edge(0)
    v = w_mid[me.h].astype(F32)
    for k in range(3):
        v = v + w_got[k].astype(F32)
    v = jnp.concatenate([v[0:8] * 0.5 ** 7, v[8:16]], axis=1)
    w_own = jnp.concatenate([v, jnp.zeros((8, 2 * D), F32)], axis=0).astype(BF16)
    lane_all = iota((1, 2 * D), 1)

    def coarse_rows(at, n, level):
        return (dkv[at:at + n, :] * jnp.where(lane_all < D, 0.5 ** level, 1.0)).astype(BF16)
    top = jnp.concatenate([coarse_rows(EXT_AT[3] + 16, 128, 3), coarse_rows(EXT_AT[4] + 16, 64, 4), coarse_rows(EXT_AT[5] + 16, 32, 5),
                           coarse_rows(EXT_AT[6] + 16, 16, 6), w_own], axis=0)
    for j in range(TILES):
        rows = slice(TILE * j, TILE * j + TILE)
        x = jnp.concatenate([coarse_rows(EXT_AT[1] + 16 + 128 * j, 128, 1), coarse_rows(EXT_AT[2] + 16 + 128 * (j // 2), 128, 2), top], axis=0)
        dall[rows, :] = (dkv[16 + TILE * j:16 + TILE * j + TILE, :] + mm(spt[rows, :], x)).astype(BF16)
    projection_grad(1, dall[:, 0:D])
    step(0, 2, 3, 4)
    step(1, 0, 0, 1)
    projection_grad(2, dall[:, D:2 * D])
    step(1, 0, 2, 3)
    for j in range(TILES):
        rows = slice(TILE * j, TILE * j + TILE)
        da1 = mm_bt(dq[rows, :], wq[0].reshape(D, D)) + mm_bt(dall[rows, 0:D], wq[1].reshape(D, D)) + mm_bt(dall[rows, D:2 * D], wq[2].reshape(D, D))
        v = tok[rows, :].astype(F32)
        center = v - jnp.mean(v, axis=-1, keepdims=True)
        inverse = lax.rsqrt(jnp.mean(center * center, axis=-1, keepdims=True) + EPS)
        n = center * inverse
        e = da1 * vecs[0:1, :]
        dv = inverse * (e - jnp.mean(e, axis=-1, keepdims=True) - n * jnp.mean(e * n, axis=-1, keepdims=True))
        tok_s[rows, :] = (dh1[rows, :] + dv).astype(BF16)
        avec[0:1, :] += jnp.sum(da1 * n, axis=0, keepdims=True)
        avec[1:2, :] += jnp.sum(da1, axis=0, keepdims=True)
        if j == 0:
            step(1, 0, 4, 5)
        elif j == 1:
            step(1, 1, 0, 1)
        elif j == 2:
            step(1, 1, 2, 3)
    done = pltpu.make_async_copy(tok_s, tok_o, out_sem.at[0])
    done.start()
    if not near:
        gq_o[...] = gq[...]
        small_o[0][...] = avec[...]
        done.wait()
        return
    avec[5:9, :] = gvec[5:9, :]
    gv[...] = pack_small(avec[...], gb1)
    start_all(small_s.first())
    step(1, 1, 4, 5)
    step(1, 2, 0, 1)
    wait_all(small_s.first())
    small_s.add()
    start_all(small_s.second())
    step(1, 2, 2, 3, 4, 5)
    step(0, 3, 0, 1, 2, 3, 4)
    step(1, 3, 0, 1, 2, 3, 4, 5)
    wait_all(small_s.second())
    t = small_s.result()
    for k, r in enumerate((0, 1, None, 5, 6, 7)):
        if r is None:
            small_o[k][...] = t[2:5, 0:16]
        else:
            small_o[k][...] = t[r:r + 1, 0:16]
    for r in range(8):
        small_o[6][0:1, 8 * r:8 * r + 8] = t[r:r + 1, 32:40]
    small_o[7][...] = t[0:1, 16:32]
    done.wait()


def backward(near, saved, wq, vecs, tok, da, dh1, gffn, gvec, gb1):
    kvx, qx, bias, a1, ao, iz, sp, spt = saved
    grid = (4, 2, 2, 2)
    vm = [VMEM(v.shape, v.dtype) for v in (kvx, qx, bias, a1, ao, iz, sp, spt, da, tok, dh1, wq, vecs)]
    scratch = vm + [VMEM((4, 160, 2048), BF16), VMEM((4, 2, 2048), F32), VMEM((4, 128, 2048), BF16), VMEM((EXT, 2 * D), F32),
                    VMEM((TOK, D), BF16), VMEM((2, 8, 16, D), BF16), VMEM((2, 8, 16, D), BF16), VMEM((8, 16, D), BF16),
                    VMEM((3, 16, D), BF16), VMEM((4, 16, D), BF16), VMEM((3,) + grid + (16, D), BF16), VMEM((16, D), F32), VMEM((TOK, D), BF16), VMEM((TOK, 2 * D), BF16),
                    SEM((13,)), SEM((1,)), SEM((6,)), SEM((6,))]
    if near:
        gffn = [g.reshape(grid + (g.shape[0] // 32, g.shape[1])) for g in gffn]
        shapes = [S((TOK, D), BF16), S((3, 16, D), F32)]
        shapes += [S((1, 16), F32), S((1, 16), F32), S((3, 16), F32), S((1, 16), F32), S((1, 16), F32), S((1, 16), F32), S((1, 64), F32), S((1, 16), F32)]
        shapes += [S(g.shape[4:], F32) for g in gffn]
        pieces = [(shape, BF16) for shape in FFN_SHAPES] + [((16, 256), BF16)] * 6
        scratch += [VMEM((4, 8, 8, 128), F32), [VMEM((4, 2, 2) + g.shape[4:], BF16) for g in gffn], SEM((3,)), SEM((11, 6)), SEM((11, 6)),
                    SEM((10,)), SEM((10,)), VMEM((7, 4, 8, 128), F32), VMEM((4, 8, 128), F32), VMEM((3, 8, 128), F32)]
        for shape, kind in pieces:
            scratch += scatter_bufs(shape, kind)
    else:
        gffn = gffn[0:3]
        shapes = [S((TOK, D), BF16), S((3,) + grid + (16, D), BF16), S((16, D), F32)]
    ordered = (da, ao, iz, sp, kvx, qx, bias, spt, a1, tok, dh1, wq, vecs)
    return pl.pallas_call(
        functools.partial(backward_kernel, near),
        out_shape=shapes,
        in_specs=[ANY] * 16 + [IN_VMEM] * 2,
        out_specs=[ANY] + [IN_VMEM] * (len(shapes) - 1),
        scratch_shapes=scratch,
        compiler_params=pltpu.CompilerParams(collective_id=1, has_side_effects=True, vmem_limit_bytes=62 << 20),
        name="backward",
    )(*ordered, *gffn, gvec, gb1)


def finish_kernel(n, *refs):
    for k in range(n):
        refs[n + k][...] = refs[k][...]


def finish(*values):
    n = len(values)
    return pl.pallas_call(
        functools.partial(finish_kernel, n),
        out_shape=[S(v.shape, v.dtype) for v in values],
        in_specs=[IN_VMEM] * n,
        out_specs=[IN_VMEM] * n,
        name="finish",
    )(*values)


BOTH = ("head", "span")


def shards(tokens, segment_ids, first_gain, first_shift, project_weight, project_bias, output_weight, output_bias,
           second_gain, second_shift, expand_weight, expand_bias, reduce_weight, reduce_bias, cotangent):
    tok, cot = tokens[0], cotangent[0]
    near = lax.axis_size("head") == 4 and lax.axis_size("span") == 8
    if near:
        vectors = (first_gain, first_shift, project_bias, output_bias, second_gain, second_shift, reduce_bias, expand_bias)
        vectors = [v if v.ndim == 2 else v[None] for v in vectors]
        *saved, wq, vecs, b1, wo, w1, w2 = forward(True, tok, segment_ids, project_weight, *vectors, output_weight, expand_weight, reduce_weight)
        wo, w1, w2 = wo.reshape(D, D), w1.reshape(D, FF), w2.reshape(FF, D)
    else:
        def full(v, axis=0):
            return lax.all_gather(v, BOTH, axis=axis, tiled=True)
        wq, wo, w1, w2 = full(project_weight, 1), full(output_weight), full(expand_weight), full(reduce_weight)
        rows = [full(first_gain), full(first_shift), *full(project_bias, 1), full(output_bias), full(second_gain), full(second_shift), full(reduce_bias)]
        vecs = jnp.pad(jnp.stack(rows), ((0, 7), (0, 0)))
        b1 = full(expand_bias)[None]
        saved = forward(False, tok, segment_ids, wq, vecs)
    ao = saved[4]
    out, dh1, da, *gffn, gvec, gb1 = middle(tok, ao, cot, wo, w1, w2, vecs, b1)
    dtok, gwq, *rest = backward(near, saved, wq, vecs, tok, da, dh1, gffn, gvec, gb1)
    if near:
        dtok, gwq, *rest = finish(dtok, gwq, *rest)
        small, (gwo, gw1, gw2) = rest[0:8], rest[8:11]
        small = [v if v.shape[0] == 3 else v.reshape(-1) for v in small]
    else:
        def part(v, axis=0):
            return lax.psum_scatter(v.astype(F32), BOTH, scatter_dimension=axis, tiled=True)
        vec, gwq = rest[0], gwq.reshape(3, D, D)
        gwq, gwo, gw1, gw2 = part(gwq, 1), part(gffn[0]), part(gffn[1]), part(gffn[2])
        small = (part(vec[0]), part(vec[1]), part(vec[2:5], 1), part(gvec[5]), part(gvec[6]), part(gvec[7]), part(gb1[0]), part(gvec[8]))
    return (out[None], dtok[None], small[0], small[1], gwq, small[2], gwo, small[3], small[4], small[5], gw1, small[6], gw2, small[7])


def solution(mesh):
    token, row, matrix = P("span", "head", None), P(BOTH), P(BOTH, None)
    three, bias = P(None, BOTH, None), P(None, BOTH)
    params = (row, row, three, bias, matrix, row, row, row, matrix, row, matrix, row)
    return jax.shard_map(shards, mesh=mesh, in_specs=(token, P("span", None)) + params + (token,),
                         out_specs=(token, token) + params, check_vma=False)
```

```python
import functools
import jax
import jax.numpy as jnp
from jax import lax
from jax.experimental import pallas as pl
from jax.experimental.pallas import tpu as pltpu
from jax.sharding import PartitionSpec as P

F32, BF16, I32 = jnp.float32, jnp.bfloat16, jnp.int32
MESH = pl.DeviceIdType.MESH
VMEM = pltpu.VMEM
NEG = -1e30
EPS = 1e-5
TOK = 1024
TILE = 256
D = 512
FF = 2048
EXT = 2384
SIZES = (1024, 512, 256, 128, 64, 32, 16)
EXT_AT = (0, 1056, 1600, 1888, 2048, 2144, 2208)
WIDE_AT = 2256
TRANS_B = (((1,), (1,)), ((), ()))
TRANS_A = (((0,), (0,)), ((), ()))


def mm(a, b):
    return jnp.dot(a, b, preferred_element_type=F32)


def mm_bt(a, b):
    return lax.dot_general(a, b, TRANS_B, preferred_element_type=F32)


def mm_at(a, b):
    return lax.dot_general(a, b, TRANS_A, preferred_element_type=F32)


def iota(shape, dim):
    return lax.broadcasted_iota(I32, shape, dim)


def split(v):
    high = v.astype(BF16)
    return high, (v - high.astype(F32)).astype(BF16)


def covers(t, c, block):
    if block == 0:
        return ((t & 255) >> 1) == c
    if block == 1:
        return ((t & 511) >> 2) == c
    if block == 2:
        return (t >> 3) == c
    level, start = mixed_levels(c)
    return (jnp.right_shift(t, level) == c - start) & (c < 124)


def mixed_levels(c):
    a, b, d, e = ((c >= edge).astype(I32) for edge in (64, 96, 112, 120))
    return 4 + a + b + d + e, 64 * a + 32 * b + 16 * d + 8 * e


def ones_where(cond):
    return jnp.where(cond, 1.0, 0.0).astype(BF16)


def identity(n):
    return ones_where(iota((n, n), 0) == iota((n, n), 1))


def fill_spread(spt):
    @pl.loop(0, TOK // TILE)
    def _(j):
        for block in range(4):
            t = iota((TILE, 128), 0) + j * TILE
            c = iota((TILE, 128), 1)
            spt[pl.ds(j * TILE, TILE), 128 * block:128 * block + 128] = ones_where(covers(t, c, block))


def fill_pool(sp):
    @pl.loop(0, TOK // TILE)
    def _(j):
        for block in range(4):
            t = iota((128, TILE), 1) + j * TILE
            c = iota((128, TILE), 0)
            sp[128 * block:128 * block + 128, pl.ds(pl.multiple_of(j * TILE, TILE), TILE)] = ones_where(covers(t, c, block))


TILES = TOK // TILE
BIAS_MIXED = 15 * 160
BIASES = BIAS_MIXED + 336


def tile_level(i):
    return 0 if i < 8 else 1 if i < 12 else 2 if i < 14 else 3


def tile_at(i):
    return 2048 if i == 15 else 128 * i + 32 * tile_level(i)


def tile_keys(i):
    return 336 if i == 15 else 160


def tile_times(i):
    if i < 15:
        return float(2 ** tile_level(i))
    level, _unused = mixed_levels(iota((1, 128), 1))
    return (1 << level).astype(F32)


INNER = (1, 2, 3, 4, 5, 6, 9, 10)
OUTER = (0, 7, 8, 11, 12, 13, 14, 15)


def labels_of(total, squares, times):
    return jnp.where(times * squares == total * total, total / times, 0.0)


def head_masks(rows):
    lane = iota((rows, 128), 1)
    return ones_where(lane < 64), ones_where(lane >= 64)


def by_head(x, masks):
    return jnp.concatenate([x * masks[0], x * masks[1]], axis=0)


def own_blocks(x):
    return jnp.concatenate([x[0:64, 0:128], x[64:128, 128:256]], axis=0)


def twice(x):
    return jnp.concatenate([x, x], axis=1)


def two_rows(a, b):
    row = iota((16, a.shape[1]), 0)
    return jnp.where(row == 0, a, jnp.where(row == 1, b, 0.0))


def lanes_of(g, base=0):
    return pl.ds(pl.multiple_of(base + g * 128, 128), 128)


def coarse_cols(ref, base, j):
    return jnp.concatenate([ref[:, base + 128 * j:base + 128 * j + 128],
                            ref[:, base + 512 + 128 * (j // 2):base + 640 + 128 * (j // 2)],
                            ref[:, base + 768:base + 1024]], axis=1)


def coarse_blocks():
    return ([(128 * j, 0, 256 * j, 256) for j in range(4)] + [(512 + 128 * j, 1, 512 * j, 512) for j in range(2)]
            + [(768, 2, 0, 1024), (896, 3, 0, 1024)])


def near_rows(side):
    o, i = iota((96, 128), 0), iota((96, 128), 1)
    level = (o >> 4) + 1
    block = i >> 4
    fine = jnp.maximum(block - 1, 0)
    value_out, value_in = (o >> 3) & 1, jnp.where(block < 2, block, (i >> 3) & 1)
    width, size = jnp.left_shift(1, fine), jnp.left_shift(1, level)
    if side == 0:
        start = ((o & 7) - 8) * size
        at = jnp.where(block < 2, (i & 15) - 16, (i & 7) - 16) * width
    else:
        start = (o & 7) * size
        at = jnp.where(block < 2, i & 15, (i & 7) + 8) * width
    inside = (value_out == value_in) & (at >= start) & (at + width <= start + size)
    share = jnp.where(value_out == 1, 1.0, width.astype(F32) / size.astype(F32))
    return jnp.where(inside, share, 0.0).astype(BF16)


def wide_rows(value):
    r, i = iota((128, 128), 0), iota((128, 128), 1)
    k, j = r & 15, (i & 15) - 8 * value
    own = ((r >> 4) == (i >> 4)) & (j >= 0) & (j < 8)
    fine, rough = own & (k < 8) & (j == k), own & (k >= 8) & (k < 12) & ((j >> 1) == k - 8)
    return jnp.where(fine, 1.0, jnp.where(rough, 1.0 if value else 0.5, 0.0)).astype(BF16)


def far_and_near(side, far, near):
    return jnp.concatenate([far, near] if side == 0 else [near, far], axis=0)


def border(side, l):
    return EXT_AT[l] + (16 + SIZES[l] if side else 0)


def own_border(side, l):
    return EXT_AT[l] + (SIZES[l] if side else 16)


def pick_far(side, rows):
    return rows[0:8] if side else rows[8:16]


def column_of(row, n):
    spread = jnp.where(iota((n, n), 0) == iota((n, n), 1), jnp.broadcast_to(row, (n, n)), 0.0)
    return jnp.broadcast_to(jnp.sum(spread, axis=1, keepdims=True), (n, 128)).astype(BF16)


def where_am_i():
    h = lax.axis_index("head")
    s = lax.axis_index("span")
    return h, s, s // 4, (s // 2) % 2, s % 2


class Peers:
    def __init__(self, near):
        h, s = lax.axis_index("head"), lax.axis_index("span")
        odd = s % 2
        self.place = odd * 4 + h
        self.odd = odd
        self.h = h
        other = s + 1 - 2 * odd
        self.z_index = [lax.rem(h + d, 4) for d in (1, 2, 3)]
        self.zs = [{"head": z} for z in self.z_index]
        self.core = {"span": other}
        opposite = {"head": 3 - h, "span": other}
        step = 1 - 2 * odd
        self.right = {"head": lax.rem(h + 1, 4), "span": s + step * ((h + 1) // 4)}
        self.left = {"head": lax.rem(h + 3, 4), "span": s + step * (1 - (h + 3) // 4)}
        self.greeted = self.zs + [self.core, opposite]
        if near:
            y, x = s // 4, (s // 2) % 2
            self.y, self.x, self.c = y, x, odd
            self.s = s
            self.px = {"span": y * 4 + (1 - x) * 2 + odd}
            self.py = {"span": (1 - y) * 4 + x * 2 + odd}
            self.s_index = [lax.rem(s + d, 8) for d in range(1, 8)]
            self.spans = [{"span": o} for o in self.s_index]
            self.greeted = self.zs + self.spans + [opposite]


def greet(devices):
    barrier = pltpu.get_barrier_semaphore()
    for d in devices:
        pl.semaphore_signal(barrier, inc=1, device_id=d, device_id_type=MESH)
    pl.semaphore_wait(barrier, len(devices))


def rcopy(src, dst, send, recv, device):
    return pltpu.make_async_remote_copy(src_ref=src, dst_ref=dst, send_sem=send, recv_sem=recv,
                                        device_id=device, device_id_type=MESH)


class Gather:
    def __init__(self, me, shard, full, swap, local, send, recv):
        self.me, self.shard, self.full, self.swap, self.local, self.send, self.recv = me, shard, full, swap, local, send, recv

    def own(self):
        m = self.me
        return pltpu.make_async_copy(self.shard, self.full(m.h, m.y, m.x, m.c), self.local)

    def hop(self, k):
        m, a = self.me, slice(None)
        if k < 3:
            return rcopy(self.shard, self.full(m.h, m.y, m.x, m.c), self.send.at[k], self.recv.at[k], m.zs[k])
        if k == 3:
            ref, dev = self.full(a, m.y, m.x, m.c), m.py if self.swap else m.px
        elif k == 4:
            ref, dev = (self.full(a, a, m.x, m.c), m.px) if self.swap else (self.full(a, m.y, a, m.c), m.py)
        else:
            ref, dev = self.full(a, a, a, m.c), m.core
        return rcopy(ref, ref, self.send.at[k], self.recv.at[k], dev)

    def start(self, stage):
        if stage == 0:
            self.own().start()
            for k in range(3):
                self.hop(k).start()
        else:
            self.hop(2 + stage).start()

    def wait(self, stage):
        if stage == 0:
            self.own().wait()
            for k in range(3):
                self.hop(k).wait()
        else:
            self.hop(2 + stage).wait()


class Scatter:
    def __init__(self, me, grad, mine, swap, bufs, send, recv):
        self.me, self.grad, self.mine, self.swap, self.bufs, self.send, self.recv = me, grad, mine, swap, bufs, send, recv

    def hops(self, stage):
        m, s, r = self.me, self.send, self.recv
        r1, r2, r3, r4 = self.bufs
        if stage == 0:
            return [rcopy(self.grad(1 - m.c), r1, s.at[0], r.at[0], m.core)]
        if stage == 1:
            src, dev = (r1.at[:, 1 - m.y], m.py) if self.swap else (r1.at[:, :, 1 - m.x], m.px)
            return [rcopy(src, r2, s.at[1], r.at[1], dev)]
        if stage == 2:
            src, dev = (r2.at[:, 1 - m.x], m.px) if self.swap else (r2.at[:, 1 - m.y], m.py)
            return [rcopy(src, r3, s.at[2], r.at[2], dev)]
        return [rcopy(r3.at[m.z_index[k]], r4.at[k], s.at[3 + k], r.at[3 + k], m.zs[k]) for k in range(3)]

    def start(self, stage):
        for cp in self.hops(stage):
            cp.start()

    def wait(self, stage):
        for cp in self.hops(stage):
            cp.wait()

    def add(self, stage):
        m = self.me
        r1, r2, r3, r4 = self.bufs

        def into(dst, key, other):
            dst[key] = (dst[key].astype(F32) + other.astype(F32)).astype(dst.dtype)
        if stage == 0:
            @pl.loop(0, 4)
            def _(hh):
                for yy in range(2):
                    for xx in range(2):
                        into(r1, (hh, yy, xx), self.mine(hh, yy, xx))
        elif stage == 1:
            @pl.loop(0, 4)
            def _(hh):
                for v in range(2):
                    into(r2, (hh, v), r1[hh, m.y, v] if self.swap else r1[hh, v, m.x])
        else:
            @pl.loop(0, 4)
            def _(hh):
                into(r3, (hh,), r2[hh, m.x if self.swap else m.y])

    def result(self):
        r1, r2, r3, r4 = self.bufs
        acc = r3[self.me.h].astype(F32)
        for k in range(3):
            acc = acc + r4[k].astype(F32)
        return acc


class SmallGather:
    def __init__(self, me, tile, full, local, send, recv):
        self.me, self.tile, self.full, self.local, self.send, self.recv = me, tile, full, local, send, recv

    def first(self):
        dst = self.full.at[self.me.h, self.me.s]
        return [rcopy(self.tile, dst, self.send.at[k], self.recv.at[k], self.me.zs[k]) for k in range(3)]

    def second(self):
        ref = self.full.at[:, self.me.s]
        return [rcopy(ref, ref, self.send.at[3 + k], self.recv.at[3 + k], self.me.spans[k]) for k in range(7)]

    def own(self):
        return pltpu.make_async_copy(self.tile, self.full.at[self.me.h, self.me.s], self.local)


class SmallScatter:
    def __init__(self, me, grad, got, total, got_z, send, recv):
        self.me, self.grad, self.got, self.total, self.got_z, self.send, self.recv = me, grad, got, total, got_z, send, recv

    def first(self):
        m = self.me
        return [rcopy(self.grad.at[:, m.s_index[k]], self.got.at[k], self.send.at[k], self.recv.at[k], m.spans[k]) for k in range(7)]

    def second(self):
        m = self.me
        return [rcopy(self.total.at[m.z_index[k]], self.got_z.at[k], self.send.at[7 + k], self.recv.at[7 + k], m.zs[k]) for k in range(3)]

    def add(self):
        v = self.grad[:, self.me.s]
        for k in range(7):
            v = v + self.got[k]
        self.total[...] = v

    def result(self):
        v = self.total[self.me.h]
        for k in range(3):
            v = v + self.got_z[k]
        return v


def start_all(copies):
    for cp in copies:
        cp.start()


def wait_all(copies):
    for cp in copies:
        cp.wait()


FFN_SHAPES = ((16, D), (16, 768), (16, 1280), (32, D), (32, D))


def ffn_index(k, whole):
    half = (k - 1) % 2
    if k == 0:
        return 0, ()
    if k < 3:
        return 1, (slice(None), whole(768 * half, 768 + 512 * half))
    return 2, (whole(32 * half, 32),)


def ffn_view(refs, k, index):
    which, tail = ffn_index(k, pl.ds)
    return refs[which].at[index + tail]


def ffn_values(refs, k, index):
    which, tail = ffn_index(k, lambda at, n: slice(at, at + n))
    return refs[which][index + tail]


def scatter_bufs(shape, dtype):
    return [VMEM((4, 2, 2) + shape, dtype), VMEM((4, 2) + shape, dtype), VMEM((4,) + shape, dtype), VMEM((3,) + shape, dtype)]


def split3(v):
    high, rest = split(v)
    mid = rest
    low = (v - high.astype(F32) - mid.astype(F32)).astype(BF16)
    return high, mid, low


def mm_exact(v, ones):
    a, b, c = split3(v)
    return mm(a, ones) + mm(b, ones) + mm(c, ones)


def small_rows(vt, g1, s1, pb, ob, g2, s2, rb, eb):
    vt[...] = jnp.zeros_like(vt)
    for r, ref in enumerate((g1, s1, None, None, None, ob, g2, s2)):
        vt[r:r + 1, 0:16] = pb[r - 2:r - 1, :] if ref is None else ref[...]
    vt[0:1, 16:32] = rb[...]
    for r in range(8):
        vt[r:r + 1, 32:40] = eb[0:1, 8 * r:8 * r + 8]


def unpack_small(gathered, vecs, b1):
    v = gathered[...].reshape(256, 128)
    row, n = iota((256, D), 0), iota((256, D), 1)
    lane, col = iota((128, D), 0), iota((128, D), 1)
    mine = (row >> 3) == (n >> 4)
    for half in range(2):
        x = mm_exact(v, ones_where(lane == (col & 15) + 16 * half))
        vecs[8 * half:8 * half + 8, :] = jnp.sum(jnp.where(mine, x, 0.0).reshape(32, 8, D), axis=0)
    x = mm_exact(v, ones_where(lane == (col & 7) + 32))
    for q in range(4):
        ok = ((row >> 3) == ((n + 512 * q) >> 6)) & ((row & 7) == ((n >> 3) & 7))
        b1[0:1, D * q:D * q + D] = jnp.sum(jnp.where(ok, x, 0.0), axis=0, keepdims=True)


def fill_bias(bias, labk, labq, place, tiles):
    def matching(i):
        kl = labk[tile_at(i):tile_at(i) + tile_keys(i), :].astype(F32)
        return (kl == labq[i:i + 1, :]) & (kl != 0.0)

    r, c = iota((160, 128), 0), iota((160, 128), 1)
    near = jnp.abs((r >> 4) - 1 - (c >> 4)) <= 1
    far = near & (jnp.abs((r >> 3) - 2 - (c >> 3)) >= 2)
    same = (r - 16) == c
    for i in tiles:
        if i == 15:
            continue
        ok = matching(i) & near | same if i < 8 else matching(i) & far
        bias[160 * i:160 * i + 160, :] = jnp.where(ok, 0.0, NEG)
    if 15 not in tiles:
        return
    r, c = iota((336, 128), 0), iota((336, 128), 1)
    inner = (r >= 96).astype(I32) + (r >= 160).astype(I32)
    start = jnp.where(inner == 0, 0, jnp.where(inner == 1, 96, 160))
    e, k = (r - 208) >> 4, (r - 208) & 15
    upper = (k >= 8).astype(I32)
    level_k = jnp.where(r < 208, 4 + inner, 7 + upper)
    pos_k = jnp.where(r < 208, r - start - 16, jnp.where(k < 8, e * 8 + k, e * 4 + k - 8))
    level_q, start_q = mixed_levels(c)
    pos_q = c - start_q + jnp.where(level_q == 7, place * 8, jnp.where(level_q == 8, place * 4, 0))
    shape = (level_k == level_q) & (jnp.abs((pos_k >> 4) - (pos_q >> 4)) <= 1) & (jnp.abs((pos_k >> 3) - (pos_q >> 3)) >= 2)
    bias[BIAS_MIXED:BIASES, :] = jnp.where(matching(15) & shape, 0.0, NEG)


def bias_of(bias, i):
    return twice(bias[160 * i:160 * i + 160, :] if i < 15 else bias[BIAS_MIXED:BIASES, :])


def forward_kernel(near, *refs):
    refs = list(refs)

    def take(n):
        out = refs[:n]
        del refs[:n]
        return out
    tok, seg = take(2)
    if near:
        wq_in, = take(1)
        small = take(8)
        ffn_in = take(3)
    else:
        wq, vecs = take(2)
    kvx_o, qx_o, bias_o, a1_o, ao_o, iz_o, sp_o, spt_o = take(8)
    if near:
        wq_o, vecs_o, b1_o = take(3)
        ffn_o = take(3)
    kvx, qx, bias, a1, ao, iz, sp, spt, xh, labq, n0, nc, z0, labk, seg2, msg, got, wbuf, out_sem, e_send, e_recv = take(21)
    if near:
        wq, vecs, b1, vt, vg, local, send, recv, send_v, recv_v = take(10)
    me = Peers(near)
    place = me.place
    outs = []

    def emit(src, dst):
        cp = pltpu.make_async_copy(src, dst, out_sem.at[len(outs)])
        cp.start()
        outs.append(cp)

    got[...] = jnp.zeros_like(got)
    if near:
        small_rows(vt, *small)
    greet(me.greeted)
    ids_core = rcopy(seg, seg2, e_send.at[6], e_recv.at[6], me.core)
    ids_core.start()
    if near:
        small_g = SmallGather(me, vt, vg, local.at[15], send_v, recv_v)
        small_g.own().start()
        start_all(small_g.first())
        first = []
        for k, (which, lanes) in enumerate((w, pl.ds(lo, 256)) for w in (pl.ds(1, 2), pl.ds(0, 1)) for lo in (0, 256)):
            first.append(Gather(me, wq_in.at[which, :, lanes], lambda h, y, x, c, which=which, lanes=lanes: wq.at[which, h, y, x, c, :, lanes],
                                k % 2 == 1, local.at[k], send.at[k], recv.at[k]))
        later = [Gather(me, ffn_view(ffn_in, k, ()), lambda h, y, x, c, k=k: ffn_view(ffn_o, k, (h, y, x, c)), k in (2, 4),
                        local.at[4 + k], send.at[4 + k], recv.at[4 + k]) for k in range(5)]

    def step(group, stage, *pieces):
        if not near:
            return
        for k in pieces:
            a = (first if group == 0 else later)[k]
            if stage >= 0:
                a.wait(stage)
            if stage < 3:
                a.start(stage + 1)

    step(0, -1, 0, 1, 2, 3)
    fill_pool(sp)
    fill_spread(spt)
    emit(sp, sp_o)
    emit(spt, spt_o)
    if near:
        small_g.own().wait()
        wait_all(small_g.first())
        start_all(small_g.second())
    step(0, 0, 0, 1, 2, 3)
    step(1, -1, 0, 1, 2, 3, 4)
    ids_core.wait()

    def chunk(ref, k):
        return ref[:, pl.ds(pl.multiple_of(TOK * k, TOK), TOK)].astype(F32)
    odd = me.odd.astype(F32)
    ids = chunk(seg, me.h)
    ids_left = jnp.where(me.h > 0, chunk(seg, lax.rem(me.h + 3, 4)), chunk(seg2, 3) * odd)
    ids_right = jnp.where(me.h < 3, chunk(seg, lax.rem(me.h + 1, 4)), chunk(seg2, 0) * (1.0 - odd))
    ids_b = jnp.broadcast_to(ids, (128, TOK)).astype(BF16)
    sq_b = jnp.broadcast_to(ids * ids, (128, TOK)).astype(BF16)
    eye = identity(TILE)
    for j in range(TILES):
        labk[16 + TILE * j:16 + TILE * j + TILE, :] = mm_bt(eye, ids_b[:, TILE * j:TILE * j + TILE]).astype(BF16)
    for i in range(8):
        labq[i:i + 1, :] = ids[:, 128 * i:128 * i + 128]
    row, t = iota((128, TOK), 0), iota((128, TOK), 1)
    level, level_row = row >> 4, iota((1, 128), 1) >> 4
    for side, v in ((0, ids_left), (1, ids_right)):
        base = jnp.right_shift(TOK, level) - 16 if side == 0 else 0
        sel = ones_where(jnp.right_shift(t, level) == base + (row & 15))
        x = mm_bt(two_rows(v, v * v).astype(BF16), sel)
        col = column_of(labels_of(x[0:1], x[1:2], jnp.left_shift(1, level_row).astype(F32)), 128)
        for l in range(7):
            labk[border(side, l):border(side, l) + 16, :] = col[16 * l:16 * l + 16]
    even_ids = [jnp.where(me.odd == 0, chunk(seg, k), chunk(seg2, k)) for k in range(4)]
    odd_ids = [jnp.where(me.odd == 0, chunk(seg2, k), chunk(seg, k)) for k in range(4)]
    all_ids = jnp.concatenate(even_ids + odd_ids, axis=0)
    x = mm_bt(jnp.concatenate([all_ids, all_ids * all_ids], axis=0).astype(BF16), sp[496:512, :])
    lab = labels_of(x[0:8], x[8:16], jnp.where(iota((8, 16), 1) < 8, 128.0, 256.0))
    lab = jnp.broadcast_to(lab[:, None, :], (8, 16, 16)).reshape(128, 16)
    lab = jnp.sum(jnp.where((iota((128, 16), 0) & 15) == iota((128, 16), 1), lab, 0.0), axis=1, keepdims=True)
    labk[WIDE_AT:EXT, :] = jnp.broadcast_to(lab, (128, 128)).astype(BF16)

    def put_coarse(dst, b, value, cols):
        at, block, _t, _n = coarse_blocks()[b]
        if block < 3:
            level = block + 1
            row = EXT_AT[level] + 16 + at - (0, 512, 768)[block]
            dst[row:row + 128, cols] = value
        else:
            for level, a, n in ((4, 0, 64), (5, 64, 32), (6, 96, 16)):
                dst[EXT_AT[level] + 16:EXT_AT[level] + 16 + n, cols] = value[a:a + n]

    for b, (at, block, t, n) in enumerate(coarse_blocks()):
        s = sp[128 * block:128 * block + 128, t:t + n]
        rows_level, _unused = mixed_levels(iota((128, 128), 0))
        cols_level, _unused = mixed_levels(iota((8, 128), 1))
        times_r = (1 << rows_level).astype(F32) if block == 3 else float(2 ** (block + 1))
        times_c = (1 << cols_level).astype(F32) if block == 3 else float(2 ** (block + 1))
        lab = labels_of(mm_bt(s, ids_b[:, t:t + n]), mm_bt(s, sq_b[:, t:t + n]), times_r)
        put_coarse(labk, b, lab.astype(BF16), slice(0, 128))
        row = labels_of(mm_bt(ids_b[0:8, t:t + n], s), mm_bt(sq_b[0:8, t:t + n], s), times_c)
        labq[8 + b:9 + b, :] = row[0:1, :]
    step(0, 1, 0, 1, 2, 3)
    fill_bias(bias, labk, labq, place, range(16))
    emit(bias, bias_o)
    for j in range(TILES):
        v = tok[TILE * j:TILE * j + TILE, :].astype(F32)
        center = v - jnp.mean(v, axis=-1, keepdims=True)
        xh[TILE * j:TILE * j + TILE, :] = center * lax.rsqrt(jnp.mean(center * center, axis=-1, keepdims=True) + EPS)
    step(0, 2, 0, 1, 2, 3)
    step(1, 0, 0, 1, 2, 3, 4)
    if near:
        wait_all(small_g.second())
        unpack_small(vg, vecs, b1)
        emit(vecs, vecs_o)
        emit(b1, b1_o)
    for j in range(TILES):
        rows = slice(TILE * j, TILE * j + TILE)
        a1[rows, :] = (xh[rows, :] * vecs[0:1, :] + vecs[1:2, :]).astype(BF16)
    emit(a1, a1_o)
    step(0, 3, 0, 1)

    def project(c):
        w = wq[c].reshape(D, D)
        for j in range(TILES):
            r = (mm(a1[TILE * j:TILE * j + TILE, :], w) + vecs[2 + c:3 + c, :]).astype(BF16)
            if c == 0:
                qx[TILE * j:TILE * j + TILE, :] = r * jnp.array(0.125, BF16)
            else:
                kvx[16 + TILE * j:16 + TILE * j + TILE, D * (c - 1):D * c] = r

    def pool_parts(block, t, n):
        if block == 3:
            level, _unused = mixed_levels(iota((128, D), 0))
            shrink = 1.0 / (1 << level).astype(F32)
        else:
            shrink = 0.5 ** (block + 1)
        return sp[128 * block:128 * block + 128, t:t + n], shrink
    project(1)
    project(2)
    step(1, 1, 0, 2)
    wide_z = [rcopy(wbuf.at[place], wbuf.at[place], e_send.at[2 + k], e_recv.at[2 + k], me.zs[k]) for k in range(3)]
    for b, (at, block, t, n) in reversed(list(enumerate(coarse_blocks()))):
        pool, shrink = pool_parts(block, t, n)
        kc, vc = mm(pool, kvx[16 + t:16 + t + n, 0:D]) * shrink, mm(pool, kvx[16 + t:16 + t + n, D:2 * D])
        put_coarse(kvx, b, kc.astype(BF16), slice(0, D))
        put_coarse(kvx, b, vc.astype(BF16), slice(D, 2 * D))
        if block == 3:
            wbuf[place] = jnp.concatenate([kc[112:120], vc[112:120]], axis=0).astype(BF16)
            start_all(wide_z)
    step(1, 1, 1)
    for side in range(2):
        for l in range(7):
            at = own_border(side, l)
            k16, v16 = kvx[at:at + 16, 0:D], kvx[at:at + 16, D:2 * D]
            if l == 0:
                msg[side, 0], msg[side, 1] = k16, v16
            else:
                far = [pick_far(side, v.astype(F32)) for v in (k16, v16)]
                msg[side, l + 1] = jnp.concatenate(far, axis=0).astype(BF16)
    to_right = rcopy(msg.at[1], got.at[0], e_send.at[0], e_recv.at[0], me.right)
    to_left = rcopy(msg.at[0], got.at[1], e_send.at[1], e_recv.at[1], me.left)
    four = wbuf.at[pl.ds(4 * me.odd, 4)]
    wide_core = rcopy(four, four, e_send.at[5], e_recv.at[5], me.core)
    not_last, not_first = place < 7, place > 0

    @pl.when(not_last)
    def _():
        to_right.start()

    @pl.when(not_first)
    def _():
        to_left.start()
    step(1, 1, 4)
    step(0, 3, 2, 3)
    project(0)
    for at, block, t, n in coarse_blocks():
        pool, shrink = pool_parts(block, t, n)
        qx[1024 + at:1024 + at + 128, :] = (mm(pool, qx[t:t + n, :]) * shrink).astype(BF16)
    emit(qx, qx_o)
    if near:
        emit(wq, wq_o)
    step(1, 1, 3)
    masks = head_masks(128)

    def tile(g, i):
        keys = slice(tile_at(i), tile_at(i) + tile_keys(i))
        kw, vw = kvx[keys, lanes_of(g)], kvx[keys, lanes_of(g, D)]
        q = by_head(qx[128 * i:128 * i + 128, lanes_of(g)], masks)
        e = jnp.exp(mm_bt(kw, q) + bias_of(bias, i))
        times = tile_times(i)
        z = jnp.sum(e, axis=0, keepdims=True)
        z0_, z1_ = z[:, 0:128] * times, z[:, 128:256] * times
        n = own_blocks(mm_at(vw, e.astype(BF16)))
        if i < 8:
            cols = slice(128 * i, 128 * i + 128)
            n0[g, :, cols] = n
            z0[g, 0:1, cols] = z0_
            z0[g, 1:2, cols] = z1_
        else:
            cols = slice(128 * i - 1024, 128 * i - 896)
            high, low = split(two_rows(z0_, z1_))
            nc[g, :, cols] = jnp.concatenate([n.astype(BF16), high, low], axis=0)

    @pl.loop(0, 4)
    def _(g):
        for k in range(4):
            @pl.when(g == k)
            def _():
                if k == 1:
                    wait_all(wide_z)
                    wide_core.start()
        for i in INNER:
            tile(g, i)

    wide_core.wait()
    w = wbuf[...].reshape(128, D)
    kvx[WIDE_AT:EXT, 0:D] = mm(wide_rows(0), w).astype(BF16)
    kvx[WIDE_AT:EXT, D:2 * D] = mm(wide_rows(1), w).astype(BF16)

    @pl.when(not_last)
    def _():
        to_right.wait_send()
        to_left.wait_recv()

    @pl.when(not_first)
    def _():
        to_left.wait_send()
        to_right.wait_recv()
    for side in range(2):
        m = got[side].reshape(128, D)
        closer = mm(near_rows(side), m)
        m = m.astype(F32)
        for l in range(7):
            at = border(side, l)
            if l == 0:
                k16, v16 = m[0:16], m[16:32]
            else:
                a, b = 16 * (l + 1), 16 * (l - 1)
                k16 = far_and_near(side, m[a:a + 8], closer[b:b + 8])
                v16 = far_and_near(side, m[a + 8:a + 16], closer[b + 8:b + 16])
            kvx[at:at + 16, 0:D] = k16.astype(BF16)
            kvx[at:at + 16, D:2 * D] = v16.astype(BF16)
    emit(kvx, kvx_o)

    @pl.loop(0, 4)
    def _(g):
        for k in range(4):
            @pl.when(g == k)
            def _():
                step(1, 2, *((0, 2), (1,), (), (4,))[k])
        for i in OUTER:
            tile(g, i)
        c_ref = nc.at[g]
        for j in range(TILES):
            cols = slice(TILE * j, TILE * j + TILE)
            r = mm(coarse_cols(c_ref, 0, j), sp[:, cols])
            n = n0[g, :, cols] + r[0:128]
            i0 = 1.0 / (z0[g, 0:1, cols] + r[128:129] + r[144:145])
            i1 = 1.0 / (z0[g, 1:2, cols] + r[129:130] + r[145:146])
            iz[g, 0:1, cols] = i0
            iz[g, 1:2, cols] = i1
            ao[pl.ds(pl.multiple_of(g * 128, 128), 64), cols] = (n[0:64] * i0).astype(BF16)
            ao[pl.ds(pl.multiple_of(g * 128 + 64, 64), 64), cols] = (n[64:128] * i1).astype(BF16)
    emit(ao, ao_o)
    emit(iz, iz_o)
    step(1, 2, 3)
    step(1, 3, 0, 1, 2, 3, 4)
    wait_all(outs)


ANY = pl.BlockSpec(memory_space=pl.ANY)
IN_VMEM = pl.BlockSpec(memory_space=pltpu.VMEM)
S = jax.ShapeDtypeStruct
SEM = pltpu.SemaphoreType.DMA


def forward(near, tok, seg, *params):
    grid = (4, 2, 2, 2)
    shapes = [S((EXT, 2 * D), BF16), S((2048, D), BF16), S((BIASES, 128), F32), S((TOK, D), BF16), S((D, TOK), BF16),
              S((4, 2, TOK), F32), S((512, TOK), BF16), S((TOK, 512), BF16)]
    scratch = [VMEM(s.shape, s.dtype) for s in shapes] + [
        VMEM((TOK, D), F32), VMEM((16, 128), F32), VMEM((4, 128, TOK), F32), VMEM((4, 160, TOK), BF16), VMEM((4, 2, TOK), F32),
        VMEM((EXT, 128), BF16), VMEM(seg.shape, I32), VMEM((2, 8, 16, D), BF16), VMEM((2, 8, 16, D), BF16), VMEM((8, 16, D), BF16),
        SEM((16,)), SEM((7,)), SEM((7,))]
    if near:
        shapes += [S((3,) + grid + (16, D), BF16), S((16, D), F32), S((1, FF), F32)]
        shapes += [S(grid + a.shape, a.dtype) for a in params[9:]]
        scratch += [VMEM((3,) + grid + (16, D), BF16), VMEM((16, D), F32), VMEM((1, FF), F32), VMEM((8, 128), F32),
                    VMEM((4, 8, 8, 128), F32), SEM((16,)), SEM((9, 6)), SEM((9, 6)), SEM((10,)), SEM((10,))]
        specs = [IN_VMEM] * 9 + [ANY] * 3
    else:
        specs = [IN_VMEM] * 2
    return pl.pallas_call(
        functools.partial(forward_kernel, near),
        out_shape=shapes,
        in_specs=[IN_VMEM, IN_VMEM] + specs,
        out_specs=[ANY] * len(shapes),
        scratch_shapes=scratch,
        compiler_params=pltpu.CompilerParams(collective_id=0, has_side_effects=True, vmem_limit_bytes=60 << 20),
        name="forward",
    )(tok, seg, *params)


C0 = 0.7978845608028654
C1 = 0.044715


def middle_kernel(tok, ao, cot, wo, w1, w2, vecs, b1, out, dh1_out, da_out, gwo, gw1, gw2, gvec, gb1,
                  awo, aw1, aw2, avec, ab1):
    j = pl.program_id(0)

    @pl.when(j == 0)
    def _():
        awo[...] = jnp.zeros_like(awo)
        aw1[...] = jnp.zeros_like(aw1)
        aw2[...] = jnp.zeros_like(aw2)
        avec[...] = jnp.zeros_like(avec)
        ab1[...] = jnp.zeros_like(ab1)
    mixed = ao[...]
    h1 = tok[...].astype(F32) + mm_at(mixed, wo[...]) + vecs[5:6, :]
    center = h1 - jnp.mean(h1, axis=-1, keepdims=True)
    inverse = lax.rsqrt(jnp.mean(center * center, axis=-1, keepdims=True) + EPS)
    xh = center * inverse
    gain = vecs[6:7, :]
    a2 = (xh * gain + vecs[7:8, :]).astype(BF16)
    dy = cot[...]
    y = h1 + vecs[8:9, :]
    da2 = jnp.zeros((1024, D), F32)
    for k in range(FF // 1024):
        cols = slice(1024 * k, 1024 * k + 1024)
        u = mm(a2, w1[:, cols]) + b1[:, cols]
        u2 = u * u
        th = jnp.tanh(u * (C0 + (C0 * C1) * u2))
        half = 0.5 * (1.0 + th)
        g = (u * half).astype(BF16)
        slope = half + 0.5 * u * (1.0 - th * th) * (C0 + (3.0 * C0 * C1) * u2)
        y = y + mm(g, w2[cols, :])
        du = (mm_bt(dy, w2[cols, :]) * slope).astype(BF16)
        aw2[cols, :] += mm_at(g, dy)
        aw1[:, cols] += mm_at(a2, du)
        ab1[:, cols] += jnp.sum(du.astype(F32), axis=0, keepdims=True)
        da2 = da2 + mm_bt(du, w1[:, cols])
    out[...] = y.astype(BF16)
    dyf = dy.astype(F32)
    e = da2 * gain
    dh1 = dyf + inverse * (e - jnp.mean(e, axis=-1, keepdims=True) - xh * jnp.mean(e * xh, axis=-1, keepdims=True))
    dh1_out[...] = dh1
    db = dh1.astype(BF16)
    awo[...] += mm(mixed, db)
    da_out[...] = mm_bt(wo[...], db).astype(BF16)
    avec[5:6, :] += jnp.sum(db.astype(F32), axis=0, keepdims=True)
    avec[6:7, :] += jnp.sum(da2 * xh, axis=0, keepdims=True)
    avec[7:8, :] += jnp.sum(da2, axis=0, keepdims=True)
    avec[8:9, :] += jnp.sum(dyf, axis=0, keepdims=True)

    @pl.when(j == TOK // 1024 - 1)
    def _():
        gwo[...] = awo[...].astype(BF16)
        gw1[...] = aw1[...].astype(BF16)
        gw2[...] = aw2[...].astype(BF16)
        gvec[...] = avec[...]
        gb1[...] = ab1[...]


def whole(shape):
    return pl.BlockSpec(shape, lambda j: (0,) * len(shape), pipeline_mode=pl.Buffered(1))


def middle(tok, ao, cot, wo, w1, w2, vecs, b1):
    tile = pl.BlockSpec((1024, D), lambda j: (j, 0))
    flat = pl.BlockSpec((D, 1024), lambda j: (0, j))
    return pl.pallas_call(
        middle_kernel,
        grid=(TOK // 1024,),
        out_shape=[S((TOK, D), BF16), S((TOK, D), F32), S((D, TOK), BF16), S((D, D), BF16), S((D, FF), BF16), S((FF, D), BF16),
                   S((16, D), F32), S((1, FF), F32)],
        in_specs=[tile, flat, tile, whole((D, D)), whole((D, FF)), whole((FF, D)), whole((16, D)), whole((1, FF))],
        out_specs=[tile, tile, flat, whole((D, D)), whole((D, FF)), whole((FF, D)), whole((16, D)), whole((1, FF))],
        scratch_shapes=[VMEM((D, D), F32), VMEM((D, FF), F32), VMEM((FF, D), F32), VMEM((16, D), F32), VMEM((1, FF), F32)],
        compiler_params=pltpu.CompilerParams(dimension_semantics=("arbitrary",), vmem_limit_bytes=60 << 20),
        name="middle",
    )(tok, ao, cot, wo, w1, w2, vecs, b1)


def pack_small(rows, b1):
    row, n = iota((256, D), 0), iota((256, D), 1)
    lane, col = iota((128, D), 0), iota((128, D), 1)
    mine = (row >> 3) == (n >> 4)

    def moved(v, ok, ones):
        total = None
        for part in split3(jnp.where(ok, v, 0.0)):
            r = mm_bt(part, ones)
            total = r if total is None else total + r
        return total
    eight = jnp.broadcast_to(rows[0:8][None], (32, 8, D)).reshape(256, D)
    out = moved(eight, mine, ones_where(lane == (col & 15)))
    out = out + moved(jnp.broadcast_to(rows[8:9], (256, D)), mine & ((row & 7) == 0), ones_where(lane == (col & 15) + 16))
    last = ones_where(lane == (col & 7) + 32)
    for q in range(4):
        ok = ((row >> 3) == ((n + 512 * q) >> 6)) & ((row & 7) == ((n >> 3) & 7))
        out = out + moved(jnp.broadcast_to(b1[0:1, D * q:D * q + D], (256, D)), ok, last)
    return out.reshape(4, 8, 8, 128)


def backward_kernel(near, *refs):
    refs = list(refs)

    def take(n):
        out = refs[:n]
        del refs[:n]
        return out
    ins = take(13)
    gffn, (gvec, gb1) = take(3), take(2)
    tok_o, gq_o = take(2)
    small_o = take(8 if near else 1)
    gffn_o = take(3 if near else 0)
    kvx, qx, bias, a1, ao, iz, sp, spt, da, tok, dh1, wq, vecs = take(13)
    gr, rm, dqt, dkv, dq, edge, e_got, w_all, w_got, w_mid, gq, avec, tok_s, dall, in_sem, out_sem, e_send, e_recv = take(18)
    if near:
        gv, f_mine, f_sem, send, recv, send_v, recv_v, v_got, v_sum, v_z = take(10)
        bufs = [take(4) for _ in range(11)]
    me = Peers(near)
    place = me.place
    loads = {}
    targets = (da, ao, iz, sp, kvx, qx, bias, spt, a1, tok, dh1, wq, vecs)
    names = ("da", "ao", "iz", "sp", "kvx", "qx", "bias", "spt", "a1", "tok", "dh1", "wq", "vecs")
    for k, name in enumerate(names):
        loads[name] = pltpu.make_async_copy(ins[k], targets[k], in_sem.at[k])
        loads[name].start()
    greet(me.greeted)
    mine_copies = []
    if near:
        for k in range(3):
            cp = pltpu.make_async_copy(gffn[k].at[:, :, :, me.c], f_mine[k], f_sem.at[k])
            cp.start()
            mine_copies.append(cp)
        every = slice(None)
        ffn = [Scatter(me, lambda c, k=k: ffn_view(gffn, k, (every, every, every, c)), lambda h, y, x, k=k: ffn_values(f_mine, k, (h, y, x)),
                       k in (2, 4), bufs[k], send.at[k], recv.at[k]) for k in range(5)]
        last = []
        for k in range(6):
            lo = 256 * (k % 2)
            last.append(Scatter(me, lambda c, k=k, lo=lo: gq.at[k // 2, :, :, :, c, :, pl.ds(lo, 256)],
                                lambda h, y, x, k=k, lo=lo: gq[k // 2, h, y, x, me.c, :, lo:lo + 256], k % 2 == 1,
                                bufs[5 + k], send.at[5 + k], recv.at[5 + k]))
        small_s = SmallScatter(me, gv, v_got, v_sum, v_z, send_v, recv_v)
        for a in ffn:
            a.start(0)

    def put_ffn(k):
        which, tail = ffn_index(k, lambda at, n: slice(at, at + n))
        gffn_o[which][tail or (slice(None),)] = ffn[k].result()

    def put_last(k):
        gq_o[k // 2, :, 256 * (k % 2):256 * (k % 2) + 256] = last[k].result()

    def step(group, stage, *pieces):
        if not near:
            return
        for k in pieces:
            a = (ffn if group == 0 else last)[k]
            a.wait(stage)
            if stage < 3:
                a.add(stage)
                a.start(stage + 1)
            elif group == 0:
                put_ffn(k)
            else:
                put_last(k)

    for name in ("da", "ao", "iz", "sp"):
        loads[name].wait()
    masks = head_masks(128)

    @pl.loop(0, 4)
    def _(g):
        lo, hi = pl.ds(pl.multiple_of(g * 128, 128), 64), pl.ds(pl.multiple_of(g * 128 + 64, 64), 64)
        for j in range(TILES):
            cols = slice(TILE * j, TILE * j + TILE)
            g0 = da[lo, cols].astype(F32) * iz[g, 0:1, cols]
            g1 = da[hi, cols].astype(F32) * iz[g, 1:2, cols]
            r0 = jnp.sum(g0 * ao[lo, cols].astype(F32), axis=0, keepdims=True)
            r1 = jnp.sum(g1 * ao[hi, cols].astype(F32), axis=0, keepdims=True)
            rm[g, 0:1, cols] = r0
            rm[g, 1:2, cols] = r1
            high, low = split(two_rows(r0, r1))
            gr[g, :, cols] = jnp.concatenate([g0.astype(BF16), g1.astype(BF16), high, low], axis=0)
        for b, (at, block, t, n) in enumerate(coarse_blocks()):
            x = mm_bt(gr[g, :, t:t + n], sp[128 * block:128 * block + 128, t:t + n])
            cols = slice(1024 + at, 1152 + at)
            gr[g, 0:128, cols] = x[0:128].astype(BF16)
            times = tile_times(8 + b)
            rm[g, 0:1, cols] = (x[128:129] + x[144:145]) * times
            rm[g, 1:2, cols] = (x[129:130] + x[145:146]) * times
    dkv[...] = jnp.zeros_like(dkv)
    for name in ("kvx", "qx", "bias"):
        loads[name].wait()
    zero = jnp.zeros((64, 128), BF16)

    def tile(g, i):
        keys = slice(tile_at(i), tile_at(i) + tile_keys(i))
        cols = slice(128 * i, 128 * i + 128)
        kw, vw = kvx[keys, lanes_of(g)], kvx[keys, lanes_of(g, D)]
        q = by_head(qx[cols, lanes_of(g)], masks)
        gt = gr[g, 0:128, cols]
        gb = jnp.concatenate([jnp.concatenate([gt[0:64], zero], axis=1), jnp.concatenate([zero, gt[64:128]], axis=1)], axis=0)
        e = jnp.exp(mm_bt(kw, q) + bias_of(bias, i))
        rest = jnp.concatenate([rm[g, 0:1, cols], rm[g, 1:2, cols]], axis=1)
        ds = (e * (mm(vw, gb) - rest)).astype(BF16)
        dkv[keys, lanes_of(g)] += mm(ds, q)
        dkv[keys, lanes_of(g, D)] += mm_bt(e.astype(BF16), gb)
        dqt[g, :, cols] = (own_blocks(mm_at(kw, ds)) * (0.125 / tile_times(i))).astype(BF16)

    if near:
        wait_all(mine_copies)
    step(0, 0, 0, 1, 2, 3, 4)

    @pl.loop(0, 4)
    def _(g):
        for i in OUTER:
            tile(g, i)
    for side in range(2):
        base, closer = [], []
        for l in range(7):
            at = border(side, l)
            k16, v16 = dkv[at:at + 16, 0:D], dkv[at:at + 16, D:2 * D]
            if l == 0:
                base += [k16, v16]
            elif side == 0:
                base += [k16[0:8], v16[0:8]]
                closer += [k16[8:16], v16[8:16]]
            else:
                base += [k16[8:16], v16[8:16]]
                closer += [k16[0:8], v16[0:8]]
        folded = mm_at(near_rows(side), jnp.concatenate(closer, axis=0).astype(BF16))
        edge[side] = (jnp.concatenate(base, axis=0) + folded).astype(BF16).reshape(8, 16, D)
    d_wide = mm_at(wide_rows(0), dkv[WIDE_AT:EXT, 0:D].astype(BF16)) + mm_at(wide_rows(1), dkv[WIDE_AT:EXT, D:2 * D].astype(BF16))
    w_all[...] = d_wide.astype(BF16).reshape(8, 16, D)
    to_right = rcopy(edge.at[1], e_got.at[0], e_send.at[0], e_recv.at[0], me.right)
    to_left = rcopy(edge.at[0], e_got.at[1], e_send.at[1], e_recv.at[1], me.left)
    wide_core = rcopy(w_all.at[pl.ds(4 * (1 - me.odd), 4)], w_mid, e_send.at[2], e_recv.at[2], me.core)
    not_last, not_first = place < 7, place > 0
    wide_core.start()

    @pl.when(not_last)
    def _():
        to_right.start()

    @pl.when(not_first)
    def _():
        to_left.start()
    step(0, 1, 0, 1, 2)

    @pl.loop(0, 2)
    def _(g):
        for i in INNER:
            tile(g, i)
    wide_core.wait()
    for k in range(4):
        w_mid[k] = (w_mid[k].astype(F32) + w_all[4 * me.odd + k].astype(F32)).astype(BF16)
    wide_z = [rcopy(w_mid.at[me.z_index[k]], w_got.at[k], e_send.at[3 + k], e_recv.at[3 + k], me.zs[k]) for k in range(3)]
    start_all(wide_z)

    @pl.loop(2, 4)
    def _(g):
        for i in INNER:
            tile(g, i)
    step(0, 1, 3, 4)

    @pl.loop(0, 4)
    def _(g):
        d_ref = dqt.at[g]
        eye = identity(TILE)
        for j in range(TILES):
            cols = slice(TILE * j, TILE * j + TILE)
            r = d_ref[:, cols].astype(F32) + mm(coarse_cols(d_ref, 1024, j), sp[:, cols])
            dq[cols, lanes_of(g)] = mm_bt(eye, r.astype(BF16)).astype(BF16)
    for name in ("spt", "a1", "tok", "dh1", "wq", "vecs"):
        loads[name].wait()
    avec[...] = jnp.zeros_like(avec)

    def projection_grad(c, d):
        aw = mm_at(a1[...], d).astype(BF16)
        avec[2 + c:3 + c, :] = jnp.sum(d.astype(F32), axis=0, keepdims=True)
        gq[c] = aw.reshape(4, 2, 2, 2, 16, D)
        if near:
            for a in last[2 * c:2 * c + 2]:
                a.start(0)
    projection_grad(0, dq[...])
    step(0, 2, 0, 1, 2)
    for cp in wide_z:
        cp.wait()

    def add_edge(side):
        m = e_got[side].reshape(128, D).astype(F32)
        for l in range(7):
            if l == 0:
                at, n = own_border(side, 0), 16
            else:
                at, n = own_border(side, l) + (0 if side else 8), 8
            a = 16 * (l + 1) if l else 0
            dkv[at:at + n, 0:D] += m[a:a + n]
            dkv[at:at + n, D:2 * D] += m[a + n:a + 2 * n]

    @pl.when(not_last)
    def _():
        to_right.wait_send()
        to_left.wait_recv()
        add_edge(1)

    @pl.when(not_first)
    def _():
        to_left.wait_send()
        to_right.wait_recv()
        add_edge(0)
    v = w_mid[me.h].astype(F32)
    for k in range(3):
        v = v + w_got[k].astype(F32)
    v = jnp.concatenate([v[0:8] * 0.5 ** 7, v[8:16]], axis=1)
    w_own = jnp.concatenate([v, jnp.zeros((8, 2 * D), F32)], axis=0).astype(BF16)
    lane_all = iota((1, 2 * D), 1)

    def coarse_rows(at, n, level):
        return (dkv[at:at + n, :] * jnp.where(lane_all < D, 0.5 ** level, 1.0)).astype(BF16)
    top = jnp.concatenate([coarse_rows(EXT_AT[3] + 16, 128, 3), coarse_rows(EXT_AT[4] + 16, 64, 4), coarse_rows(EXT_AT[5] + 16, 32, 5),
                           coarse_rows(EXT_AT[6] + 16, 16, 6), w_own], axis=0)
    for j in range(TILES):
        rows = slice(TILE * j, TILE * j + TILE)
        x = jnp.concatenate([coarse_rows(EXT_AT[1] + 16 + 128 * j, 128, 1), coarse_rows(EXT_AT[2] + 16 + 128 * (j // 2), 128, 2), top], axis=0)
        dall[rows, :] = (dkv[16 + TILE * j:16 + TILE * j + TILE, :] + mm(spt[rows, :], x)).astype(BF16)
    projection_grad(1, dall[:, 0:D])
    step(0, 2, 3, 4)
    step(1, 0, 0, 1)
    projection_grad(2, dall[:, D:2 * D])
    step(1, 0, 2, 3)
    for j in range(TILES):
        rows = slice(TILE * j, TILE * j + TILE)
        da1 = mm_bt(dq[rows, :], wq[0].reshape(D, D)) + mm_bt(dall[rows, 0:D], wq[1].reshape(D, D)) + mm_bt(dall[rows, D:2 * D], wq[2].reshape(D, D))
        v = tok[rows, :].astype(F32)
        center = v - jnp.mean(v, axis=-1, keepdims=True)
        inverse = lax.rsqrt(jnp.mean(center * center, axis=-1, keepdims=True) + EPS)
        n = center * inverse
        e = da1 * vecs[0:1, :]
        dv = inverse * (e - jnp.mean(e, axis=-1, keepdims=True) - n * jnp.mean(e * n, axis=-1, keepdims=True))
        tok_s[rows, :] = (dh1[rows, :] + dv).astype(BF16)
        avec[0:1, :] += jnp.sum(da1 * n, axis=0, keepdims=True)
        avec[1:2, :] += jnp.sum(da1, axis=0, keepdims=True)
        if j == 0:
            step(1, 0, 4, 5)
        elif j == 1:
            step(1, 1, 0, 1)
        elif j == 2:
            step(1, 1, 2, 3)
    done = pltpu.make_async_copy(tok_s, tok_o, out_sem.at[0])
    done.start()
    if not near:
        gq_o[...] = gq[...]
        small_o[0][...] = avec[...]
        done.wait()
        return
    avec[5:9, :] = gvec[5:9, :]
    gv[...] = pack_small(avec[...], gb1)
    start_all(small_s.first())
    step(1, 1, 4, 5)
    step(1, 2, 0, 1)
    wait_all(small_s.first())
    small_s.add()
    start_all(small_s.second())
    step(1, 2, 2, 3, 4, 5)
    step(0, 3, 0, 1, 2, 3, 4)
    step(1, 3, 0, 1, 2, 3, 4, 5)
    wait_all(small_s.second())
    t = small_s.result()
    for k, r in enumerate((0, 1, None, 5, 6, 7)):
        if r is None:
            small_o[k][...] = t[2:5, 0:16]
        else:
            small_o[k][...] = t[r:r + 1, 0:16]
    for r in range(8):
        small_o[6][0:1, 8 * r:8 * r + 8] = t[r:r + 1, 32:40]
    small_o[7][...] = t[0:1, 16:32]
    done.wait()


def backward(near, saved, wq, vecs, tok, da, dh1, gffn, gvec, gb1):
    kvx, qx, bias, a1, ao, iz, sp, spt = saved
    grid = (4, 2, 2, 2)
    vm = [VMEM(v.shape, v.dtype) for v in (kvx, qx, bias, a1, ao, iz, sp, spt, da, tok, dh1, wq, vecs)]
    scratch = vm + [VMEM((4, 160, 2048), BF16), VMEM((4, 2, 2048), F32), VMEM((4, 128, 2048), BF16), VMEM((EXT, 2 * D), F32),
                    VMEM((TOK, D), BF16), VMEM((2, 8, 16, D), BF16), VMEM((2, 8, 16, D), BF16), VMEM((8, 16, D), BF16),
                    VMEM((3, 16, D), BF16), VMEM((4, 16, D), BF16), VMEM((3,) + grid + (16, D), BF16), VMEM((16, D), F32), VMEM((TOK, D), BF16), VMEM((TOK, 2 * D), BF16),
                    SEM((13,)), SEM((1,)), SEM((6,)), SEM((6,))]
    if near:
        gffn = [g.reshape(grid + (g.shape[0] // 32, g.shape[1])) for g in gffn]
        shapes = [S((TOK, D), BF16), S((3, 16, D), F32)]
        shapes += [S((1, 16), F32), S((1, 16), F32), S((3, 16), F32), S((1, 16), F32), S((1, 16), F32), S((1, 16), F32), S((1, 64), F32), S((1, 16), F32)]
        shapes += [S(g.shape[4:], F32) for g in gffn]
        pieces = [(shape, BF16) for shape in FFN_SHAPES] + [((16, 256), BF16)] * 6
        scratch += [VMEM((4, 8, 8, 128), F32), [VMEM((4, 2, 2) + g.shape[4:], BF16) for g in gffn], SEM((3,)), SEM((11, 6)), SEM((11, 6)),
                    SEM((10,)), SEM((10,)), VMEM((7, 4, 8, 128), F32), VMEM((4, 8, 128), F32), VMEM((3, 8, 128), F32)]
        for shape, kind in pieces:
            scratch += scatter_bufs(shape, kind)
    else:
        gffn = gffn[0:3]
        shapes = [S((TOK, D), BF16), S((3,) + grid + (16, D), BF16), S((16, D), F32)]
    ordered = (da, ao, iz, sp, kvx, qx, bias, spt, a1, tok, dh1, wq, vecs)
    return pl.pallas_call(
        functools.partial(backward_kernel, near),
        out_shape=shapes,
        in_specs=[ANY] * 16 + [IN_VMEM] * 2,
        out_specs=[ANY] + [IN_VMEM] * (len(shapes) - 1),
        scratch_shapes=scratch,
        compiler_params=pltpu.CompilerParams(collective_id=1, has_side_effects=True, vmem_limit_bytes=62 << 20),
        name="backward",
    )(*ordered, *gffn, gvec, gb1)


def finish_kernel(n, *refs):
    for k in range(n):
        refs[n + k][...] = refs[k][...]


def finish(*values):
    n = len(values)
    return pl.pallas_call(
        functools.partial(finish_kernel, n),
        out_shape=[S(v.shape, v.dtype) for v in values],
        in_specs=[IN_VMEM] * n,
        out_specs=[IN_VMEM] * n,
        name="finish",
    )(*values)


BOTH = ("head", "span")


def shards(tokens, segment_ids, first_gain, first_shift, project_weight, project_bias, output_weight, output_bias,
           second_gain, second_shift, expand_weight, expand_bias, reduce_weight, reduce_bias, cotangent):
    tok, cot = tokens[0], cotangent[0]
    near = lax.axis_size("head") == 4 and lax.axis_size("span") == 8
    if near:
        vectors = (first_gain, first_shift, project_bias, output_bias, second_gain, second_shift, reduce_bias, expand_bias)
        vectors = [v if v.ndim == 2 else v[None] for v in vectors]
        *saved, wq, vecs, b1, wo, w1, w2 = forward(True, tok, segment_ids, project_weight, *vectors, output_weight, expand_weight, reduce_weight)
        wo, w1, w2 = wo.reshape(D, D), w1.reshape(D, FF), w2.reshape(FF, D)
    else:
        def full(v, axis=0):
            return lax.all_gather(v, BOTH, axis=axis, tiled=True)
        wq, wo, w1, w2 = full(project_weight, 1), full(output_weight), full(expand_weight), full(reduce_weight)
        rows = [full(first_gain), full(first_shift), *full(project_bias, 1), full(output_bias), full(second_gain), full(second_shift), full(reduce_bias)]
        vecs = jnp.pad(jnp.stack(rows), ((0, 7), (0, 0)))
        b1 = full(expand_bias)[None]
        saved = forward(False, tok, segment_ids, wq, vecs)
    ao = saved[4]
    out, dh1, da, *gffn, gvec, gb1 = middle(tok, ao, cot, wo, w1, w2, vecs, b1)
    dtok, gwq, *rest = backward(near, saved, wq, vecs, tok, da, dh1, gffn, gvec, gb1)
    if near:
        dtok, gwq, *rest = finish(dtok, gwq, *rest)
        small, (gwo, gw1, gw2) = rest[0:8], rest[8:11]
        small = [v if v.shape[0] == 3 else v.reshape(-1) for v in small]
    else:
        def part(v, axis=0):
            return lax.psum_scatter(v.astype(F32), BOTH, scatter_dimension=axis, tiled=True)
        vec, gwq = rest[0], gwq.reshape(3, D, D)
        gwq, gwo, gw1, gw2 = part(gwq, 1), part(gffn[0]), part(gffn[1]), part(gffn[2])
        small = (part(vec[0]), part(vec[1]), part(vec[2:5], 1), part(gvec[5]), part(gvec[6]), part(gvec[7]), part(gb1[0]), part(gvec[8]))
    return (out[None], dtok[None], small[0], small[1], gwq, small[2], gwo, small[3], small[4], small[5], gw1, small[6], gw2, small[7])


def solution(mesh):
    token, row, matrix = P("span", "head", None), P(BOTH), P(BOTH, None)
    three, bias = P(None, BOTH, None), P(None, BOTH)
    params = (row, row, three, bias, matrix, row, row, row, matrix, row, matrix, row)
    return jax.shard_map(shards, mesh=mesh, in_specs=(token, P("span", None)) + params + (token,),
                         out_specs=(token, token) + params, check_vma=False)
```

```python
import functools
import jax
import jax.numpy as jnp
from jax import lax
from jax.experimental import pallas as pl
from jax.experimental.pallas import tpu as pltpu
from jax.sharding import PartitionSpec as P

F32, BF16, I32 = jnp.float32, jnp.bfloat16, jnp.int32
MESH = pl.DeviceIdType.MESH
VMEM = pltpu.VMEM
NEG = -1e30
EPS = 1e-5
TOK = 1024
TILE = 256
D = 512
FF = 2048
EXT = 2384
SIZES = (1024, 512, 256, 128, 64, 32, 16)
EXT_AT = (0, 1056, 1600, 1888, 2048, 2144, 2208)
WIDE_AT = 2256
TRANS_B = (((1,), (1,)), ((), ()))
TRANS_A = (((0,), (0,)), ((), ()))


def mm(a, b):
    return jnp.dot(a, b, preferred_element_type=F32)


def mm_bt(a, b):
    return lax.dot_general(a, b, TRANS_B, preferred_element_type=F32)


def mm_at(a, b):
    return lax.dot_general(a, b, TRANS_A, preferred_element_type=F32)


def iota(shape, dim):
    return lax.broadcasted_iota(I32, shape, dim)


def split(v):
    high = v.astype(BF16)
    return high, (v - high.astype(F32)).astype(BF16)


def covers(t, c, block):
    if block == 0:
        return ((t & 255) >> 1) == c
    if block == 1:
        return ((t & 511) >> 2) == c
    if block == 2:
        return (t >> 3) == c
    level, start = mixed_levels(c)
    return (jnp.right_shift(t, level) == c - start) & (c < 124)


def mixed_levels(c):
    a, b, d, e = ((c >= edge).astype(I32) for edge in (64, 96, 112, 120))
    return 4 + a + b + d + e, 64 * a + 32 * b + 16 * d + 8 * e


def ones_where(cond):
    return jnp.where(cond, 1.0, 0.0).astype(BF16)


def identity(n):
    return ones_where(iota((n, n), 0) == iota((n, n), 1))


def fill_spread(spt):
    @pl.loop(0, TOK // TILE)
    def _(j):
        for block in range(4):
            t = iota((TILE, 128), 0) + j * TILE
            c = iota((TILE, 128), 1)
            spt[pl.ds(j * TILE, TILE), 128 * block:128 * block + 128] = ones_where(covers(t, c, block))


def fill_pool(sp):
    @pl.loop(0, TOK // TILE)
    def _(j):
        for block in range(4):
            t = iota((128, TILE), 1) + j * TILE
            c = iota((128, TILE), 0)
            sp[128 * block:128 * block + 128, pl.ds(pl.multiple_of(j * TILE, TILE), TILE)] = ones_where(covers(t, c, block))


TILES = TOK // TILE
BIAS_MIXED = 15 * 160
BIASES = BIAS_MIXED + 336


def tile_level(i):
    return 0 if i < 8 else 1 if i < 12 else 2 if i < 14 else 3


def tile_at(i):
    return 2048 if i == 15 else 128 * i + 32 * tile_level(i)


def tile_keys(i):
    return 336 if i == 15 else 160


def tile_times(i):
    if i < 15:
        return float(2 ** tile_level(i))
    level, _unused = mixed_levels(iota((1, 128), 1))
    return (1 << level).astype(F32)


INNER = (1, 2, 3, 4, 5, 6, 9, 10)
OUTER = (0, 7, 8, 11, 12, 13, 14, 15)


def labels_of(total, squares, times):
    return jnp.where(times * squares == total * total, total / times, 0.0)


def head_masks(rows):
    lane = iota((rows, 128), 1)
    return ones_where(lane < 64), ones_where(lane >= 64)


def by_head(x, masks):
    return jnp.concatenate([x * masks[0], x * masks[1]], axis=0)


def own_blocks(x):
    return jnp.concatenate([x[0:64, 0:128], x[64:128, 128:256]], axis=0)


def twice(x):
    return jnp.concatenate([x, x], axis=1)


def two_rows(a, b):
    row = iota((16, a.shape[1]), 0)
    return jnp.where(row == 0, a, jnp.where(row == 1, b, 0.0))


def lanes_of(g, base=0):
    return pl.ds(pl.multiple_of(base + g * 128, 128), 128)


def coarse_cols(ref, base, j):
    return jnp.concatenate([ref[:, base + 128 * j:base + 128 * j + 128],
                            ref[:, base + 512 + 128 * (j // 2):base + 640 + 128 * (j // 2)],
                            ref[:, base + 768:base + 1024]], axis=1)


def coarse_blocks():
    return ([(128 * j, 0, 256 * j, 256) for j in range(4)] + [(512 + 128 * j, 1, 512 * j, 512) for j in range(2)]
            + [(768, 2, 0, 1024), (896, 3, 0, 1024)])


def near_rows(side):
    o, i = iota((96, 128), 0), iota((96, 128), 1)
    level = (o >> 4) + 1
    block = i >> 4
    fine = jnp.maximum(block - 1, 0)
    value_out, value_in = (o >> 3) & 1, jnp.where(block < 2, block, (i >> 3) & 1)
    width, size = jnp.left_shift(1, fine), jnp.left_shift(1, level)
    if side == 0:
        start = ((o & 7) - 8) * size
        at = jnp.where(block < 2, (i & 15) - 16, (i & 7) - 16) * width
    else:
        start = (o & 7) * size
        at = jnp.where(block < 2, i & 15, (i & 7) + 8) * width
    inside = (value_out == value_in) & (at >= start) & (at + width <= start + size)
    share = jnp.where(value_out == 1, 1.0, width.astype(F32) / size.astype(F32))
    return jnp.where(inside, share, 0.0).astype(BF16)


def wide_rows(value):
    r, i = iota((128, 128), 0), iota((128, 128), 1)
    k, j = r & 15, (i & 15) - 8 * value
    own = ((r >> 4) == (i >> 4)) & (j >= 0) & (j < 8)
    fine, rough = own & (k < 8) & (j == k), own & (k >= 8) & (k < 12) & ((j >> 1) == k - 8)
    return jnp.where(fine, 1.0, jnp.where(rough, 1.0 if value else 0.5, 0.0)).astype(BF16)


def far_and_near(side, far, near):
    return jnp.concatenate([far, near] if side == 0 else [near, far], axis=0)


def border(side, l):
    return EXT_AT[l] + (16 + SIZES[l] if side else 0)


def own_border(side, l):
    return EXT_AT[l] + (SIZES[l] if side else 16)


def pick_far(side, rows):
    return rows[0:8] if side else rows[8:16]


def column_of(row, n):
    spread = jnp.where(iota((n, n), 0) == iota((n, n), 1), jnp.broadcast_to(row, (n, n)), 0.0)
    return jnp.broadcast_to(jnp.sum(spread, axis=1, keepdims=True), (n, 128)).astype(BF16)


def where_am_i():
    h = lax.axis_index("head")
    s = lax.axis_index("span")
    return h, s, s // 4, (s // 2) % 2, s % 2


class Peers:
    def __init__(self, near):
        h, s = lax.axis_index("head"), lax.axis_index("span")
        odd = s % 2
        self.place = odd * 4 + h
        self.odd = odd
        self.h = h
        other = s + 1 - 2 * odd
        self.z_index = [lax.rem(h + d, 4) for d in (1, 2, 3)]
        self.zs = [{"head": z} for z in self.z_index]
        self.core = {"span": other}
        opposite = {"head": 3 - h, "span": other}
        step = 1 - 2 * odd
        self.right = {"head": lax.rem(h + 1, 4), "span": s + step * ((h + 1) // 4)}
        self.left = {"head": lax.rem(h + 3, 4), "span": s + step * (1 - (h + 3) // 4)}
        self.greeted = self.zs + [self.core, opposite]
        if near:
            y, x = s // 4, (s // 2) % 2
            self.y, self.x, self.c = y, x, odd
            self.s = s
            self.px = {"span": y * 4 + (1 - x) * 2 + odd}
            self.py = {"span": (1 - y) * 4 + x * 2 + odd}
            self.s_index = [lax.rem(s + d, 8) for d in range(1, 8)]
            self.spans = [{"span": o} for o in self.s_index]
            self.greeted = self.zs + self.spans + [opposite]


def greet(devices):
    barrier = pltpu.get_barrier_semaphore()
    for d in devices:
        pl.semaphore_signal(barrier, inc=1, device_id=d, device_id_type=MESH)
    pl.semaphore_wait(barrier, len(devices))


def rcopy(src, dst, send, recv, device):
    return pltpu.make_async_remote_copy(src_ref=src, dst_ref=dst, send_sem=send, recv_sem=recv,
                                        device_id=device, device_id_type=MESH)


class Gather:
    def __init__(self, me, shard, full, swap, local, send, recv):
        self.me, self.shard, self.full, self.swap, self.local, self.send, self.recv = me, shard, full, swap, local, send, recv

    def own(self):
        m = self.me
        return pltpu.make_async_copy(self.shard, self.full(m.h, m.y, m.x, m.c), self.local)

    def hop(self, k):
        m, a = self.me, slice(None)
        if k < 3:
            return rcopy(self.shard, self.full(m.h, m.y, m.x, m.c), self.send.at[k], self.recv.at[k], m.zs[k])
        if k == 3:
            ref, dev = self.full(a, m.y, m.x, m.c), m.py if self.swap else m.px
        elif k == 4:
            ref, dev = (self.full(a, a, m.x, m.c), m.px) if self.swap else (self.full(a, m.y, a, m.c), m.py)
        else:
            ref, dev = self.full(a, a, a, m.c), m.core
        return rcopy(ref, ref, self.send.at[k], self.recv.at[k], dev)

    def start(self, stage):
        if stage == 0:
            self.own().start()
            for k in range(3):
                self.hop(k).start()
        else:
            self.hop(2 + stage).start()

    def wait(self, stage):
        if stage == 0:
            self.own().wait()
            for k in range(3):
                self.hop(k).wait()
        else:
            self.hop(2 + stage).wait()


class Scatter:
    def __init__(self, me, grad, mine, swap, bufs, send, recv):
        self.me, self.grad, self.mine, self.swap, self.bufs, self.send, self.recv = me, grad, mine, swap, bufs, send, recv

    def hops(self, stage):
        m, s, r = self.me, self.send, self.recv
        r1, r2, r3, r4 = self.bufs
        if stage == 0:
            return [rcopy(self.grad(1 - m.c), r1, s.at[0], r.at[0], m.core)]
        if stage == 1:
            src, dev = (r1.at[:, 1 - m.y], m.py) if self.swap else (r1.at[:, :, 1 - m.x], m.px)
            return [rcopy(src, r2, s.at[1], r.at[1], dev)]
        if stage == 2:
            src, dev = (r2.at[:, 1 - m.x], m.px) if self.swap else (r2.at[:, 1 - m.y], m.py)
            return [rcopy(src, r3, s.at[2], r.at[2], dev)]
        return [rcopy(r3.at[m.z_index[k]], r4.at[k], s.at[3 + k], r.at[3 + k], m.zs[k]) for k in range(3)]

    def start(self, stage):
        for cp in self.hops(stage):
            cp.start()

    def wait(self, stage):
        for cp in self.hops(stage):
            cp.wait()

    def add(self, stage):
        m = self.me
        r1, r2, r3, r4 = self.bufs

        def into(dst, key, other):
            dst[key] = (dst[key].astype(F32) + other.astype(F32)).astype(dst.dtype)
        if stage == 0:
            @pl.loop(0, 4)
            def _(hh):
                for yy in range(2):
                    for xx in range(2):
                        into(r1, (hh, yy, xx), self.mine(hh, yy, xx))
        elif stage == 1:
            @pl.loop(0, 4)
            def _(hh):
                for v in range(2):
                    into(r2, (hh, v), r1[hh, m.y, v] if self.swap else r1[hh, v, m.x])
        else:
            @pl.loop(0, 4)
            def _(hh):
                into(r3, (hh,), r2[hh, m.x if self.swap else m.y])

    def result(self):
        r1, r2, r3, r4 = self.bufs
        acc = r3[self.me.h].astype(F32)
        for k in range(3):
            acc = acc + r4[k].astype(F32)
        return acc


class SmallGather:
    def __init__(self, me, tile, full, local, send, recv):
        self.me, self.tile, self.full, self.local, self.send, self.recv = me, tile, full, local, send, recv

    def first(self):
        dst = self.full.at[self.me.h, self.me.s]
        return [rcopy(self.tile, dst, self.send.at[k], self.recv.at[k], self.me.zs[k]) for k in range(3)]

    def second(self):
        ref = self.full.at[:, self.me.s]
        return [rcopy(ref, ref, self.send.at[3 + k], self.recv.at[3 + k], self.me.spans[k]) for k in range(7)]

    def own(self):
        return pltpu.make_async_copy(self.tile, self.full.at[self.me.h, self.me.s], self.local)


class SmallScatter:
    def __init__(self, me, grad, got, total, got_z, send, recv):
        self.me, self.grad, self.got, self.total, self.got_z, self.send, self.recv = me, grad, got, total, got_z, send, recv

    def first(self):
        m = self.me
        return [rcopy(self.grad.at[:, m.s_index[k]], self.got.at[k], self.send.at[k], self.recv.at[k], m.spans[k]) for k in range(7)]

    def second(self):
        m = self.me
        return [rcopy(self.total.at[m.z_index[k]], self.got_z.at[k], self.send.at[7 + k], self.recv.at[7 + k], m.zs[k]) for k in range(3)]

    def add(self):
        v = self.grad[:, self.me.s]
        for k in range(7):
            v = v + self.got[k]
        self.total[...] = v

    def result(self):
        v = self.total[self.me.h]
        for k in range(3):
            v = v + self.got_z[k]
        return v


def start_all(copies):
    for cp in copies:
        cp.start()


def wait_all(copies):
    for cp in copies:
        cp.wait()


FFN_SHAPES = ((16, D), (16, 768), (16, 1280), (32, D), (32, D))


def ffn_index(k, whole):
    half = (k - 1) % 2
    if k == 0:
        return 0, ()
    if k < 3:
        return 1, (slice(None), whole(768 * half, 768 + 512 * half))
    return 2, (whole(32 * half, 32),)


def ffn_view(refs, k, index):
    which, tail = ffn_index(k, pl.ds)
    return refs[which].at[index + tail]


def ffn_values(refs, k, index):
    which, tail = ffn_index(k, lambda at, n: slice(at, at + n))
    return refs[which][index + tail]


def scatter_bufs(shape, dtype):
    return [VMEM((4, 2, 2) + shape, dtype), VMEM((4, 2) + shape, dtype), VMEM((4,) + shape, dtype), VMEM((3,) + shape, dtype)]


def split3(v):
    high, rest = split(v)
    mid = rest
    low = (v - high.astype(F32) - mid.astype(F32)).astype(BF16)
    return high, mid, low


def mm_exact(v, ones):
    a, b, c = split3(v)
    return mm(a, ones) + mm(b, ones) + mm(c, ones)


def small_rows(vt, g1, s1, pb, ob, g2, s2, rb, eb):
    vt[...] = jnp.zeros_like(vt)
    for r, ref in enumerate((g1, s1, None, None, None, ob, g2, s2)):
        vt[r:r + 1, 0:16] = pb[r - 2:r - 1, :] if ref is None else ref[...]
    vt[0:1, 16:32] = rb[...]
    for r in range(8):
        vt[r:r + 1, 32:40] = eb[0:1, 8 * r:8 * r + 8]


def unpack_small(gathered, vecs, b1):
    v = gathered[...].reshape(256, 128)
    row, n = iota((256, D), 0), iota((256, D), 1)
    lane, col = iota((128, D), 0), iota((128, D), 1)
    mine = (row >> 3) == (n >> 4)
    for half in range(2):
        x = mm_exact(v, ones_where(lane == (col & 15) + 16 * half))
        vecs[8 * half:8 * half + 8, :] = jnp.sum(jnp.where(mine, x, 0.0).reshape(32, 8, D), axis=0)
    x = mm_exact(v, ones_where(lane == (col & 7) + 32))
    for q in range(4):
        ok = ((row >> 3) == ((n + 512 * q) >> 6)) & ((row & 7) == ((n >> 3) & 7))
        b1[0:1, D * q:D * q + D] = jnp.sum(jnp.where(ok, x, 0.0), axis=0, keepdims=True)


def fill_bias(bias, labk, labq, place, tiles):
    def matching(i):
        kl = labk[tile_at(i):tile_at(i) + tile_keys(i), :].astype(F32)
        return (kl == labq[i:i + 1, :]) & (kl != 0.0)

    r, c = iota((160, 128), 0), iota((160, 128), 1)
    near = jnp.abs((r >> 4) - 1 - (c >> 4)) <= 1
    far = near & (jnp.abs((r >> 3) - 2 - (c >> 3)) >= 2)
    same = (r - 16) == c
    for i in tiles:
        if i == 15:
            continue
        ok = matching(i) & near | same if i < 8 else matching(i) & far
        bias[160 * i:160 * i + 160, :] = jnp.where(ok, 0.0, NEG)
    if 15 not in tiles:
        return
    r, c = iota((336, 128), 0), iota((336, 128), 1)
    inner = (r >= 96).astype(I32) + (r >= 160).astype(I32)
    start = jnp.where(inner == 0, 0, jnp.where(inner == 1, 96, 160))
    e, k = (r - 208) >> 4, (r - 208) & 15
    upper = (k >= 8).astype(I32)
    level_k = jnp.where(r < 208, 4 + inner, 7 + upper)
    pos_k = jnp.where(r < 208, r - start - 16, jnp.where(k < 8, e * 8 + k, e * 4 + k - 8))
    level_q, start_q = mixed_levels(c)
    pos_q = c - start_q + jnp.where(level_q == 7, place * 8, jnp.where(level_q == 8, place * 4, 0))
    shape = (level_k == level_q) & (jnp.abs((pos_k >> 4) - (pos_q >> 4)) <= 1) & (jnp.abs((pos_k >> 3) - (pos_q >> 3)) >= 2)
    bias[BIAS_MIXED:BIASES, :] = jnp.where(matching(15) & shape, 0.0, NEG)


def bias_of(bias, i):
    return twice(bias[160 * i:160 * i + 160, :] if i < 15 else bias[BIAS_MIXED:BIASES, :])


def forward_kernel(near, *refs):
    refs = list(refs)

    def take(n):
        out = refs[:n]
        del refs[:n]
        return out
    tok, seg = take(2)
    if near:
        wq_in, = take(1)
        small = take(8)
        ffn_in = take(3)
    else:
        wq, vecs = take(2)
    kvx_o, qx_o, bias_o, a1_o, ao_o, iz_o, sp_o, spt_o = take(8)
    if near:
        wq_o, vecs_o, b1_o = take(3)
        ffn_o = take(3)
    kvx, qx, bias, a1, ao, iz, sp, spt, xh, labq, n0, nc, z0, labk, seg2, msg, got, wbuf, out_sem, e_send, e_recv = take(21)
    if near:
        wq, vecs, b1, vt, vg, local, send, recv, send_v, recv_v = take(10)
    me = Peers(near)
    place = me.place
    outs = []

    def emit(src, dst):
        cp = pltpu.make_async_copy(src, dst, out_sem.at[len(outs)])
        cp.start()
        outs.append(cp)

    got[...] = jnp.zeros_like(got)
    if near:
        small_rows(vt, *small)
    greet(me.greeted)
    ids_core = rcopy(seg, seg2, e_send.at[6], e_recv.at[6], me.core)
    ids_core.start()
    if near:
        small_g = SmallGather(me, vt, vg, local.at[15], send_v, recv_v)
        small_g.own().start()
        start_all(small_g.first())
        first = []
        for k, (which, lanes) in enumerate((w, pl.ds(lo, 256)) for w in (pl.ds(1, 2), pl.ds(0, 1)) for lo in (0, 256)):
            first.append(Gather(me, wq_in.at[which, :, lanes], lambda h, y, x, c, which=which, lanes=lanes: wq.at[which, h, y, x, c, :, lanes],
                                k % 2 == 1, local.at[k], send.at[k], recv.at[k]))
        later = [Gather(me, ffn_view(ffn_in, k, ()), lambda h, y, x, c, k=k: ffn_view(ffn_o, k, (h, y, x, c)), k in (2, 4),
                        local.at[4 + k], send.at[4 + k], recv.at[4 + k]) for k in range(5)]

    def step(group, stage, *pieces):
        if not near:
            return
        for k in pieces:
            a = (first if group == 0 else later)[k]
            if stage >= 0:
                a.wait(stage)
            if stage < 3:
                a.start(stage + 1)

    step(0, -1, 0, 1, 2, 3)
    fill_pool(sp)
    fill_spread(spt)
    emit(sp, sp_o)
    emit(spt, spt_o)
    if near:
        small_g.own().wait()
        wait_all(small_g.first())
        start_all(small_g.second())
    step(0, 0, 0, 1, 2, 3)
    step(1, -1, 0, 1, 2, 3, 4)
    ids_core.wait()

    def chunk(ref, k):
        return ref[:, pl.ds(pl.multiple_of(TOK * k, TOK), TOK)].astype(F32)
    odd = me.odd.astype(F32)
    ids = chunk(seg, me.h)
    ids_left = jnp.where(me.h > 0, chunk(seg, lax.rem(me.h + 3, 4)), chunk(seg2, 3) * odd)
    ids_right = jnp.where(me.h < 3, chunk(seg, lax.rem(me.h + 1, 4)), chunk(seg2, 0) * (1.0 - odd))
    ids_b = jnp.broadcast_to(ids, (128, TOK)).astype(BF16)
    sq_b = jnp.broadcast_to(ids * ids, (128, TOK)).astype(BF16)
    eye = identity(TILE)
    for j in range(TILES):
        labk[16 + TILE * j:16 + TILE * j + TILE, :] = mm_bt(eye, ids_b[:, TILE * j:TILE * j + TILE]).astype(BF16)
    for i in range(8):
        labq[i:i + 1, :] = ids[:, 128 * i:128 * i + 128]
    row, t = iota((128, TOK), 0), iota((128, TOK), 1)
    level, level_row = row >> 4, iota((1, 128), 1) >> 4
    for side, v in ((0, ids_left), (1, ids_right)):
        base = jnp.right_shift(TOK, level) - 16 if side == 0 else 0
        sel = ones_where(jnp.right_shift(t, level) == base + (row & 15))
        x = mm_bt(two_rows(v, v * v).astype(BF16), sel)
        col = column_of(labels_of(x[0:1], x[1:2], jnp.left_shift(1, level_row).astype(F32)), 128)
        for l in range(7):
            labk[border(side, l):border(side, l) + 16, :] = col[16 * l:16 * l + 16]
    even_ids = [jnp.where(me.odd == 0, chunk(seg, k), chunk(seg2, k)) for k in range(4)]
    odd_ids = [jnp.where(me.odd == 0, chunk(seg2, k), chunk(seg, k)) for k in range(4)]
    all_ids = jnp.concatenate(even_ids + odd_ids, axis=0)
    x = mm_bt(jnp.concatenate([all_ids, all_ids * all_ids], axis=0).astype(BF16), sp[496:512, :])
    lab = labels_of(x[0:8], x[8:16], jnp.where(iota((8, 16), 1) < 8, 128.0, 256.0))
    lab = jnp.broadcast_to(lab[:, None, :], (8, 16, 16)).reshape(128, 16)
    lab = jnp.sum(jnp.where((iota((128, 16), 0) & 15) == iota((128, 16), 1), lab, 0.0), axis=1, keepdims=True)
    labk[WIDE_AT:EXT, :] = jnp.broadcast_to(lab, (128, 128)).astype(BF16)

    def put_coarse(dst, b, value, cols):
        at, block, _t, _n = coarse_blocks()[b]
        if block < 3:
            level = block + 1
            row = EXT_AT[level] + 16 + at - (0, 512, 768)[block]
            dst[row:row + 128, cols] = value
        else:
            for level, a, n in ((4, 0, 64), (5, 64, 32), (6, 96, 16)):
                dst[EXT_AT[level] + 16:EXT_AT[level] + 16 + n, cols] = value[a:a + n]

    for b, (at, block, t, n) in enumerate(coarse_blocks()):
        s = sp[128 * block:128 * block + 128, t:t + n]
        rows_level, _unused = mixed_levels(iota((128, 128), 0))
        cols_level, _unused = mixed_levels(iota((8, 128), 1))
        times_r = (1 << rows_level).astype(F32) if block == 3 else float(2 ** (block + 1))
        times_c = (1 << cols_level).astype(F32) if block == 3 else float(2 ** (block + 1))
        lab = labels_of(mm_bt(s, ids_b[:, t:t + n]), mm_bt(s, sq_b[:, t:t + n]), times_r)
        put_coarse(labk, b, lab.astype(BF16), slice(0, 128))
        row = labels_of(mm_bt(ids_b[0:8, t:t + n], s), mm_bt(sq_b[0:8, t:t + n], s), times_c)
        labq[8 + b:9 + b, :] = row[0:1, :]
    step(0, 1, 0, 1, 2, 3)
    fill_bias(bias, labk, labq, place, range(16))
    emit(bias, bias_o)
    @pl.loop(0, TILES)
    def _(j):
        rows = pl.ds(pl.multiple_of(TILE * j, TILE), TILE)
        v = tok[rows, :].astype(F32)
        center = v - jnp.mean(v, axis=-1, keepdims=True)
        xh[rows, :] = center * lax.rsqrt(jnp.mean(center * center, axis=-1, keepdims=True) + EPS)
    step(0, 2, 0, 1, 2, 3)
    step(1, 0, 0, 1, 2, 3, 4)
    if near:
        wait_all(small_g.second())
        unpack_small(vg, vecs, b1)
        emit(vecs, vecs_o)
        emit(b1, b1_o)
    @pl.loop(0, TILES)
    def _(j):
        rows = pl.ds(pl.multiple_of(TILE * j, TILE), TILE)
        a1[rows, :] = (xh[rows, :] * vecs[0:1, :] + vecs[1:2, :]).astype(BF16)
    emit(a1, a1_o)
    step(0, 3, 0, 1)

    def project(c):
        w = wq[c].reshape(D, D)
        for j in range(TILES):
            r = (mm(a1[TILE * j:TILE * j + TILE, :], w) + vecs[2 + c:3 + c, :]).astype(BF16)
            if c == 0:
                qx[TILE * j:TILE * j + TILE, :] = r * jnp.array(0.125, BF16)
            else:
                kvx[16 + TILE * j:16 + TILE * j + TILE, D * (c - 1):D * c] = r

    def pool_parts(block, t, n):
        if block == 3:
            level, _unused = mixed_levels(iota((128, D), 0))
            shrink = 1.0 / (1 << level).astype(F32)
        else:
            shrink = 0.5 ** (block + 1)
        return sp[128 * block:128 * block + 128, t:t + n], shrink
    project(1)
    project(2)
    step(1, 1, 0, 2)
    wide_z = [rcopy(wbuf.at[place], wbuf.at[place], e_send.at[2 + k], e_recv.at[2 + k], me.zs[k]) for k in range(3)]
    for b, (at, block, t, n) in reversed(list(enumerate(coarse_blocks()))):
        pool, shrink = pool_parts(block, t, n)
        kc, vc = mm(pool, kvx[16 + t:16 + t + n, 0:D]) * shrink, mm(pool, kvx[16 + t:16 + t + n, D:2 * D])
        put_coarse(kvx, b, kc.astype(BF16), slice(0, D))
        put_coarse(kvx, b, vc.astype(BF16), slice(D, 2 * D))
        if block == 3:
            wbuf[place] = jnp.concatenate([kc[112:120], vc[112:120]], axis=0).astype(BF16)
            start_all(wide_z)
    step(1, 1, 1)
    for side in range(2):
        for l in range(7):
            at = own_border(side, l)
            k16, v16 = kvx[at:at + 16, 0:D], kvx[at:at + 16, D:2 * D]
            if l == 0:
                msg[side, 0], msg[side, 1] = k16, v16
            else:
                far = [pick_far(side, v.astype(F32)) for v in (k16, v16)]
                msg[side, l + 1] = jnp.concatenate(far, axis=0).astype(BF16)
    to_right = rcopy(msg.at[1], got.at[0], e_send.at[0], e_recv.at[0], me.right)
    to_left = rcopy(msg.at[0], got.at[1], e_send.at[1], e_recv.at[1], me.left)
    four = wbuf.at[pl.ds(4 * me.odd, 4)]
    wide_core = rcopy(four, four, e_send.at[5], e_recv.at[5], me.core)
    not_last, not_first = place < 7, place > 0

    @pl.when(not_last)
    def _():
        to_right.start()

    @pl.when(not_first)
    def _():
        to_left.start()
    step(1, 1, 4)
    step(0, 3, 2, 3)
    project(0)
    for at, block, t, n in coarse_blocks():
        pool, shrink = pool_parts(block, t, n)
        qx[1024 + at:1024 + at + 128, :] = (mm(pool, qx[t:t + n, :]) * shrink).astype(BF16)
    emit(qx, qx_o)
    if near:
        emit(wq, wq_o)
    step(1, 1, 3)
    masks = head_masks(128)

    def tile(g, i):
        keys = slice(tile_at(i), tile_at(i) + tile_keys(i))
        kw, vw = kvx[keys, lanes_of(g)], kvx[keys, lanes_of(g, D)]
        q = by_head(qx[128 * i:128 * i + 128, lanes_of(g)], masks)
        e = jnp.exp(mm_bt(kw, q) + bias_of(bias, i))
        times = tile_times(i)
        z = jnp.sum(e, axis=0, keepdims=True)
        z0_, z1_ = z[:, 0:128] * times, z[:, 128:256] * times
        n = own_blocks(mm_at(vw, e.astype(BF16)))
        if i < 8:
            cols = slice(128 * i, 128 * i + 128)
            n0[g, :, cols] = n
            z0[g, 0:1, cols] = z0_
            z0[g, 1:2, cols] = z1_
        else:
            cols = slice(128 * i - 1024, 128 * i - 896)
            high, low = split(two_rows(z0_, z1_))
            nc[g, :, cols] = jnp.concatenate([n.astype(BF16), high, low], axis=0)

    @pl.loop(0, 4)
    def _(g):
        for k in range(4):
            @pl.when(g == k)
            def _():
                if k == 1:
                    wait_all(wide_z)
                    wide_core.start()
        for i in INNER:
            tile(g, i)

    wide_core.wait()
    w = wbuf[...].reshape(128, D)
    kvx[WIDE_AT:EXT, 0:D] = mm(wide_rows(0), w).astype(BF16)
    kvx[WIDE_AT:EXT, D:2 * D] = mm(wide_rows(1), w).astype(BF16)

    @pl.when(not_last)
    def _():
        to_right.wait_send()
        to_left.wait_recv()

    @pl.when(not_first)
    def _():
        to_left.wait_send()
        to_right.wait_recv()
    for side in range(2):
        m = got[side].reshape(128, D)
        closer = mm(near_rows(side), m)
        m = m.astype(F32)
        for l in range(7):
            at = border(side, l)
            if l == 0:
                k16, v16 = m[0:16], m[16:32]
            else:
                a, b = 16 * (l + 1), 16 * (l - 1)
                k16 = far_and_near(side, m[a:a + 8], closer[b:b + 8])
                v16 = far_and_near(side, m[a + 8:a + 16], closer[b + 8:b + 16])
            kvx[at:at + 16, 0:D] = k16.astype(BF16)
            kvx[at:at + 16, D:2 * D] = v16.astype(BF16)
    emit(kvx, kvx_o)

    @pl.loop(0, 4)
    def _(g):
        for k in range(4):
            @pl.when(g == k)
            def _():
                step(1, 2, *((0, 2), (1,), (), (4,))[k])
        for i in OUTER:
            tile(g, i)
        c_ref = nc.at[g]
        for j in range(TILES):
            cols = slice(TILE * j, TILE * j + TILE)
            r = mm(coarse_cols(c_ref, 0, j), sp[:, cols])
            n = n0[g, :, cols] + r[0:128]
            i0 = 1.0 / (z0[g, 0:1, cols] + r[128:129] + r[144:145])
            i1 = 1.0 / (z0[g, 1:2, cols] + r[129:130] + r[145:146])
            iz[g, 0:1, cols] = i0
            iz[g, 1:2, cols] = i1
            ao[pl.ds(pl.multiple_of(g * 128, 128), 64), cols] = (n[0:64] * i0).astype(BF16)
            ao[pl.ds(pl.multiple_of(g * 128 + 64, 64), 64), cols] = (n[64:128] * i1).astype(BF16)
    emit(ao, ao_o)
    emit(iz, iz_o)
    step(1, 2, 3)
    step(1, 3, 0, 1, 2, 3, 4)
    wait_all(outs)


ANY = pl.BlockSpec(memory_space=pl.ANY)
IN_VMEM = pl.BlockSpec(memory_space=pltpu.VMEM)
S = jax.ShapeDtypeStruct
SEM = pltpu.SemaphoreType.DMA


def forward(near, tok, seg, *params):
    grid = (4, 2, 2, 2)
    shapes = [S((EXT, 2 * D), BF16), S((2048, D), BF16), S((BIASES, 128), F32), S((TOK, D), BF16), S((D, TOK), BF16),
              S((4, 2, TOK), F32), S((512, TOK), BF16), S((TOK, 512), BF16)]
    scratch = [VMEM(s.shape, s.dtype) for s in shapes] + [
        VMEM((TOK, D), F32), VMEM((16, 128), F32), VMEM((4, 128, TOK), F32), VMEM((4, 160, TOK), BF16), VMEM((4, 2, TOK), F32),
        VMEM((EXT, 128), BF16), VMEM(seg.shape, I32), VMEM((2, 8, 16, D), BF16), VMEM((2, 8, 16, D), BF16), VMEM((8, 16, D), BF16),
        SEM((16,)), SEM((7,)), SEM((7,))]
    if near:
        shapes += [S((3,) + grid + (16, D), BF16), S((16, D), F32), S((1, FF), F32)]
        shapes += [S(grid + a.shape, a.dtype) for a in params[9:]]
        scratch += [VMEM((3,) + grid + (16, D), BF16), VMEM((16, D), F32), VMEM((1, FF), F32), VMEM((8, 128), F32),
                    VMEM((4, 8, 8, 128), F32), SEM((16,)), SEM((9, 6)), SEM((9, 6)), SEM((10,)), SEM((10,))]
        specs = [IN_VMEM] * 9 + [ANY] * 3
    else:
        specs = [IN_VMEM] * 2
    return pl.pallas_call(
        functools.partial(forward_kernel, near),
        out_shape=shapes,
        in_specs=[IN_VMEM, IN_VMEM] + specs,
        out_specs=[ANY] * len(shapes),
        scratch_shapes=scratch,
        compiler_params=pltpu.CompilerParams(collective_id=0, has_side_effects=True, vmem_limit_bytes=60 << 20),
        name="forward",
    )(tok, seg, *params)


C0 = 0.7978845608028654
C1 = 0.044715


def middle_kernel(tok, ao, cot, wo, w1, w2, vecs, b1, out, dh1_out, da_out, gwo, gw1, gw2, gvec, gb1,
                  awo, aw1, aw2, avec, ab1):
    j = pl.program_id(0)

    @pl.when(j == 0)
    def _():
        awo[...] = jnp.zeros_like(awo)
        aw1[...] = jnp.zeros_like(aw1)
        aw2[...] = jnp.zeros_like(aw2)
        avec[...] = jnp.zeros_like(avec)
        ab1[...] = jnp.zeros_like(ab1)
    mixed = ao[...]
    h1 = tok[...].astype(F32) + mm_at(mixed, wo[...]) + vecs[5:6, :]
    center = h1 - jnp.mean(h1, axis=-1, keepdims=True)
    inverse = lax.rsqrt(jnp.mean(center * center, axis=-1, keepdims=True) + EPS)
    xh = center * inverse
    gain = vecs[6:7, :]
    a2 = (xh * gain + vecs[7:8, :]).astype(BF16)
    dy = cot[...]
    y = h1 + vecs[8:9, :]
    da2 = jnp.zeros((512, D), F32)
    for k in range(FF // D):
        cols = slice(D * k, D * k + D)
        u = mm(a2, w1[:, cols]) + b1[:, cols]
        u2 = u * u
        th = jnp.tanh(u * (C0 + (C0 * C1) * u2))
        half = 0.5 * (1.0 + th)
        g = (u * half).astype(BF16)
        slope = half + 0.5 * u * (1.0 - th * th) * (C0 + (3.0 * C0 * C1) * u2)
        y = y + mm(g, w2[cols, :])
        du = (mm_bt(dy, w2[cols, :]) * slope).astype(BF16)
        aw2[cols, :] += mm_at(g, dy)
        aw1[:, cols] += mm_at(a2, du)
        ab1[:, cols] += jnp.sum(du.astype(F32), axis=0, keepdims=True)
        da2 = da2 + mm_bt(du, w1[:, cols])
    out[...] = y.astype(BF16)
    dyf = dy.astype(F32)
    e = da2 * gain
    dh1 = dyf + inverse * (e - jnp.mean(e, axis=-1, keepdims=True) - xh * jnp.mean(e * xh, axis=-1, keepdims=True))
    dh1_out[...] = dh1
    db = dh1.astype(BF16)
    awo[...] += mm(mixed, db)
    da_out[...] = mm_bt(wo[...], db).astype(BF16)
    avec[5:6, :] += jnp.sum(db.astype(F32), axis=0, keepdims=True)
    avec[6:7, :] += jnp.sum(da2 * xh, axis=0, keepdims=True)
    avec[7:8, :] += jnp.sum(da2, axis=0, keepdims=True)
    avec[8:9, :] += jnp.sum(dyf, axis=0, keepdims=True)

    @pl.when(j == TOK // 512 - 1)
    def _():
        gwo[...] = awo[...].astype(BF16)
        gw1[...] = aw1[...].astype(BF16)
        gw2[...] = aw2[...].astype(BF16)
        gvec[...] = avec[...]
        gb1[...] = ab1[...]


def whole(shape):
    return pl.BlockSpec(shape, lambda j: (0,) * len(shape), pipeline_mode=pl.Buffered(1))


def middle(tok, ao, cot, wo, w1, w2, vecs, b1):
    tile = pl.BlockSpec((512, D), lambda j: (j, 0))
    flat = pl.BlockSpec((D, 512), lambda j: (0, j))
    return pl.pallas_call(
        middle_kernel,
        grid=(TOK // 512,),
        out_shape=[S((TOK, D), BF16), S((TOK, D), F32), S((D, TOK), BF16), S((D, D), BF16), S((D, FF), BF16), S((FF, D), BF16),
                   S((16, D), F32), S((1, FF), F32)],
        in_specs=[tile, flat, tile, whole((D, D)), whole((D, FF)), whole((FF, D)), whole((16, D)), whole((1, FF))],
        out_specs=[tile, tile, flat, whole((D, D)), whole((D, FF)), whole((FF, D)), whole((16, D)), whole((1, FF))],
        scratch_shapes=[VMEM((D, D), F32), VMEM((D, FF), F32), VMEM((FF, D), F32), VMEM((16, D), F32), VMEM((1, FF), F32)],
        compiler_params=pltpu.CompilerParams(dimension_semantics=("arbitrary",), vmem_limit_bytes=60 << 20),
        name="middle",
    )(tok, ao, cot, wo, w1, w2, vecs, b1)


def pack_small(rows, b1):
    row, n = iota((256, D), 0), iota((256, D), 1)
    lane, col = iota((128, D), 0), iota((128, D), 1)
    mine = (row >> 3) == (n >> 4)

    def moved(v, ok, ones):
        total = None
        for part in split3(jnp.where(ok, v, 0.0)):
            r = mm_bt(part, ones)
            total = r if total is None else total + r
        return total
    eight = jnp.broadcast_to(rows[0:8][None], (32, 8, D)).reshape(256, D)
    out = moved(eight, mine, ones_where(lane == (col & 15)))
    out = out + moved(jnp.broadcast_to(rows[8:9], (256, D)), mine & ((row & 7) == 0), ones_where(lane == (col & 15) + 16))
    last = ones_where(lane == (col & 7) + 32)
    for q in range(4):
        ok = ((row >> 3) == ((n + 512 * q) >> 6)) & ((row & 7) == ((n >> 3) & 7))
        out = out + moved(jnp.broadcast_to(b1[0:1, D * q:D * q + D], (256, D)), ok, last)
    return out.reshape(4, 8, 8, 128)


def backward_kernel(near, *refs):
    refs = list(refs)

    def take(n):
        out = refs[:n]
        del refs[:n]
        return out
    ins = take(13)
    gffn, (gvec, gb1) = take(3), take(2)
    tok_o, gq_o = take(2)
    small_o = take(8 if near else 1)
    gffn_o = take(3 if near else 0)
    kvx, qx, bias, a1, ao, iz, sp, spt, da, tok, dh1, wq, vecs = take(13)
    gr, rm, dqt, dkv, dq, edge, e_got, w_all, w_got, w_mid, gq, avec, tok_s, dall, in_sem, out_sem, e_send, e_recv = take(18)
    if near:
        gv, f_mine, f_sem, send, recv, send_v, recv_v, v_got, v_sum, v_z = take(10)
        bufs = [take(4) for _ in range(11)]
    me = Peers(near)
    place = me.place
    loads = {}
    targets = (da, ao, iz, sp, kvx, qx, bias, spt, a1, tok, dh1, wq, vecs)
    names = ("da", "ao", "iz", "sp", "kvx", "qx", "bias", "spt", "a1", "tok", "dh1", "wq", "vecs")
    for k, name in enumerate(names):
        loads[name] = pltpu.make_async_copy(ins[k], targets[k], in_sem.at[k])
        loads[name].start()
    greet(me.greeted)
    mine_copies = []
    if near:
        for k in range(3):
            cp = pltpu.make_async_copy(gffn[k].at[:, :, :, me.c], f_mine[k], f_sem.at[k])
            cp.start()
            mine_copies.append(cp)
        every = slice(None)
        ffn = [Scatter(me, lambda c, k=k: ffn_view(gffn, k, (every, every, every, c)), lambda h, y, x, k=k: ffn_values(f_mine, k, (h, y, x)),
                       k in (2, 4), bufs[k], send.at[k], recv.at[k]) for k in range(5)]
        last = []
        for k in range(6):
            lo = 256 * (k % 2)
            last.append(Scatter(me, lambda c, k=k, lo=lo: gq.at[k // 2, :, :, :, c, :, pl.ds(lo, 256)],
                                lambda h, y, x, k=k, lo=lo: gq[k // 2, h, y, x, me.c, :, lo:lo + 256], k % 2 == 1,
                                bufs[5 + k], send.at[5 + k], recv.at[5 + k]))
        small_s = SmallScatter(me, gv, v_got, v_sum, v_z, send_v, recv_v)
        for a in ffn:
            a.start(0)

    def put_ffn(k):
        which, tail = ffn_index(k, lambda at, n: slice(at, at + n))
        gffn_o[which][tail or (slice(None),)] = ffn[k].result()

    def put_last(k):
        gq_o[k // 2, :, 256 * (k % 2):256 * (k % 2) + 256] = last[k].result()

    def step(group, stage, *pieces):
        if not near:
            return
        for k in pieces:
            a = (ffn if group == 0 else last)[k]
            a.wait(stage)
            if stage < 3:
                a.add(stage)
                a.start(stage + 1)
            elif group == 0:
                put_ffn(k)
            else:
                put_last(k)

    for name in ("da", "ao", "iz", "sp"):
        loads[name].wait()
    masks = head_masks(128)

    @pl.loop(0, 4)
    def _(g):
        lo, hi = pl.ds(pl.multiple_of(g * 128, 128), 64), pl.ds(pl.multiple_of(g * 128 + 64, 64), 64)
        for j in range(TILES):
            cols = slice(TILE * j, TILE * j + TILE)
            g0 = da[lo, cols].astype(F32) * iz[g, 0:1, cols]
            g1 = da[hi, cols].astype(F32) * iz[g, 1:2, cols]
            r0 = jnp.sum(g0 * ao[lo, cols].astype(F32), axis=0, keepdims=True)
            r1 = jnp.sum(g1 * ao[hi, cols].astype(F32), axis=0, keepdims=True)
            rm[g, 0:1, cols] = r0
            rm[g, 1:2, cols] = r1
            high, low = split(two_rows(r0, r1))
            gr[g, :, cols] = jnp.concatenate([g0.astype(BF16), g1.astype(BF16), high, low], axis=0)
        for b, (at, block, t, n) in enumerate(coarse_blocks()):
            x = mm_bt(gr[g, :, t:t + n], sp[128 * block:128 * block + 128, t:t + n])
            cols = slice(1024 + at, 1152 + at)
            gr[g, 0:128, cols] = x[0:128].astype(BF16)
            times = tile_times(8 + b)
            rm[g, 0:1, cols] = (x[128:129] + x[144:145]) * times
            rm[g, 1:2, cols] = (x[129:130] + x[145:146]) * times
    dkv[...] = jnp.zeros_like(dkv)
    for name in ("kvx", "qx", "bias"):
        loads[name].wait()
    zero = jnp.zeros((64, 128), BF16)

    def tile(g, i):
        keys = slice(tile_at(i), tile_at(i) + tile_keys(i))
        cols = slice(128 * i, 128 * i + 128)
        kw, vw = kvx[keys, lanes_of(g)], kvx[keys, lanes_of(g, D)]
        q = by_head(qx[cols, lanes_of(g)], masks)
        gt = gr[g, 0:128, cols]
        gb = jnp.concatenate([jnp.concatenate([gt[0:64], zero], axis=1), jnp.concatenate([zero, gt[64:128]], axis=1)], axis=0)
        e = jnp.exp(mm_bt(kw, q) + bias_of(bias, i))
        rest = jnp.concatenate([rm[g, 0:1, cols], rm[g, 1:2, cols]], axis=1)
        ds = (e * (mm(vw, gb) - rest)).astype(BF16)
        dkv[keys, lanes_of(g)] += mm(ds, q)
        dkv[keys, lanes_of(g, D)] += mm_bt(e.astype(BF16), gb)
        dqt[g, :, cols] = (own_blocks(mm_at(kw, ds)) * (0.125 / tile_times(i))).astype(BF16)

    if near:
        wait_all(mine_copies)
    step(0, 0, 0, 1, 2, 3, 4)

    @pl.loop(0, 4)
    def _(g):
        for i in OUTER:
            tile(g, i)
    for side in range(2):
        base, closer = [], []
        for l in range(7):
            at = border(side, l)
            k16, v16 = dkv[at:at + 16, 0:D], dkv[at:at + 16, D:2 * D]
            if l == 0:
                base += [k16, v16]
            elif side == 0:
                base += [k16[0:8], v16[0:8]]
                closer += [k16[8:16], v16[8:16]]
            else:
                base += [k16[8:16], v16[8:16]]
                closer += [k16[0:8], v16[0:8]]
        folded = mm_at(near_rows(side), jnp.concatenate(closer, axis=0).astype(BF16))
        edge[side] = (jnp.concatenate(base, axis=0) + folded).astype(BF16).reshape(8, 16, D)
    d_wide = mm_at(wide_rows(0), dkv[WIDE_AT:EXT, 0:D].astype(BF16)) + mm_at(wide_rows(1), dkv[WIDE_AT:EXT, D:2 * D].astype(BF16))
    w_all[...] = d_wide.astype(BF16).reshape(8, 16, D)
    to_right = rcopy(edge.at[1], e_got.at[0], e_send.at[0], e_recv.at[0], me.right)
    to_left = rcopy(edge.at[0], e_got.at[1], e_send.at[1], e_recv.at[1], me.left)
    wide_core = rcopy(w_all.at[pl.ds(4 * (1 - me.odd), 4)], w_mid, e_send.at[2], e_recv.at[2], me.core)
    not_last, not_first = place < 7, place > 0
    wide_core.start()

    @pl.when(not_last)
    def _():
        to_right.start()

    @pl.when(not_first)
    def _():
        to_left.start()
    step(0, 1, 0, 1, 2)

    @pl.loop(0, 2)
    def _(g):
        for i in INNER:
            tile(g, i)
    wide_core.wait()
    for k in range(4):
        w_mid[k] = (w_mid[k].astype(F32) + w_all[4 * me.odd + k].astype(F32)).astype(BF16)
    wide_z = [rcopy(w_mid.at[me.z_index[k]], w_got.at[k], e_send.at[3 + k], e_recv.at[3 + k], me.zs[k]) for k in range(3)]
    start_all(wide_z)

    @pl.loop(2, 4)
    def _(g):
        for i in INNER:
            tile(g, i)
    step(0, 1, 3, 4)

    @pl.loop(0, 4)
    def _(g):
        d_ref = dqt.at[g]
        eye = identity(TILE)
        for j in range(TILES):
            cols = slice(TILE * j, TILE * j + TILE)
            r = d_ref[:, cols].astype(F32) + mm(coarse_cols(d_ref, 1024, j), sp[:, cols])
            dq[cols, lanes_of(g)] = mm_bt(eye, r.astype(BF16)).astype(BF16)
    for name in ("spt", "a1", "tok", "dh1", "wq", "vecs"):
        loads[name].wait()
    avec[...] = jnp.zeros_like(avec)

    def projection_grad(c, d):
        aw = mm_at(a1[...], d).astype(BF16)
        avec[2 + c:3 + c, :] = jnp.sum(d.astype(F32), axis=0, keepdims=True)
        gq[c] = aw.reshape(4, 2, 2, 2, 16, D)
        if near:
            for a in last[2 * c:2 * c + 2]:
                a.start(0)
    projection_grad(0, dq[...])
    step(0, 2, 0, 1, 2)
    for cp in wide_z:
        cp.wait()

    def add_edge(side):
        m = e_got[side].reshape(128, D).astype(F32)
        for l in range(7):
            if l == 0:
                at, n = own_border(side, 0), 16
            else:
                at, n = own_border(side, l) + (0 if side else 8), 8
            a = 16 * (l + 1) if l else 0
            dkv[at:at + n, 0:D] += m[a:a + n]
            dkv[at:at + n, D:2 * D] += m[a + n:a + 2 * n]

    @pl.when(not_last)
    def _():
        to_right.wait_send()
        to_left.wait_recv()
        add_edge(1)

    @pl.when(not_first)
    def _():
        to_left.wait_send()
        to_right.wait_recv()
        add_edge(0)
    v = w_mid[me.h].astype(F32)
    for k in range(3):
        v = v + w_got[k].astype(F32)
    v = jnp.concatenate([v[0:8] * 0.5 ** 7, v[8:16]], axis=1)
    w_own = jnp.concatenate([v, jnp.zeros((8, 2 * D), F32)], axis=0).astype(BF16)
    lane_all = iota((1, 2 * D), 1)

    def coarse_rows(at, n, level):
        return (dkv[at:at + n, :] * jnp.where(lane_all < D, 0.5 ** level, 1.0)).astype(BF16)
    top = jnp.concatenate([coarse_rows(EXT_AT[3] + 16, 128, 3), coarse_rows(EXT_AT[4] + 16, 64, 4), coarse_rows(EXT_AT[5] + 16, 32, 5),
                           coarse_rows(EXT_AT[6] + 16, 16, 6), w_own], axis=0)
    for j in range(TILES):
        rows = slice(TILE * j, TILE * j + TILE)
        x = jnp.concatenate([coarse_rows(EXT_AT[1] + 16 + 128 * j, 128, 1), coarse_rows(EXT_AT[2] + 16 + 128 * (j // 2), 128, 2), top], axis=0)
        dall[rows, :] = (dkv[16 + TILE * j:16 + TILE * j + TILE, :] + mm(spt[rows, :], x)).astype(BF16)
    projection_grad(1, dall[:, 0:D])
    step(0, 2, 3, 4)
    step(1, 0, 0, 1)
    projection_grad(2, dall[:, D:2 * D])
    step(1, 0, 2, 3)
    @pl.loop(0, TILES)
    def _(j):
        rows = pl.ds(pl.multiple_of(TILE * j, TILE), TILE)
        da1 = mm_bt(dq[rows, :], wq[0].reshape(D, D)) + mm_bt(dall[rows, 0:D], wq[1].reshape(D, D)) + mm_bt(dall[rows, D:2 * D], wq[2].reshape(D, D))
        v = tok[rows, :].astype(F32)
        center = v - jnp.mean(v, axis=-1, keepdims=True)
        inverse = lax.rsqrt(jnp.mean(center * center, axis=-1, keepdims=True) + EPS)
        n = center * inverse
        e = da1 * vecs[0:1, :]
        dv = inverse * (e - jnp.mean(e, axis=-1, keepdims=True) - n * jnp.mean(e * n, axis=-1, keepdims=True))
        tok_s[rows, :] = (dh1[rows, :] + dv).astype(BF16)
        avec[0:1, :] += jnp.sum(da1 * n, axis=0, keepdims=True)
        avec[1:2, :] += jnp.sum(da1, axis=0, keepdims=True)
        for k, what in enumerate(((0, 4, 5), (1, 0, 1), (1, 2, 3))):
            @pl.when(j == k)
            def _():
                step(1, *what)
    done = pltpu.make_async_copy(tok_s, tok_o, out_sem.at[0])
    done.start()
    if not near:
        gq_o[...] = gq[...]
        small_o[0][...] = avec[...]
        done.wait()
        return
    avec[5:9, :] = gvec[5:9, :]
    gv[...] = pack_small(avec[...], gb1)
    start_all(small_s.first())
    step(1, 1, 4, 5)
    step(1, 2, 0, 1)
    wait_all(small_s.first())
    small_s.add()
    start_all(small_s.second())
    step(1, 2, 2, 3, 4, 5)
    step(0, 3, 0, 1, 2, 3, 4)
    step(1, 3, 0, 1, 2, 3, 4, 5)
    wait_all(small_s.second())
    t = small_s.result()
    for k, r in enumerate((0, 1, None, 5, 6, 7)):
        if r is None:
            small_o[k][...] = t[2:5, 0:16]
        else:
            small_o[k][...] = t[r:r + 1, 0:16]
    for r in range(8):
        small_o[6][0:1, 8 * r:8 * r + 8] = t[r:r + 1, 32:40]
    small_o[7][...] = t[0:1, 16:32]
    done.wait()


def backward(near, saved, wq, vecs, tok, da, dh1, gffn, gvec, gb1):
    kvx, qx, bias, a1, ao, iz, sp, spt = saved
    grid = (4, 2, 2, 2)
    vm = [VMEM(v.shape, v.dtype) for v in (kvx, qx, bias, a1, ao, iz, sp, spt, da, tok, dh1, wq, vecs)]
    scratch = vm + [VMEM((4, 160, 2048), BF16), VMEM((4, 2, 2048), F32), VMEM((4, 128, 2048), BF16), VMEM((EXT, 2 * D), F32),
                    VMEM((TOK, D), BF16), VMEM((2, 8, 16, D), BF16), VMEM((2, 8, 16, D), BF16), VMEM((8, 16, D), BF16),
                    VMEM((3, 16, D), BF16), VMEM((4, 16, D), BF16), VMEM((3,) + grid + (16, D), BF16), VMEM((16, D), F32), VMEM((TOK, D), BF16), VMEM((TOK, 2 * D), BF16),
                    SEM((13,)), SEM((1,)), SEM((6,)), SEM((6,))]
    if near:
        gffn = [g.reshape(grid + (g.shape[0] // 32, g.shape[1])) for g in gffn]
        shapes = [S((TOK, D), BF16), S((3, 16, D), F32)]
        shapes += [S((1, 16), F32), S((1, 16), F32), S((3, 16), F32), S((1, 16), F32), S((1, 16), F32), S((1, 16), F32), S((1, 64), F32), S((1, 16), F32)]
        shapes += [S(g.shape[4:], F32) for g in gffn]
        pieces = [(shape, BF16) for shape in FFN_SHAPES] + [((16, 256), BF16)] * 6
        scratch += [VMEM((4, 8, 8, 128), F32), [VMEM((4, 2, 2) + g.shape[4:], BF16) for g in gffn], SEM((3,)), SEM((11, 6)), SEM((11, 6)),
                    SEM((10,)), SEM((10,)), VMEM((7, 4, 8, 128), F32), VMEM((4, 8, 128), F32), VMEM((3, 8, 128), F32)]
        for shape, kind in pieces:
            scratch += scatter_bufs(shape, kind)
    else:
        gffn = gffn[0:3]
        shapes = [S((TOK, D), BF16), S((3,) + grid + (16, D), BF16), S((16, D), F32)]
    ordered = (da, ao, iz, sp, kvx, qx, bias, spt, a1, tok, dh1, wq, vecs)
    return pl.pallas_call(
        functools.partial(backward_kernel, near),
        out_shape=shapes,
        in_specs=[ANY] * 16 + [IN_VMEM] * 2,
        out_specs=[ANY] + [IN_VMEM] * (len(shapes) - 1),
        scratch_shapes=scratch,
        compiler_params=pltpu.CompilerParams(collective_id=1, has_side_effects=True, vmem_limit_bytes=62 << 20),
        name="backward",
    )(*ordered, *gffn, gvec, gb1)


def finish_kernel(n, *refs):
    for k in range(n):
        refs[n + k][...] = refs[k][...]


def finish(*values):
    n = len(values)
    return pl.pallas_call(
        functools.partial(finish_kernel, n),
        out_shape=[S(v.shape, v.dtype) for v in values],
        in_specs=[IN_VMEM] * n,
        out_specs=[IN_VMEM] * n,
        name="finish",
    )(*values)


BOTH = ("head", "span")


def shards(tokens, segment_ids, first_gain, first_shift, project_weight, project_bias, output_weight, output_bias,
           second_gain, second_shift, expand_weight, expand_bias, reduce_weight, reduce_bias, cotangent):
    tok, cot = tokens[0], cotangent[0]
    near = lax.axis_size("head") == 4 and lax.axis_size("span") == 8
    if near:
        vectors = (first_gain, first_shift, project_bias, output_bias, second_gain, second_shift, reduce_bias, expand_bias)
        vectors = [v if v.ndim == 2 else v[None] for v in vectors]
        *saved, wq, vecs, b1, wo, w1, w2 = forward(True, tok, segment_ids, project_weight, *vectors, output_weight, expand_weight, reduce_weight)
        wo, w1, w2 = wo.reshape(D, D), w1.reshape(D, FF), w2.reshape(FF, D)
    else:
        def full(v, axis=0):
            return lax.all_gather(v, BOTH, axis=axis, tiled=True)
        wq, wo, w1, w2 = full(project_weight, 1), full(output_weight), full(expand_weight), full(reduce_weight)
        rows = [full(first_gain), full(first_shift), *full(project_bias, 1), full(output_bias), full(second_gain), full(second_shift), full(reduce_bias)]
        vecs = jnp.pad(jnp.stack(rows), ((0, 7), (0, 0)))
        b1 = full(expand_bias)[None]
        saved = forward(False, tok, segment_ids, wq, vecs)
    ao = saved[4]
    out, dh1, da, *gffn, gvec, gb1 = middle(tok, ao, cot, wo, w1, w2, vecs, b1)
    dtok, gwq, *rest = backward(near, saved, wq, vecs, tok, da, dh1, gffn, gvec, gb1)
    if near:
        dtok, gwq, *rest = finish(dtok, gwq, *rest)
        small, (gwo, gw1, gw2) = rest[0:8], rest[8:11]
        small = [v if v.shape[0] == 3 else v.reshape(-1) for v in small]
    else:
        def part(v, axis=0):
            return lax.psum_scatter(v.astype(F32), BOTH, scatter_dimension=axis, tiled=True)
        vec, gwq = rest[0], gwq.reshape(3, D, D)
        gwq, gwo, gw1, gw2 = part(gwq, 1), part(gffn[0]), part(gffn[1]), part(gffn[2])
        small = (part(vec[0]), part(vec[1]), part(vec[2:5], 1), part(gvec[5]), part(gvec[6]), part(gvec[7]), part(gb1[0]), part(gvec[8]))
    return (out[None], dtok[None], small[0], small[1], gwq, small[2], gwo, small[3], small[4], small[5], gw1, small[6], gw2, small[7])


def solution(mesh):
    token, row, matrix = P("span", "head", None), P(BOTH), P(BOTH, None)
    three, bias = P(None, BOTH, None), P(None, BOTH)
    params = (row, row, three, bias, matrix, row, row, row, matrix, row, matrix, row)
    return jax.shard_map(shards, mesh=mesh, in_specs=(token, P("span", None)) + params + (token,),
                         out_specs=(token, token) + params, check_vma=False)
```

```python
import functools
import jax
import jax.numpy as jnp
from jax import lax
from jax.experimental import pallas as pl
from jax.experimental.pallas import tpu as pltpu
from jax.sharding import PartitionSpec as P

F32, BF16, I32 = jnp.float32, jnp.bfloat16, jnp.int32
MESH = pl.DeviceIdType.MESH
VMEM = pltpu.VMEM
NEG = -1e30
EPS = 1e-5
TOK = 1024
TILE = 256
D = 512
FF = 2048
EXT = 2384
SIZES = (1024, 512, 256, 128, 64, 32, 16)
EXT_AT = (0, 1056, 1600, 1888, 2048, 2144, 2208)
WIDE_AT = 2256
TRANS_B = (((1,), (1,)), ((), ()))
TRANS_A = (((0,), (0,)), ((), ()))


def mm(a, b):
    return jnp.dot(a, b, preferred_element_type=F32)


def mm_bt(a, b):
    return lax.dot_general(a, b, TRANS_B, preferred_element_type=F32)


def mm_at(a, b):
    return lax.dot_general(a, b, TRANS_A, preferred_element_type=F32)


def iota(shape, dim):
    return lax.broadcasted_iota(I32, shape, dim)


def split(v):
    high = v.astype(BF16)
    return high, (v - high.astype(F32)).astype(BF16)


def covers(t, c, block):
    if block == 0:
        return ((t & 255) >> 1) == c
    if block == 1:
        return ((t & 511) >> 2) == c
    if block == 2:
        return (t >> 3) == c
    level, start = mixed_levels(c)
    return (jnp.right_shift(t, level) == c - start) & (c < 124)


def mixed_levels(c):
    a, b, d, e = ((c >= edge).astype(I32) for edge in (64, 96, 112, 120))
    return 4 + a + b + d + e, 64 * a + 32 * b + 16 * d + 8 * e


def ones_where(cond):
    return jnp.where(cond, 1.0, 0.0).astype(BF16)


def identity(n):
    return ones_where(iota((n, n), 0) == iota((n, n), 1))


def fill_spread(spt):
    @pl.loop(0, TOK // TILE)
    def _(j):
        for block in range(4):
            t = iota((TILE, 128), 0) + j * TILE
            c = iota((TILE, 128), 1)
            spt[pl.ds(j * TILE, TILE), 128 * block:128 * block + 128] = ones_where(covers(t, c, block))


def fill_pool(sp):
    @pl.loop(0, TOK // TILE)
    def _(j):
        for block in range(4):
            t = iota((128, TILE), 1) + j * TILE
            c = iota((128, TILE), 0)
            sp[128 * block:128 * block + 128, pl.ds(pl.multiple_of(j * TILE, TILE), TILE)] = ones_where(covers(t, c, block))


TILES = TOK // TILE
BIAS_MIXED = 15 * 160
BIASES = BIAS_MIXED + 336


def tile_level(i):
    return 0 if i < 8 else 1 if i < 12 else 2 if i < 14 else 3


def tile_at(i):
    return 2048 if i == 15 else 128 * i + 32 * tile_level(i)


def tile_keys(i):
    return 336 if i == 15 else 160


def tile_times(i):
    if i < 15:
        return float(2 ** tile_level(i))
    level, _unused = mixed_levels(iota((1, 128), 1))
    return (1 << level).astype(F32)


INNER = (1, 2, 3, 4, 5, 6, 9, 10)
OUTER = (0, 7, 8, 11, 12, 13, 14, 15)


def labels_of(total, squares, times):
    return jnp.where(times * squares == total * total, total / times, 0.0)


def head_masks(rows):
    lane = iota((rows, 128), 1)
    return ones_where(lane < 64), ones_where(lane >= 64)


def by_head(x, masks):
    return jnp.concatenate([x * masks[0], x * masks[1]], axis=0)


def own_blocks(x):
    return jnp.concatenate([x[0:64, 0:128], x[64:128, 128:256]], axis=0)


def twice(x):
    return jnp.concatenate([x, x], axis=1)


def two_rows(a, b):
    row = iota((16, a.shape[1]), 0)
    return jnp.where(row == 0, a, jnp.where(row == 1, b, 0.0))


def lanes_of(g, base=0):
    return pl.ds(pl.multiple_of(base + g * 128, 128), 128)


def coarse_cols(ref, base, j):
    return jnp.concatenate([ref[:, base + 128 * j:base + 128 * j + 128],
                            ref[:, base + 512 + 128 * (j // 2):base + 640 + 128 * (j // 2)],
                            ref[:, base + 768:base + 1024]], axis=1)


def coarse_blocks():
    return ([(128 * j, 0, 256 * j, 256) for j in range(4)] + [(512 + 128 * j, 1, 512 * j, 512) for j in range(2)]
            + [(768, 2, 0, 1024), (896, 3, 0, 1024)])


def near_rows(side):
    o, i = iota((96, 128), 0), iota((96, 128), 1)
    level = (o >> 4) + 1
    block = i >> 4
    fine = jnp.maximum(block - 1, 0)
    value_out, value_in = (o >> 3) & 1, jnp.where(block < 2, block, (i >> 3) & 1)
    width, size = jnp.left_shift(1, fine), jnp.left_shift(1, level)
    if side == 0:
        start = ((o & 7) - 8) * size
        at = jnp.where(block < 2, (i & 15) - 16, (i & 7) - 16) * width
    else:
        start = (o & 7) * size
        at = jnp.where(block < 2, i & 15, (i & 7) + 8) * width
    inside = (value_out == value_in) & (at >= start) & (at + width <= start + size)
    share = jnp.where(value_out == 1, 1.0, width.astype(F32) / size.astype(F32))
    return jnp.where(inside, share, 0.0).astype(BF16)


def wide_rows(value):
    r, i = iota((128, 128), 0), iota((128, 128), 1)
    k, j = r & 15, (i & 15) - 8 * value
    own = ((r >> 4) == (i >> 4)) & (j >= 0) & (j < 8)
    fine, rough = own & (k < 8) & (j == k), own & (k >= 8) & (k < 12) & ((j >> 1) == k - 8)
    return jnp.where(fine, 1.0, jnp.where(rough, 1.0 if value else 0.5, 0.0)).astype(BF16)


def far_and_near(side, far, near):
    return jnp.concatenate([far, near] if side == 0 else [near, far], axis=0)


def border(side, l):
    return EXT_AT[l] + (16 + SIZES[l] if side else 0)


def own_border(side, l):
    return EXT_AT[l] + (SIZES[l] if side else 16)


def pick_far(side, rows):
    return rows[0:8] if side else rows[8:16]


def column_of(row, n):
    spread = jnp.where(iota((n, n), 0) == iota((n, n), 1), jnp.broadcast_to(row, (n, n)), 0.0)
    return jnp.broadcast_to(jnp.sum(spread, axis=1, keepdims=True), (n, 128)).astype(BF16)


def where_am_i():
    h = lax.axis_index("head")
    s = lax.axis_index("span")
    return h, s, s // 4, (s // 2) % 2, s % 2


class Peers:
    def __init__(self, near):
        h, s = lax.axis_index("head"), lax.axis_index("span")
        odd = s % 2
        self.place = odd * 4 + h
        self.odd = odd
        self.h = h
        other = s + 1 - 2 * odd
        self.z_index = [lax.rem(h + d, 4) for d in (1, 2, 3)]
        self.zs = [{"head": z} for z in self.z_index]
        self.core = {"span": other}
        opposite = {"head": 3 - h, "span": other}
        step = 1 - 2 * odd
        self.right = {"head": lax.rem(h + 1, 4), "span": s + step * ((h + 1) // 4)}
        self.left = {"head": lax.rem(h + 3, 4), "span": s + step * (1 - (h + 3) // 4)}
        self.greeted = self.zs + [self.core, opposite]
        if near:
            y, x = s // 4, (s // 2) % 2
            self.y, self.x, self.c = y, x, odd
            self.s = s
            self.px = {"span": y * 4 + (1 - x) * 2 + odd}
            self.py = {"span": (1 - y) * 4 + x * 2 + odd}
            self.s_index = [lax.rem(s + d, 8) for d in range(1, 8)]
            self.spans = [{"span": o} for o in self.s_index]
            self.greeted = self.zs + self.spans + [opposite]


def greet(devices):
    barrier = pltpu.get_barrier_semaphore()
    for d in devices:
        pl.semaphore_signal(barrier, inc=1, device_id=d, device_id_type=MESH)
    pl.semaphore_wait(barrier, len(devices))


def rcopy(src, dst, send, recv, device):
    return pltpu.make_async_remote_copy(src_ref=src, dst_ref=dst, send_sem=send, recv_sem=recv,
                                        device_id=device, device_id_type=MESH)


class Gather:
    def __init__(self, me, shard, full, swap, local, send, recv):
        self.me, self.shard, self.full, self.swap, self.local, self.send, self.recv = me, shard, full, swap, local, send, recv

    def own(self):
        m = self.me
        return pltpu.make_async_copy(self.shard, self.full(m.h, m.y, m.x, m.c), self.local)

    def hop(self, k):
        m, a = self.me, slice(None)
        if k < 3:
            return rcopy(self.shard, self.full(m.h, m.y, m.x, m.c), self.send.at[k], self.recv.at[k], m.zs[k])
        if k == 3:
            ref, dev = self.full(a, m.y, m.x, m.c), m.py if self.swap else m.px
        elif k == 4:
            ref, dev = (self.full(a, a, m.x, m.c), m.px) if self.swap else (self.full(a, m.y, a, m.c), m.py)
        else:
            ref, dev = self.full(a, a, a, m.c), m.core
        return rcopy(ref, ref, self.send.at[k], self.recv.at[k], dev)

    def start(self, stage):
        if stage == 0:
            self.own().start()
            for k in range(3):
                self.hop(k).start()
        else:
            self.hop(2 + stage).start()

    def wait(self, stage):
        if stage == 0:
            self.own().wait()
            for k in range(3):
                self.hop(k).wait()
        else:
            self.hop(2 + stage).wait()


class Scatter:
    def __init__(self, me, grad, mine, swap, bufs, send, recv):
        self.me, self.grad, self.mine, self.swap, self.bufs, self.send, self.recv = me, grad, mine, swap, bufs, send, recv

    def hops(self, stage):
        m, s, r = self.me, self.send, self.recv
        r1, r2, r3, r4 = self.bufs
        if stage == 0:
            return [rcopy(self.grad(1 - m.c), r1, s.at[0], r.at[0], m.core)]
        if stage == 1:
            src, dev = (r1.at[:, 1 - m.y], m.py) if self.swap else (r1.at[:, :, 1 - m.x], m.px)
            return [rcopy(src, r2, s.at[1], r.at[1], dev)]
        if stage == 2:
            src, dev = (r2.at[:, 1 - m.x], m.px) if self.swap else (r2.at[:, 1 - m.y], m.py)
            return [rcopy(src, r3, s.at[2], r.at[2], dev)]
        return [rcopy(r3.at[m.z_index[k]], r4.at[k], s.at[3 + k], r.at[3 + k], m.zs[k]) for k in range(3)]

    def start(self, stage):
        for cp in self.hops(stage):
            cp.start()

    def wait(self, stage):
        for cp in self.hops(stage):
            cp.wait()

    def add(self, stage):
        m = self.me
        r1, r2, r3, r4 = self.bufs

        def into(dst, key, other):
            dst[key] = (dst[key].astype(F32) + other.astype(F32)).astype(dst.dtype)
        if stage == 0:
            @pl.loop(0, 4)
            def _(hh):
                for yy in range(2):
                    for xx in range(2):
                        into(r1, (hh, yy, xx), self.mine(hh, yy, xx))
        elif stage == 1:
            @pl.loop(0, 4)
            def _(hh):
                for v in range(2):
                    into(r2, (hh, v), r1[hh, m.y, v] if self.swap else r1[hh, v, m.x])
        else:
            @pl.loop(0, 4)
            def _(hh):
                into(r3, (hh,), r2[hh, m.x if self.swap else m.y])

    def result(self):
        r1, r2, r3, r4 = self.bufs
        acc = r3[self.me.h].astype(F32)
        for k in range(3):
            acc = acc + r4[k].astype(F32)
        return acc


class SmallGather:
    def __init__(self, me, tile, full, local, send, recv):
        self.me, self.tile, self.full, self.local, self.send, self.recv = me, tile, full, local, send, recv

    def first(self):
        dst = self.full.at[self.me.h, self.me.s]
        return [rcopy(self.tile, dst, self.send.at[k], self.recv.at[k], self.me.zs[k]) for k in range(3)]

    def second(self):
        ref = self.full.at[:, self.me.s]
        return [rcopy(ref, ref, self.send.at[3 + k], self.recv.at[3 + k], self.me.spans[k]) for k in range(7)]

    def own(self):
        return pltpu.make_async_copy(self.tile, self.full.at[self.me.h, self.me.s], self.local)


class SmallScatter:
    def __init__(self, me, grad, got, total, got_z, send, recv):
        self.me, self.grad, self.got, self.total, self.got_z, self.send, self.recv = me, grad, got, total, got_z, send, recv

    def first(self):
        m = self.me
        return [rcopy(self.grad.at[:, m.s_index[k]], self.got.at[k], self.send.at[k], self.recv.at[k], m.spans[k]) for k in range(7)]

    def second(self):
        m = self.me
        return [rcopy(self.total.at[m.z_index[k]], self.got_z.at[k], self.send.at[7 + k], self.recv.at[7 + k], m.zs[k]) for k in range(3)]

    def add(self):
        v = self.grad[:, self.me.s]
        for k in range(7):
            v = v + self.got[k]
        self.total[...] = v

    def result(self):
        v = self.total[self.me.h]
        for k in range(3):
            v = v + self.got_z[k]
        return v


def start_all(copies):
    for cp in copies:
        cp.start()


def wait_all(copies):
    for cp in copies:
        cp.wait()


FFN_SHAPES = ((16, D), (16, 768), (16, 1280), (32, D), (32, D))


def ffn_index(k, whole):
    half = (k - 1) % 2
    if k == 0:
        return 0, ()
    if k < 3:
        return 1, (slice(None), whole(768 * half, 768 + 512 * half))
    return 2, (whole(32 * half, 32),)


def ffn_view(refs, k, index):
    which, tail = ffn_index(k, pl.ds)
    return refs[which].at[index + tail]


def ffn_values(refs, k, index):
    which, tail = ffn_index(k, lambda at, n: slice(at, at + n))
    return refs[which][index + tail]


def scatter_bufs(shape, dtype):
    return [VMEM((4, 2, 2) + shape, dtype), VMEM((4, 2) + shape, dtype), VMEM((4,) + shape, dtype), VMEM((3,) + shape, dtype)]


def split3(v):
    high, rest = split(v)
    mid = rest
    low = (v - high.astype(F32) - mid.astype(F32)).astype(BF16)
    return high, mid, low


def mm_exact(v, ones):
    a, b, c = split3(v)
    return mm(a, ones) + mm(b, ones) + mm(c, ones)


def small_rows(vt, g1, s1, pb, ob, g2, s2, rb, eb):
    vt[...] = jnp.zeros_like(vt)
    for r, ref in enumerate((g1, s1, None, None, None, ob, g2, s2)):
        vt[r:r + 1, 0:16] = pb[r - 2:r - 1, :] if ref is None else ref[...]
    vt[0:1, 16:32] = rb[...]
    for r in range(8):
        vt[r:r + 1, 32:40] = eb[0:1, 8 * r:8 * r + 8]


def unpack_small(gathered, vecs, b1):
    v = gathered[...].reshape(256, 128)
    row, n = iota((256, D), 0), iota((256, D), 1)
    lane, col = iota((128, D), 0), iota((128, D), 1)
    mine = (row >> 3) == (n >> 4)
    for half in range(2):
        x = mm_exact(v, ones_where(lane == (col & 15) + 16 * half))
        vecs[8 * half:8 * half + 8, :] = jnp.sum(jnp.where(mine, x, 0.0).reshape(32, 8, D), axis=0)
    x = mm_exact(v, ones_where(lane == (col & 7) + 32))
    for q in range(4):
        ok = ((row >> 3) == ((n + 512 * q) >> 6)) & ((row & 7) == ((n >> 3) & 7))
        b1[0:1, D * q:D * q + D] = jnp.sum(jnp.where(ok, x, 0.0), axis=0, keepdims=True)


def fill_bias(bias, labk, labq, place, tiles):
    def matching(i):
        kl = labk[tile_at(i):tile_at(i) + tile_keys(i), :].astype(F32)
        return (kl == labq[i:i + 1, :]) & (kl != 0.0)

    r, c = iota((160, 128), 0), iota((160, 128), 1)
    near = jnp.abs((r >> 4) - 1 - (c >> 4)) <= 1
    far = near & (jnp.abs((r >> 3) - 2 - (c >> 3)) >= 2)
    same = (r - 16) == c
    for i in tiles:
        if i == 15:
            continue
        ok = matching(i) & near | same if i < 8 else matching(i) & far
        bias[160 * i:160 * i + 160, :] = jnp.where(ok, 0.0, NEG)
    if 15 not in tiles:
        return
    r, c = iota((336, 128), 0), iota((336, 128), 1)
    inner = (r >= 96).astype(I32) + (r >= 160).astype(I32)
    start = jnp.where(inner == 0, 0, jnp.where(inner == 1, 96, 160))
    e, k = (r - 208) >> 4, (r - 208) & 15
    upper = (k >= 8).astype(I32)
    level_k = jnp.where(r < 208, 4 + inner, 7 + upper)
    pos_k = jnp.where(r < 208, r - start - 16, jnp.where(k < 8, e * 8 + k, e * 4 + k - 8))
    level_q, start_q = mixed_levels(c)
    pos_q = c - start_q + jnp.where(level_q == 7, place * 8, jnp.where(level_q == 8, place * 4, 0))
    shape = (level_k == level_q) & (jnp.abs((pos_k >> 4) - (pos_q >> 4)) <= 1) & (jnp.abs((pos_k >> 3) - (pos_q >> 3)) >= 2)
    bias[BIAS_MIXED:BIASES, :] = jnp.where(matching(15) & shape, 0.0, NEG)


def bias_of(bias, i):
    return twice(bias[160 * i:160 * i + 160, :] if i < 15 else bias[BIAS_MIXED:BIASES, :])


def forward_kernel(near, *refs):
    refs = list(refs)

    def take(n):
        out = refs[:n]
        del refs[:n]
        return out
    tok, seg = take(2)
    if near:
        wq_in, = take(1)
        small = take(8)
        ffn_in = take(3)
    else:
        wq, vecs = take(2)
    kvx_o, qx_o, bias_o, a1_o, ao_o, iz_o, sp_o, spt_o = take(8)
    if near:
        wq_o, vecs_o, b1_o = take(3)
        ffn_o = take(3)
    kvx, qx, bias, a1, ao, iz, sp, spt, xh, labq, n0, nc, z0, labk, seg2, msg, got, wbuf, out_sem, e_send, e_recv = take(21)
    if near:
        wq, vecs, b1, vt, vg, local, send, recv, send_v, recv_v = take(10)
    me = Peers(near)
    place = me.place
    outs = []

    def emit(src, dst):
        cp = pltpu.make_async_copy(src, dst, out_sem.at[len(outs)])
        cp.start()
        outs.append(cp)

    got[...] = jnp.zeros_like(got)
    if near:
        small_rows(vt, *small)
    greet(me.greeted)
    ids_core = rcopy(seg, seg2, e_send.at[6], e_recv.at[6], me.core)
    ids_core.start()
    if near:
        small_g = SmallGather(me, vt, vg, local.at[15], send_v, recv_v)
        small_g.own().start()
        start_all(small_g.first())
        first = []
        for k, (which, lanes) in enumerate((w, pl.ds(lo, 256)) for w in (pl.ds(1, 2), pl.ds(0, 1)) for lo in (0, 256)):
            first.append(Gather(me, wq_in.at[which, :, lanes], lambda h, y, x, c, which=which, lanes=lanes: wq.at[which, h, y, x, c, :, lanes],
                                k % 2 == 1, local.at[k], send.at[k], recv.at[k]))
        later = [Gather(me, ffn_view(ffn_in, k, ()), lambda h, y, x, c, k=k: ffn_view(ffn_o, k, (h, y, x, c)), k in (2, 4),
                        local.at[4 + k], send.at[4 + k], recv.at[4 + k]) for k in range(5)]

    def step(group, stage, *pieces):
        if not near:
            return
        for k in pieces:
            a = (first if group == 0 else later)[k]
            if stage >= 0:
                a.wait(stage)
            if stage < 3:
                a.start(stage + 1)

    step(0, -1, 0, 1, 2, 3)
    fill_pool(sp)
    fill_spread(spt)
    emit(sp, sp_o)
    emit(spt, spt_o)
    if near:
        small_g.own().wait()
        wait_all(small_g.first())
        start_all(small_g.second())
    step(0, 0, 0, 1, 2, 3)
    step(1, -1, 0, 1, 2, 3, 4)
    ids_core.wait()

    def chunk(ref, k):
        return ref[:, pl.ds(pl.multiple_of(TOK * k, TOK), TOK)].astype(F32)
    odd = me.odd.astype(F32)
    ids = chunk(seg, me.h)
    ids_left = jnp.where(me.h > 0, chunk(seg, lax.rem(me.h + 3, 4)), chunk(seg2, 3) * odd)
    ids_right = jnp.where(me.h < 3, chunk(seg, lax.rem(me.h + 1, 4)), chunk(seg2, 0) * (1.0 - odd))
    ids_b = jnp.broadcast_to(ids, (128, TOK)).astype(BF16)
    sq_b = jnp.broadcast_to(ids * ids, (128, TOK)).astype(BF16)
    eye = identity(TILE)
    for j in range(TILES):
        labk[16 + TILE * j:16 + TILE * j + TILE, :] = mm_bt(eye, ids_b[:, TILE * j:TILE * j + TILE]).astype(BF16)
    for i in range(8):
        labq[i:i + 1, :] = ids[:, 128 * i:128 * i + 128]
    row, t = iota((128, TOK), 0), iota((128, TOK), 1)
    level, level_row = row >> 4, iota((1, 128), 1) >> 4
    for side, v in ((0, ids_left), (1, ids_right)):
        base = jnp.right_shift(TOK, level) - 16 if side == 0 else 0
        sel = ones_where(jnp.right_shift(t, level) == base + (row & 15))
        x = mm_bt(two_rows(v, v * v).astype(BF16), sel)
        col = column_of(labels_of(x[0:1], x[1:2], jnp.left_shift(1, level_row).astype(F32)), 128)
        for l in range(7):
            labk[border(side, l):border(side, l) + 16, :] = col[16 * l:16 * l + 16]
    even_ids = [jnp.where(me.odd == 0, chunk(seg, k), chunk(seg2, k)) for k in range(4)]
    odd_ids = [jnp.where(me.odd == 0, chunk(seg2, k), chunk(seg, k)) for k in range(4)]
    all_ids = jnp.concatenate(even_ids + odd_ids, axis=0)
    x = mm_bt(jnp.concatenate([all_ids, all_ids * all_ids], axis=0).astype(BF16), sp[496:512, :])
    lab = labels_of(x[0:8], x[8:16], jnp.where(iota((8, 16), 1) < 8, 128.0, 256.0))
    lab = jnp.broadcast_to(lab[:, None, :], (8, 16, 16)).reshape(128, 16)
    lab = jnp.sum(jnp.where((iota((128, 16), 0) & 15) == iota((128, 16), 1), lab, 0.0), axis=1, keepdims=True)
    labk[WIDE_AT:EXT, :] = jnp.broadcast_to(lab, (128, 128)).astype(BF16)

    def put_coarse(dst, b, value, cols):
        at, block, _t, _n = coarse_blocks()[b]
        if block < 3:
            level = block + 1
            row = EXT_AT[level] + 16 + at - (0, 512, 768)[block]
            dst[row:row + 128, cols] = value
        else:
            for level, a, n in ((4, 0, 64), (5, 64, 32), (6, 96, 16)):
                dst[EXT_AT[level] + 16:EXT_AT[level] + 16 + n, cols] = value[a:a + n]

    for b, (at, block, t, n) in enumerate(coarse_blocks()):
        s = sp[128 * block:128 * block + 128, t:t + n]
        rows_level, _unused = mixed_levels(iota((128, 128), 0))
        cols_level, _unused = mixed_levels(iota((8, 128), 1))
        times_r = (1 << rows_level).astype(F32) if block == 3 else float(2 ** (block + 1))
        times_c = (1 << cols_level).astype(F32) if block == 3 else float(2 ** (block + 1))
        lab = labels_of(mm_bt(s, ids_b[:, t:t + n]), mm_bt(s, sq_b[:, t:t + n]), times_r)
        put_coarse(labk, b, lab.astype(BF16), slice(0, 128))
        row = labels_of(mm_bt(ids_b[0:8, t:t + n], s), mm_bt(sq_b[0:8, t:t + n], s), times_c)
        labq[8 + b:9 + b, :] = row[0:1, :]
    step(0, 1, 0, 1, 2, 3)
    fill_bias(bias, labk, labq, place, range(16))
    emit(bias, bias_o)
    step(1, 0, 0, 1, 2)
    @pl.loop(0, TILES)
    def _(j):
        rows = pl.ds(pl.multiple_of(TILE * j, TILE), TILE)
        v = tok[rows, :].astype(F32)
        center = v - jnp.mean(v, axis=-1, keepdims=True)
        xh[rows, :] = center * lax.rsqrt(jnp.mean(center * center, axis=-1, keepdims=True) + EPS)
    step(0, 2, 0, 1, 2, 3)
    step(1, 0, 3, 4)
    if near:
        wait_all(small_g.second())
        unpack_small(vg, vecs, b1)
        emit(vecs, vecs_o)
        emit(b1, b1_o)
    @pl.loop(0, TILES)
    def _(j):
        rows = pl.ds(pl.multiple_of(TILE * j, TILE), TILE)
        a1[rows, :] = (xh[rows, :] * vecs[0:1, :] + vecs[1:2, :]).astype(BF16)
    emit(a1, a1_o)
    step(0, 3, 0, 1)

    def project(c):
        w = wq[c].reshape(D, D)
        for j in range(TILES):
            r = (mm(a1[TILE * j:TILE * j + TILE, :], w) + vecs[2 + c:3 + c, :]).astype(BF16)
            if c == 0:
                qx[TILE * j:TILE * j + TILE, :] = r * jnp.array(0.125, BF16)
            else:
                kvx[16 + TILE * j:16 + TILE * j + TILE, D * (c - 1):D * c] = r

    def pool_parts(block, t, n):
        if block == 3:
            level, _unused = mixed_levels(iota((128, D), 0))
            shrink = 1.0 / (1 << level).astype(F32)
        else:
            shrink = 0.5 ** (block + 1)
        return sp[128 * block:128 * block + 128, t:t + n], shrink
    project(1)
    project(2)
    step(1, 1, 0, 2)
    wide_z = [rcopy(wbuf.at[place], wbuf.at[place], e_send.at[2 + k], e_recv.at[2 + k], me.zs[k]) for k in range(3)]
    for b, (at, block, t, n) in reversed(list(enumerate(coarse_blocks()))):
        pool, shrink = pool_parts(block, t, n)
        kc, vc = mm(pool, kvx[16 + t:16 + t + n, 0:D]) * shrink, mm(pool, kvx[16 + t:16 + t + n, D:2 * D])
        put_coarse(kvx, b, kc.astype(BF16), slice(0, D))
        put_coarse(kvx, b, vc.astype(BF16), slice(D, 2 * D))
        if block == 3:
            wbuf[place] = jnp.concatenate([kc[112:120], vc[112:120]], axis=0).astype(BF16)
            start_all(wide_z)
    step(1, 1, 1)
    for side in range(2):
        for l in range(7):
            at = own_border(side, l)
            k16, v16 = kvx[at:at + 16, 0:D], kvx[at:at + 16, D:2 * D]
            if l == 0:
                msg[side, 0], msg[side, 1] = k16, v16
            else:
                far = [pick_far(side, v.astype(F32)) for v in (k16, v16)]
                msg[side, l + 1] = jnp.concatenate(far, axis=0).astype(BF16)
    to_right = rcopy(msg.at[1], got.at[0], e_send.at[0], e_recv.at[0], me.right)
    to_left = rcopy(msg.at[0], got.at[1], e_send.at[1], e_recv.at[1], me.left)
    four = wbuf.at[pl.ds(4 * me.odd, 4)]
    wide_core = rcopy(four, four, e_send.at[5], e_recv.at[5], me.core)
    not_last, not_first = place < 7, place > 0

    @pl.when(not_last)
    def _():
        to_right.start()

    @pl.when(not_first)
    def _():
        to_left.start()
    step(1, 1, 4)
    step(0, 3, 2, 3)
    project(0)
    for at, block, t, n in coarse_blocks():
        pool, shrink = pool_parts(block, t, n)
        qx[1024 + at:1024 + at + 128, :] = (mm(pool, qx[t:t + n, :]) * shrink).astype(BF16)
    emit(qx, qx_o)
    if near:
        emit(wq, wq_o)
    step(1, 1, 3)
    masks = head_masks(128)

    def tile(g, i):
        keys = slice(tile_at(i), tile_at(i) + tile_keys(i))
        kw, vw = kvx[keys, lanes_of(g)], kvx[keys, lanes_of(g, D)]
        q = by_head(qx[128 * i:128 * i + 128, lanes_of(g)], masks)
        e = jnp.exp(mm_bt(kw, q) + bias_of(bias, i))
        times = tile_times(i)
        z = jnp.sum(e, axis=0, keepdims=True)
        z0_, z1_ = z[:, 0:128] * times, z[:, 128:256] * times
        n = own_blocks(mm_at(vw, e.astype(BF16)))
        if i < 8:
            cols = slice(128 * i, 128 * i + 128)
            n0[g, :, cols] = n
            z0[g, 0:1, cols] = z0_
            z0[g, 1:2, cols] = z1_
        else:
            cols = slice(128 * i - 1024, 128 * i - 896)
            high, low = split(two_rows(z0_, z1_))
            nc[g, :, cols] = jnp.concatenate([n.astype(BF16), high, low], axis=0)

    @pl.loop(0, 4)
    def _(g):
        for k in range(4):
            @pl.when(g == k)
            def _():
                if k == 1:
                    wait_all(wide_z)
                    wide_core.start()
        for i in INNER:
            tile(g, i)

    wide_core.wait()
    w = wbuf[...].reshape(128, D)
    kvx[WIDE_AT:EXT, 0:D] = mm(wide_rows(0), w).astype(BF16)
    kvx[WIDE_AT:EXT, D:2 * D] = mm(wide_rows(1), w).astype(BF16)

    @pl.when(not_last)
    def _():
        to_right.wait_send()
        to_left.wait_recv()

    @pl.when(not_first)
    def _():
        to_left.wait_send()
        to_right.wait_recv()
    for side in range(2):
        m = got[side].reshape(128, D)
        closer = mm(near_rows(side), m)
        m = m.astype(F32)
        for l in range(7):
            at = border(side, l)
            if l == 0:
                k16, v16 = m[0:16], m[16:32]
            else:
                a, b = 16 * (l + 1), 16 * (l - 1)
                k16 = far_and_near(side, m[a:a + 8], closer[b:b + 8])
                v16 = far_and_near(side, m[a + 8:a + 16], closer[b + 8:b + 16])
            kvx[at:at + 16, 0:D] = k16.astype(BF16)
            kvx[at:at + 16, D:2 * D] = v16.astype(BF16)
    emit(kvx, kvx_o)

    @pl.loop(0, 4)
    def _(g):
        for k in range(4):
            @pl.when(g == k)
            def _():
                step(1, 2, *((0, 2), (1,), (), (4,))[k])
        for i in OUTER:
            tile(g, i)
        c_ref = nc.at[g]
        for j in range(TILES):
            cols = slice(TILE * j, TILE * j + TILE)
            r = mm(coarse_cols(c_ref, 0, j), sp[:, cols])
            n = n0[g, :, cols] + r[0:128]
            i0 = 1.0 / (z0[g, 0:1, cols] + r[128:129] + r[144:145])
            i1 = 1.0 / (z0[g, 1:2, cols] + r[129:130] + r[145:146])
            iz[g, 0:1, cols] = i0
            iz[g, 1:2, cols] = i1
            ao[pl.ds(pl.multiple_of(g * 128, 128), 64), cols] = (n[0:64] * i0).astype(BF16)
            ao[pl.ds(pl.multiple_of(g * 128 + 64, 64), 64), cols] = (n[64:128] * i1).astype(BF16)
    emit(ao, ao_o)
    emit(iz, iz_o)
    step(1, 2, 3)
    step(1, 3, 0, 1, 2, 3, 4)
    wait_all(outs)


ANY = pl.BlockSpec(memory_space=pl.ANY)
IN_VMEM = pl.BlockSpec(memory_space=pltpu.VMEM)
S = jax.ShapeDtypeStruct
SEM = pltpu.SemaphoreType.DMA


def forward(near, tok, seg, *params):
    grid = (4, 2, 2, 2)
    shapes = [S((EXT, 2 * D), BF16), S((2048, D), BF16), S((BIASES, 128), F32), S((TOK, D), BF16), S((D, TOK), BF16),
              S((4, 2, TOK), F32), S((512, TOK), BF16), S((TOK, 512), BF16)]
    scratch = [VMEM(s.shape, s.dtype) for s in shapes] + [
        VMEM((TOK, D), F32), VMEM((16, 128), F32), VMEM((4, 128, TOK), F32), VMEM((4, 160, TOK), BF16), VMEM((4, 2, TOK), F32),
        VMEM((EXT, 128), BF16), VMEM(seg.shape, I32), VMEM((2, 8, 16, D), BF16), VMEM((2, 8, 16, D), BF16), VMEM((8, 16, D), BF16),
        SEM((16,)), SEM((7,)), SEM((7,))]
    if near:
        shapes += [S((3,) + grid + (16, D), BF16), S((16, D), F32), S((1, FF), F32)]
        shapes += [S(grid + a.shape, a.dtype) for a in params[9:]]
        scratch += [VMEM((3,) + grid + (16, D), BF16), VMEM((16, D), F32), VMEM((1, FF), F32), VMEM((8, 128), F32),
                    VMEM((4, 8, 8, 128), F32), SEM((16,)), SEM((9, 6)), SEM((9, 6)), SEM((10,)), SEM((10,))]
        specs = [IN_VMEM] * 9 + [ANY] * 3
    else:
        specs = [IN_VMEM] * 2
    return pl.pallas_call(
        functools.partial(forward_kernel, near),
        out_shape=shapes,
        in_specs=[IN_VMEM, IN_VMEM] + specs,
        out_specs=[ANY] * len(shapes),
        scratch_shapes=scratch,
        compiler_params=pltpu.CompilerParams(collective_id=0, has_side_effects=True, vmem_limit_bytes=60 << 20),
        name="forward",
    )(tok, seg, *params)


C0 = 0.7978845608028654
C1 = 0.044715


def middle_kernel(tok, ao, cot, wo, w1, w2, vecs, b1, out, dh1_out, da_out, gwo, gw1, gw2, gvec, gb1,
                  awo, aw1, aw2, avec, ab1):
    j = pl.program_id(0)

    @pl.when(j == 0)
    def _():
        awo[...] = jnp.zeros_like(awo)
        aw1[...] = jnp.zeros_like(aw1)
        aw2[...] = jnp.zeros_like(aw2)
        avec[...] = jnp.zeros_like(avec)
        ab1[...] = jnp.zeros_like(ab1)
    mixed = ao[...]
    h1 = tok[...].astype(F32) + mm_at(mixed, wo[...]) + vecs[5:6, :]
    center = h1 - jnp.mean(h1, axis=-1, keepdims=True)
    inverse = lax.rsqrt(jnp.mean(center * center, axis=-1, keepdims=True) + EPS)
    xh = center * inverse
    gain = vecs[6:7, :]
    a2 = (xh * gain + vecs[7:8, :]).astype(BF16)
    dy = cot[...]
    y = h1 + vecs[8:9, :]
    da2 = jnp.zeros((512, D), F32)
    for k in range(FF // D):
        cols = slice(D * k, D * k + D)
        u = mm(a2, w1[:, cols]) + b1[:, cols]
        u2 = u * u
        th = jnp.tanh(u * (C0 + (C0 * C1) * u2))
        half = 0.5 * (1.0 + th)
        g = (u * half).astype(BF16)
        slope = half + 0.5 * u * (1.0 - th * th) * (C0 + (3.0 * C0 * C1) * u2)
        y = y + mm(g, w2[cols, :])
        du = (mm_bt(dy, w2[cols, :]) * slope).astype(BF16)
        aw2[cols, :] += mm_at(g, dy)
        aw1[:, cols] += mm_at(a2, du)
        ab1[:, cols] += jnp.sum(du.astype(F32), axis=0, keepdims=True)
        da2 = da2 + mm_bt(du, w1[:, cols])
    out[...] = y.astype(BF16)
    dyf = dy.astype(F32)
    e = da2 * gain
    dh1 = dyf + inverse * (e - jnp.mean(e, axis=-1, keepdims=True) - xh * jnp.mean(e * xh, axis=-1, keepdims=True))
    dh1_out[...] = dh1
    db = dh1.astype(BF16)
    awo[...] += mm(mixed, db)
    da_out[...] = mm_bt(wo[...], db).astype(BF16)
    avec[5:6, :] += jnp.sum(db.astype(F32), axis=0, keepdims=True)
    avec[6:7, :] += jnp.sum(da2 * xh, axis=0, keepdims=True)
    avec[7:8, :] += jnp.sum(da2, axis=0, keepdims=True)
    avec[8:9, :] += jnp.sum(dyf, axis=0, keepdims=True)

    @pl.when(j == TOK // 512 - 1)
    def _():
        gwo[...] = awo[...].astype(BF16)
        gw1[...] = aw1[...].astype(BF16)
        gw2[...] = aw2[...].astype(BF16)
        gvec[...] = avec[...]
        gb1[...] = ab1[...]


def whole(shape):
    return pl.BlockSpec(shape, lambda j: (0,) * len(shape), pipeline_mode=pl.Buffered(1))


def middle(tok, ao, cot, wo, w1, w2, vecs, b1):
    tile = pl.BlockSpec((512, D), lambda j: (j, 0))
    flat = pl.BlockSpec((D, 512), lambda j: (0, j))
    return pl.pallas_call(
        middle_kernel,
        grid=(TOK // 512,),
        out_shape=[S((TOK, D), BF16), S((TOK, D), F32), S((D, TOK), BF16), S((D, D), BF16), S((D, FF), BF16), S((FF, D), BF16),
                   S((16, D), F32), S((1, FF), F32)],
        in_specs=[tile, flat, tile, whole((D, D)), whole((D, FF)), whole((FF, D)), whole((16, D)), whole((1, FF))],
        out_specs=[tile, tile, flat, whole((D, D)), whole((D, FF)), whole((FF, D)), whole((16, D)), whole((1, FF))],
        scratch_shapes=[VMEM((D, D), F32), VMEM((D, FF), F32), VMEM((FF, D), F32), VMEM((16, D), F32), VMEM((1, FF), F32)],
        compiler_params=pltpu.CompilerParams(dimension_semantics=("arbitrary",), vmem_limit_bytes=60 << 20),
        name="middle",
    )(tok, ao, cot, wo, w1, w2, vecs, b1)


def pack_small(rows, b1):
    row, n = iota((256, D), 0), iota((256, D), 1)
    lane, col = iota((128, D), 0), iota((128, D), 1)
    mine = (row >> 3) == (n >> 4)

    def moved(v, ok, ones):
        total = None
        for part in split3(jnp.where(ok, v, 0.0)):
            r = mm_bt(part, ones)
            total = r if total is None else total + r
        return total
    eight = jnp.broadcast_to(rows[0:8][None], (32, 8, D)).reshape(256, D)
    out = moved(eight, mine, ones_where(lane == (col & 15)))
    out = out + moved(jnp.broadcast_to(rows[8:9], (256, D)), mine & ((row & 7) == 0), ones_where(lane == (col & 15) + 16))
    last = ones_where(lane == (col & 7) + 32)
    for q in range(4):
        ok = ((row >> 3) == ((n + 512 * q) >> 6)) & ((row & 7) == ((n >> 3) & 7))
        out = out + moved(jnp.broadcast_to(b1[0:1, D * q:D * q + D], (256, D)), ok, last)
    return out.reshape(4, 8, 8, 128)


def backward_kernel(near, *refs):
    refs = list(refs)

    def take(n):
        out = refs[:n]
        del refs[:n]
        return out
    ins = take(13)
    gffn, (gvec, gb1) = take(3), take(2)
    tok_o, gq_o = take(2)
    small_o = take(8 if near else 1)
    gffn_o = take(3 if near else 0)
    kvx, qx, bias, a1, ao, iz, sp, spt, da, tok, dh1, wq, vecs = take(13)
    gr, rm, dqt, dkv, dq, edge, e_got, w_all, w_got, w_mid, gq, avec, tok_s, dall, in_sem, out_sem, e_send, e_recv = take(18)
    if near:
        gv, f_mine, f_sem, send, recv, send_v, recv_v, v_got, v_sum, v_z = take(10)
        bufs = [take(4) for _ in range(11)]
    me = Peers(near)
    place = me.place
    loads = {}
    targets = (da, ao, iz, sp, kvx, qx, bias, spt, a1, tok, dh1, wq, vecs)
    names = ("da", "ao", "iz", "sp", "kvx", "qx", "bias", "spt", "a1", "tok", "dh1", "wq", "vecs")
    for k, name in enumerate(names):
        loads[name] = pltpu.make_async_copy(ins[k], targets[k], in_sem.at[k])
        loads[name].start()
    greet(me.greeted)
    mine_copies = []
    if near:
        for k in range(3):
            cp = pltpu.make_async_copy(gffn[k].at[:, :, :, me.c], f_mine[k], f_sem.at[k])
            cp.start()
            mine_copies.append(cp)
        every = slice(None)
        ffn = [Scatter(me, lambda c, k=k: ffn_view(gffn, k, (every, every, every, c)), lambda h, y, x, k=k: ffn_values(f_mine, k, (h, y, x)),
                       k in (2, 4), bufs[k], send.at[k], recv.at[k]) for k in range(5)]
        last = []
        for k in range(6):
            lo = 256 * (k % 2)
            last.append(Scatter(me, lambda c, k=k, lo=lo: gq.at[k // 2, :, :, :, c, :, pl.ds(lo, 256)],
                                lambda h, y, x, k=k, lo=lo: gq[k // 2, h, y, x, me.c, :, lo:lo + 256], k % 2 == 1,
                                bufs[5 + k], send.at[5 + k], recv.at[5 + k]))
        small_s = SmallScatter(me, gv, v_got, v_sum, v_z, send_v, recv_v)
        for a in ffn:
            a.start(0)

    def put_ffn(k):
        which, tail = ffn_index(k, lambda at, n: slice(at, at + n))
        gffn_o[which][tail or (slice(None),)] = ffn[k].result()

    def put_last(k):
        gq_o[k // 2, :, 256 * (k % 2):256 * (k % 2) + 256] = last[k].result()

    def step(group, stage, *pieces):
        if not near:
            return
        for k in pieces:
            a = (ffn if group == 0 else last)[k]
            a.wait(stage)
            if stage < 3:
                a.add(stage)
                a.start(stage + 1)
            elif group == 0:
                put_ffn(k)
            else:
                put_last(k)

    for name in ("da", "ao", "iz", "sp"):
        loads[name].wait()
    masks = head_masks(128)

    @pl.loop(0, 4)
    def _(g):
        lo, hi = pl.ds(pl.multiple_of(g * 128, 128), 64), pl.ds(pl.multiple_of(g * 128 + 64, 64), 64)
        for j in range(TILES):
            cols = slice(TILE * j, TILE * j + TILE)
            g0 = da[lo, cols].astype(F32) * iz[g, 0:1, cols]
            g1 = da[hi, cols].astype(F32) * iz[g, 1:2, cols]
            r0 = jnp.sum(g0 * ao[lo, cols].astype(F32), axis=0, keepdims=True)
            r1 = jnp.sum(g1 * ao[hi, cols].astype(F32), axis=0, keepdims=True)
            rm[g, 0:1, cols] = r0
            rm[g, 1:2, cols] = r1
            high, low = split(two_rows(r0, r1))
            gr[g, :, cols] = jnp.concatenate([g0.astype(BF16), g1.astype(BF16), high, low], axis=0)
        for b, (at, block, t, n) in enumerate(coarse_blocks()):
            x = mm_bt(gr[g, :, t:t + n], sp[128 * block:128 * block + 128, t:t + n])
            cols = slice(1024 + at, 1152 + at)
            gr[g, 0:128, cols] = x[0:128].astype(BF16)
            times = tile_times(8 + b)
            rm[g, 0:1, cols] = (x[128:129] + x[144:145]) * times
            rm[g, 1:2, cols] = (x[129:130] + x[145:146]) * times
    dkv[...] = jnp.zeros_like(dkv)
    for name in ("kvx", "qx", "bias"):
        loads[name].wait()
    zero = jnp.zeros((64, 128), BF16)

    def tile(g, i):
        keys = slice(tile_at(i), tile_at(i) + tile_keys(i))
        cols = slice(128 * i, 128 * i + 128)
        kw, vw = kvx[keys, lanes_of(g)], kvx[keys, lanes_of(g, D)]
        q = by_head(qx[cols, lanes_of(g)], masks)
        gt = gr[g, 0:128, cols]
        gb = jnp.concatenate([jnp.concatenate([gt[0:64], zero], axis=1), jnp.concatenate([zero, gt[64:128]], axis=1)], axis=0)
        e = jnp.exp(mm_bt(kw, q) + bias_of(bias, i))
        rest = jnp.concatenate([rm[g, 0:1, cols], rm[g, 1:2, cols]], axis=1)
        ds = (e * (mm(vw, gb) - rest)).astype(BF16)
        dkv[keys, lanes_of(g)] += mm(ds, q)
        dkv[keys, lanes_of(g, D)] += mm_bt(e.astype(BF16), gb)
        dqt[g, :, cols] = (own_blocks(mm_at(kw, ds)) * (0.125 / tile_times(i))).astype(BF16)

    if near:
        wait_all(mine_copies)
    step(0, 0, 0, 1, 2, 3, 4)

    @pl.loop(0, 4)
    def _(g):
        for i in OUTER:
            tile(g, i)
    for side in range(2):
        base, closer = [], []
        for l in range(7):
            at = border(side, l)
            k16, v16 = dkv[at:at + 16, 0:D], dkv[at:at + 16, D:2 * D]
            if l == 0:
                base += [k16, v16]
            elif side == 0:
                base += [k16[0:8], v16[0:8]]
                closer += [k16[8:16], v16[8:16]]
            else:
                base += [k16[8:16], v16[8:16]]
                closer += [k16[0:8], v16[0:8]]
        folded = mm_at(near_rows(side), jnp.concatenate(closer, axis=0).astype(BF16))
        edge[side] = (jnp.concatenate(base, axis=0) + folded).astype(BF16).reshape(8, 16, D)
    d_wide = mm_at(wide_rows(0), dkv[WIDE_AT:EXT, 0:D].astype(BF16)) + mm_at(wide_rows(1), dkv[WIDE_AT:EXT, D:2 * D].astype(BF16))
    w_all[...] = d_wide.astype(BF16).reshape(8, 16, D)
    to_right = rcopy(edge.at[1], e_got.at[0], e_send.at[0], e_recv.at[0], me.right)
    to_left = rcopy(edge.at[0], e_got.at[1], e_send.at[1], e_recv.at[1], me.left)
    wide_core = rcopy(w_all.at[pl.ds(4 * (1 - me.odd), 4)], w_mid, e_send.at[2], e_recv.at[2], me.core)
    not_last, not_first = place < 7, place > 0
    wide_core.start()

    @pl.when(not_last)
    def _():
        to_right.start()

    @pl.when(not_first)
    def _():
        to_left.start()
    step(0, 1, 0, 1, 2)

    @pl.loop(0, 2)
    def _(g):
        for i in INNER:
            tile(g, i)
    wide_core.wait()
    for k in range(4):
        w_mid[k] = (w_mid[k].astype(F32) + w_all[4 * me.odd + k].astype(F32)).astype(BF16)
    wide_z = [rcopy(w_mid.at[me.z_index[k]], w_got.at[k], e_send.at[3 + k], e_recv.at[3 + k], me.zs[k]) for k in range(3)]
    start_all(wide_z)

    @pl.loop(2, 4)
    def _(g):
        for i in INNER:
            tile(g, i)
    step(0, 1, 3, 4)

    @pl.loop(0, 4)
    def _(g):
        d_ref = dqt.at[g]
        eye = identity(TILE)
        for j in range(TILES):
            cols = slice(TILE * j, TILE * j + TILE)
            r = d_ref[:, cols].astype(F32) + mm(coarse_cols(d_ref, 1024, j), sp[:, cols])
            dq[cols, lanes_of(g)] = mm_bt(eye, r.astype(BF16)).astype(BF16)
    for name in ("spt", "a1", "tok", "dh1", "wq", "vecs"):
        loads[name].wait()
    avec[...] = jnp.zeros_like(avec)

    def projection_grad(c, d):
        aw = mm_at(a1[...], d).astype(BF16)
        avec[2 + c:3 + c, :] = jnp.sum(d.astype(F32), axis=0, keepdims=True)
        gq[c] = aw.reshape(4, 2, 2, 2, 16, D)
        if near:
            for a in last[2 * c:2 * c + 2]:
                a.start(0)
    projection_grad(0, dq[...])
    step(0, 2, 0, 1, 2)
    for cp in wide_z:
        cp.wait()

    def add_edge(side):
        m = e_got[side].reshape(128, D).astype(F32)
        for l in range(7):
            if l == 0:
                at, n = own_border(side, 0), 16
            else:
                at, n = own_border(side, l) + (0 if side else 8), 8
            a = 16 * (l + 1) if l else 0
            dkv[at:at + n, 0:D] += m[a:a + n]
            dkv[at:at + n, D:2 * D] += m[a + n:a + 2 * n]

    @pl.when(not_last)
    def _():
        to_right.wait_send()
        to_left.wait_recv()
        add_edge(1)

    @pl.when(not_first)
    def _():
        to_left.wait_send()
        to_right.wait_recv()
        add_edge(0)
    v = w_mid[me.h].astype(F32)
    for k in range(3):
        v = v + w_got[k].astype(F32)
    v = jnp.concatenate([v[0:8] * 0.5 ** 7, v[8:16]], axis=1)
    w_own = jnp.concatenate([v, jnp.zeros((8, 2 * D), F32)], axis=0).astype(BF16)
    lane_all = iota((1, 2 * D), 1)

    def coarse_rows(at, n, level):
        return (dkv[at:at + n, :] * jnp.where(lane_all < D, 0.5 ** level, 1.0)).astype(BF16)
    top = jnp.concatenate([coarse_rows(EXT_AT[3] + 16, 128, 3), coarse_rows(EXT_AT[4] + 16, 64, 4), coarse_rows(EXT_AT[5] + 16, 32, 5),
                           coarse_rows(EXT_AT[6] + 16, 16, 6), w_own], axis=0)
    for j in range(TILES):
        rows = slice(TILE * j, TILE * j + TILE)
        x = jnp.concatenate([coarse_rows(EXT_AT[1] + 16 + 128 * j, 128, 1), coarse_rows(EXT_AT[2] + 16 + 128 * (j // 2), 128, 2), top], axis=0)
        dall[rows, :] = (dkv[16 + TILE * j:16 + TILE * j + TILE, :] + mm(spt[rows, :], x)).astype(BF16)
    projection_grad(1, dall[:, 0:D])
    step(0, 2, 3, 4)
    step(1, 0, 0, 1)
    projection_grad(2, dall[:, D:2 * D])
    step(1, 0, 2, 3)
    @pl.loop(0, TILES)
    def _(j):
        rows = pl.ds(pl.multiple_of(TILE * j, TILE), TILE)
        da1 = mm_bt(dq[rows, :], wq[0].reshape(D, D)) + mm_bt(dall[rows, 0:D], wq[1].reshape(D, D)) + mm_bt(dall[rows, D:2 * D], wq[2].reshape(D, D))
        v = tok[rows, :].astype(F32)
        center = v - jnp.mean(v, axis=-1, keepdims=True)
        inverse = lax.rsqrt(jnp.mean(center * center, axis=-1, keepdims=True) + EPS)
        n = center * inverse
        e = da1 * vecs[0:1, :]
        dv = inverse * (e - jnp.mean(e, axis=-1, keepdims=True) - n * jnp.mean(e * n, axis=-1, keepdims=True))
        tok_s[rows, :] = (dh1[rows, :] + dv).astype(BF16)
        avec[0:1, :] += jnp.sum(da1 * n, axis=0, keepdims=True)
        avec[1:2, :] += jnp.sum(da1, axis=0, keepdims=True)
        for k, what in enumerate(((0, 4, 5), (1, 0, 1), (1, 2, 3))):
            @pl.when(j == k)
            def _():
                step(1, *what)
    done = pltpu.make_async_copy(tok_s, tok_o, out_sem.at[0])
    done.start()
    if not near:
        gq_o[...] = gq[...]
        small_o[0][...] = avec[...]
        done.wait()
        return
    avec[5:9, :] = gvec[5:9, :]
    gv[...] = pack_small(avec[...], gb1)
    start_all(small_s.first())
    step(1, 1, 4, 5)
    step(1, 2, 0, 1)
    wait_all(small_s.first())
    small_s.add()
    start_all(small_s.second())
    step(1, 2, 2, 3, 4, 5)
    step(0, 3, 0, 1, 2, 3, 4)
    step(1, 3, 0, 1, 2, 3, 4, 5)
    wait_all(small_s.second())
    t = small_s.result()
    for k, r in enumerate((0, 1, None, 5, 6, 7)):
        if r is None:
            small_o[k][...] = t[2:5, 0:16]
        else:
            small_o[k][...] = t[r:r + 1, 0:16]
    for r in range(8):
        small_o[6][0:1, 8 * r:8 * r + 8] = t[r:r + 1, 32:40]
    small_o[7][...] = t[0:1, 16:32]
    done.wait()


def backward(near, saved, wq, vecs, tok, da, dh1, gffn, gvec, gb1):
    kvx, qx, bias, a1, ao, iz, sp, spt = saved
    grid = (4, 2, 2, 2)
    vm = [VMEM(v.shape, v.dtype) for v in (kvx, qx, bias, a1, ao, iz, sp, spt, da, tok, dh1, wq, vecs)]
    scratch = vm + [VMEM((4, 160, 2048), BF16), VMEM((4, 2, 2048), F32), VMEM((4, 128, 2048), BF16), VMEM((EXT, 2 * D), F32),
                    VMEM((TOK, D), BF16), VMEM((2, 8, 16, D), BF16), VMEM((2, 8, 16, D), BF16), VMEM((8, 16, D), BF16),
                    VMEM((3, 16, D), BF16), VMEM((4, 16, D), BF16), VMEM((3,) + grid + (16, D), BF16), VMEM((16, D), F32), VMEM((TOK, D), BF16), VMEM((TOK, 2 * D), BF16),
                    SEM((13,)), SEM((1,)), SEM((6,)), SEM((6,))]
    if near:
        gffn = [g.reshape(grid + (g.shape[0] // 32, g.shape[1])) for g in gffn]
        shapes = [S((TOK, D), BF16), S((3, 16, D), F32)]
        shapes += [S((1, 16), F32), S((1, 16), F32), S((3, 16), F32), S((1, 16), F32), S((1, 16), F32), S((1, 16), F32), S((1, 64), F32), S((1, 16), F32)]
        shapes += [S(g.shape[4:], F32) for g in gffn]
        pieces = [(shape, BF16) for shape in FFN_SHAPES] + [((16, 256), BF16)] * 6
        scratch += [VMEM((4, 8, 8, 128), F32), [VMEM((4, 2, 2) + g.shape[4:], BF16) for g in gffn], SEM((3,)), SEM((11, 6)), SEM((11, 6)),
                    SEM((10,)), SEM((10,)), VMEM((7, 4, 8, 128), F32), VMEM((4, 8, 128), F32), VMEM((3, 8, 128), F32)]
        for shape, kind in pieces:
            scratch += scatter_bufs(shape, kind)
    else:
        gffn = gffn[0:3]
        shapes = [S((TOK, D), BF16), S((3,) + grid + (16, D), BF16), S((16, D), F32)]
    ordered = (da, ao, iz, sp, kvx, qx, bias, spt, a1, tok, dh1, wq, vecs)
    return pl.pallas_call(
        functools.partial(backward_kernel, near),
        out_shape=shapes,
        in_specs=[ANY] * 16 + [IN_VMEM] * 2,
        out_specs=[ANY] + [IN_VMEM] * (len(shapes) - 1),
        scratch_shapes=scratch,
        compiler_params=pltpu.CompilerParams(collective_id=1, has_side_effects=True, vmem_limit_bytes=62 << 20),
        name="backward",
    )(*ordered, *gffn, gvec, gb1)


def finish_kernel(n, *refs):
    for k in range(n):
        refs[n + k][...] = refs[k][...]


def finish(*values):
    n = len(values)
    return pl.pallas_call(
        functools.partial(finish_kernel, n),
        out_shape=[S(v.shape, v.dtype) for v in values],
        in_specs=[IN_VMEM] * n,
        out_specs=[IN_VMEM] * n,
        name="finish",
    )(*values)


BOTH = ("head", "span")


def shards(tokens, segment_ids, first_gain, first_shift, project_weight, project_bias, output_weight, output_bias,
           second_gain, second_shift, expand_weight, expand_bias, reduce_weight, reduce_bias, cotangent):
    tok, cot = tokens[0], cotangent[0]
    near = lax.axis_size("head") == 4 and lax.axis_size("span") == 8
    if near:
        vectors = (first_gain, first_shift, project_bias, output_bias, second_gain, second_shift, reduce_bias, expand_bias)
        vectors = [v if v.ndim == 2 else v[None] for v in vectors]
        *saved, wq, vecs, b1, wo, w1, w2 = forward(True, tok, segment_ids, project_weight, *vectors, output_weight, expand_weight, reduce_weight)
        wo, w1, w2 = wo.reshape(D, D), w1.reshape(D, FF), w2.reshape(FF, D)
    else:
        def full(v, axis=0):
            return lax.all_gather(v, BOTH, axis=axis, tiled=True)
        wq, wo, w1, w2 = full(project_weight, 1), full(output_weight), full(expand_weight), full(reduce_weight)
        rows = [full(first_gain), full(first_shift), *full(project_bias, 1), full(output_bias), full(second_gain), full(second_shift), full(reduce_bias)]
        vecs = jnp.pad(jnp.stack(rows), ((0, 7), (0, 0)))
        b1 = full(expand_bias)[None]
        saved = forward(False, tok, segment_ids, wq, vecs)
    ao = saved[4]
    out, dh1, da, *gffn, gvec, gb1 = middle(tok, ao, cot, wo, w1, w2, vecs, b1)
    dtok, gwq, *rest = backward(near, saved, wq, vecs, tok, da, dh1, gffn, gvec, gb1)
    if near:
        dtok, gwq, *rest = finish(dtok, gwq, *rest)
        small, (gwo, gw1, gw2) = rest[0:8], rest[8:11]
        small = [v if v.shape[0] == 3 else v.reshape(-1) for v in small]
    else:
        def part(v, axis=0):
            return lax.psum_scatter(v.astype(F32), BOTH, scatter_dimension=axis, tiled=True)
        vec, gwq = rest[0], gwq.reshape(3, D, D)
        gwq, gwo, gw1, gw2 = part(gwq, 1), part(gffn[0]), part(gffn[1]), part(gffn[2])
        small = (part(vec[0]), part(vec[1]), part(vec[2:5], 1), part(gvec[5]), part(gvec[6]), part(gvec[7]), part(gb1[0]), part(gvec[8]))
    return (out[None], dtok[None], small[0], small[1], gwq, small[2], gwo, small[3], small[4], small[5], gw1, small[6], gw2, small[7])


def solution(mesh):
    token, row, matrix = P("span", "head", None), P(BOTH), P(BOTH, None)
    three, bias = P(None, BOTH, None), P(None, BOTH)
    params = (row, row, three, bias, matrix, row, row, row, matrix, row, matrix, row)
    return jax.shard_map(shards, mesh=mesh, in_specs=(token, P("span", None)) + params + (token,),
                         out_specs=(token, token) + params, check_vma=False)
```
